32 devices in a mesh: wide: 8 (over z, x), narrow: 4 (over y, core).
Axes of the slice: x: 2, y: 2, z: 4, core: 2. Of those that a mesh axis runs over, the one named last changes fastest.
Arguments:
- tokens: bfloat16 [16, 1024, 768], P('wide', 'narrow'), may hold values from -6 to 6
- segment_ids: int32 [16, 1024], P('wide'), may hold values from -1 to 7, as said below
- cotangent: bfloat16 [16, 1024, 768], P('wide', 'narrow'), may hold values from -6 to 6
- attn_w: float32 [4, 768, 768], P(None, 'wide', 'narrow')
- attn_m: float32 [4, 768, 768], P(None, 'wide', 'narrow')
- attn_v: float32 [4, 768, 768], P(None, 'wide', 'narrow')
- mlp_w: float32 [2, 768, 3072], P(None, 'wide', 'narrow')
- mlp_m: float32 [2, 768, 3072], P(None, 'wide', 'narrow')
- mlp_v: float32 [2, 768, 3072], P(None, 'wide', 'narrow')
- vectors: float32 [12, 768], replicated
- vec_m: float32 [12, 768], replicated
- vec_v: float32 [12, 768], replicated
Outputs:
- block_out: bfloat16 [16, 1024, 768], P('wide', 'narrow')
- block_input_gradient: float32 [16, 1024, 768], P('wide', 'narrow')
- attn_grad: float32 [4, 768, 768], P(None, 'wide', 'narrow')
- attn_new: float32 [4, 768, 768], P(None, 'wide', 'narrow')
- attn_m_new: float32 [4, 768, 768], P(None, 'wide', 'narrow')
- attn_v_new: float32 [4, 768, 768], P(None, 'wide', 'narrow')
- mlp_grad: float32 [2, 768, 3072], P(None, 'wide', 'narrow')
- mlp_new: float32 [2, 768, 3072], P(None, 'wide', 'narrow')
- mlp_m_new: float32 [2, 768, 3072], P(None, 'wide', 'narrow')
- mlp_v_new: float32 [2, 768, 3072], P(None, 'wide', 'narrow')
- vec_grad: float32 [12, 768], replicated
- vec_new: float32 [12, 768], replicated
- vec_m_new: float32 [12, 768], replicated
- vec_v_new: float32 [12, 768], replicated
The draws below stay inside these ranges and needn't reach their ends.
Inputs may be any that keep to these rules, and one draw needn't show every extreme that they name: `segment_ids`: in each row the ids start at 0, never fall along the slots and are at most 7; the last slots of a row (at most 51) hold -1 for padding.
All inputs are finite; a program needn't handle non-finite values.
Results may differ from the reference program's by a relative error of at most 0.019.
Values may be sent and summed in bfloat16 or wider, within the bound.
No kernel may reach another device: no remote copies, remote signals or barrier semaphores. Data moves between devices by JAX's collectives and lax.ppermute only.
A program may use at most 128 MiB of HBM per device.

```python
import math
import jax
import jax.numpy as jnp
from jax import lax

D = 768
HEAD_DIM = 64
FF = 3072
L = 1024
STEP = 10
ROWS = 16
VROWS = 12


def grad_scale():
    return math.sqrt(ROWS * L)


def draw_segment_ids(key, part):
    starts = jax.random.randint(jax.random.fold_in(key, 1), (ROWS, L), 0, max(L // 16, 4))
    starts = jnp.where(starts == 0, 1, 0).astype(jnp.int32)
    row_index = jnp.arange(ROWS, dtype=jnp.int32)[:, None]
    slots = jnp.arange(L, dtype=jnp.int32)[None, :]
    forced = (row_index == 0) & (slots % (L // 8) == 0) & (slots > 0)
    starts = jnp.where(forced, 1, starts).astype(jnp.int32)
    starts = starts.at[:, 0].set(0)
    doc_ids = jnp.minimum(jnp.cumsum(starts, axis=1), 7).astype(jnp.int32)
    padding = jax.random.randint(jax.random.fold_in(key, 2), (ROWS, 1), 0, L // 20 + 1)
    padding = jnp.maximum(padding, jnp.where(row_index == 0, 1, 0)).astype(jnp.int32)
    return jnp.where(slots >= L - padding, -1, doc_ids).astype(jnp.int32)


def draw_attn_w(key, part):
    normal_draw = jnp.clip(jax.random.normal(jax.random.fold_in(key, 3), (4, D, D), jnp.float32), -4.0, 4.0)
    factors = jnp.array([1.3, 1.3, 1.0, 3.0], jnp.float32)
    return normal_draw * factors[:, None, None] / math.sqrt(D)


def draw_mlp_w(key, part):
    normal_draw = jnp.clip(jax.random.normal(jax.random.fold_in(key, 4), (2, D, FF), jnp.float32), -4.0, 4.0)
    factors = jnp.array([1.0 / math.sqrt(D), 1.5 / math.sqrt(FF)], jnp.float32)
    return normal_draw * factors[:, None, None]


def vector_factors():
    return jnp.concatenate([jnp.array([1.0, 1.0, 1.0, 1.0, 1.2, 1.0, 0.5, 1.0], jnp.float32), jnp.full((FF // D,), 0.45, jnp.float32)])


def draw_vectors(key, part):
    normal_draw = jnp.clip(jax.random.normal(jax.random.fold_in(key, 5), (VROWS, D), jnp.float32), -4.0, 4.0) * 0.2
    gains = jax.random.uniform(jax.random.fold_in(key, 6), (VROWS, D), jnp.float32, 0.7, 1.3)
    rows_idx = jnp.arange(VROWS)[:, None]
    is_gain = (rows_idx == 0) | (rows_idx == 2)
    return jnp.where(is_gain, gains, normal_draw)


def first_moment(key, shape, scales):
    normal_draw = jnp.clip(jax.random.normal(jax.random.fold_in(key, 7), shape, jnp.float32), -4.0, 4.0)
    return normal_draw * scales


def second_moment(key, shape, scales):
    spread = jax.random.uniform(jax.random.fold_in(key, 8), shape, jnp.float32, 0.0, math.log(4.0))
    return scales * scales * jnp.exp(spread)


def draw_attn_m(key, part):
    scales = jnp.array([0.5, 0.5, 1.0, 0.35], jnp.float32)[:, None, None] * grad_scale()
    return first_moment(key, (4, D, D), scales)


def draw_attn_v(key, part):
    scales = jnp.array([0.5, 0.5, 1.0, 0.35], jnp.float32)[:, None, None] * grad_scale()
    return second_moment(key, (4, D, D), scales)


def draw_mlp_m(key, part):
    scales = jnp.array([0.45, 0.5], jnp.float32)[:, None, None] * grad_scale()
    return first_moment(key, (2, D, FF), scales)


def draw_mlp_v(key, part):
    scales = jnp.array([0.45, 0.5], jnp.float32)[:, None, None] * grad_scale()
    return second_moment(key, (2, D, FF), scales)


def draw_vec_m(key, part):
    scales = vector_factors()[:, None] * grad_scale()
    return first_moment(key, (VROWS, D), scales)


def draw_vec_v(key, part):
    scales = vector_factors()[:, None] * grad_scale()
    return second_moment(key, (VROWS, D), scales)


def levels(stream_key, shape, shards, low, high):
    loudness = 1.0
    for dim, shards_of in shards:
        steps = jax.random.uniform(jax.random.fold_in(jax.random.fold_in(stream_key, 6), dim), (shards_of,), jnp.float32, low / len(shards), high / len(shards))
        loudness = loudness * jnp.repeat(jnp.exp(steps), shape[dim] // shards_of).reshape((-1,) + (1,) * (len(shape) - 1 - dim))
    return loudness


def bell_draw(stream_key, shape, width, limit, split=(), kind=jnp.bfloat16):
    entries = width * jax.random.normal(stream_key, shape, jnp.float32)
    if split:
        entries = entries * levels(stream_key, shape, split, -0.22, 0.18)
    return jnp.clip(entries, -limit, limit).astype(kind)


def setup_inputs(seed: int = 0) -> dict:
    seeds = jax.random.split(jax.random.key(seed), 13)
    return {
        "tokens": bell_draw(seeds[0], (ROWS, L, D), 1.0, 6.0, ((0, 8), (1, 4))),
        "segment_ids": draw_segment_ids(jax.random.fold_in(seeds[12], 71), 0),
        "cotangent": bell_draw(seeds[2], (ROWS, L, D), 1.0, 6.0, ((0, 8), (1, 4))),
        "attn_w": draw_attn_w(jax.random.fold_in(seeds[12], 71), 0),
        "attn_m": draw_attn_m(jax.random.fold_in(seeds[12], 71), 0),
        "attn_v": draw_attn_v(jax.random.fold_in(seeds[12], 71), 0),
        "mlp_w": draw_mlp_w(jax.random.fold_in(seeds[12], 71), 0),
        "mlp_m": draw_mlp_m(jax.random.fold_in(seeds[12], 71), 0),
        "mlp_v": draw_mlp_v(jax.random.fold_in(seeds[12], 71), 0),
        "vectors": draw_vectors(jax.random.fold_in(seeds[12], 71), 0),
        "vec_m": draw_vec_m(jax.random.fold_in(seeds[12], 71), 0),
        "vec_v": draw_vec_v(jax.random.fold_in(seeds[12], 71), 0),
    }


EPS_NORM = 1e-06
MASKED_SCORE = -1e+30
BETA_ONE = 0.5
BETA_TWO = 0.5
EPS_ADAM = 1e-08
RATE_MATRIX = 0.04
RATE_VECTOR = 0.3
DECAY_MATRIX = 0.05
HIGHEST = lax.Precision.HIGHEST

@jax.custom_vjp
def low(v):
    return lax.optimization_barrier(v.astype(jnp.bfloat16)).astype(jnp.float32)

@jax.custom_vjp
def low_back(v):
    return v

def low_keep(v):
    return (low(v), None)

def low_pass(kept, grad):
    return (grad,)

def back_keep(v):
    return (v, None)

def back_low(kept, grad):
    return (low(grad),)
low.defvjp(low_keep, low_pass)
low_back.defvjp(back_keep, back_low)

def matmul(left, right):
    return jnp.dot(left, right, precision=HIGHEST, preferred_element_type=jnp.float32)

def layer_norm(values_in, gain_vec, shift_vec):
    row_mean = lax.optimization_barrier(jnp.mean(values_in, axis=-1, keepdims=True))
    centred = values_in - row_mean
    row_var = lax.optimization_barrier(jnp.mean(centred * centred, axis=-1, keepdims=True))
    return centred * lax.rsqrt(row_var + EPS_NORM) * gain_vec + shift_vec

def row_forward(params, row_tokens, row_segments):
    attn_w, mlp_w, vectors = params
    attn_low = low(attn_w)
    mlp_low = low(mlp_w)
    heads_n = D // HEAD_DIM
    first_in = low(layer_norm(row_tokens, vectors[0], vectors[1]))
    queries = low(low_back(matmul(first_in, attn_low[0]) + vectors[6]))
    key_rows = low(low_back(matmul(first_in, attn_low[1])))
    value_rows = low(low_back(matmul(first_in, attn_low[2]) + vectors[7]))
    query_heads = queries.reshape(L, heads_n, HEAD_DIM)
    key_heads = key_rows.reshape(L, heads_n, HEAD_DIM)
    value_heads = value_rows.reshape(L, heads_n, HEAD_DIM)
    scores = jnp.einsum('qhd,khd->hqk', query_heads, key_heads, precision=HIGHEST) * HEAD_DIM ** (-0.5)
    scores = low_back(scores)
    same_doc = row_segments[:, None] == row_segments[None, :]
    attn_probs = jax.nn.softmax(jnp.where(same_doc[None], scores, MASKED_SCORE), axis=-1)
    context = jnp.einsum('hqk,khd->qhd', low(attn_probs), value_heads, precision=HIGHEST).reshape(L, D)
    context = low(low_back(context))
    hidden = row_tokens + low_back(matmul(context, attn_low[3].T)) + vectors[4]
    second_in = low(layer_norm(hidden, vectors[2], vectors[3]))
    up_bias = vectors[8:].reshape(FF)
    pre_act = low_back(matmul(second_in, mlp_low[0]) + up_bias)
    activated = low(jax.nn.gelu(pre_act, approximate=False))
    return hidden + low_back(matmul(activated, mlp_low[1].T)) + vectors[5]

def forward(input_tokens, attn_w, mlp_w, vectors, segment_ids):
    row_step = jax.checkpoint(lambda row_pair: row_forward((attn_w, mlp_w, vectors), row_pair[0], row_pair[1]))
    return lax.map(row_step, (input_tokens, segment_ids))

def adamw_update(weight, first_mom, second, gradient, step_rate, decay_rate):
    first_new = BETA_ONE * first_mom + (1.0 - BETA_ONE) * gradient
    second_new = BETA_TWO * second + (1.0 - BETA_TWO) * gradient * gradient
    corrected = first_new / (1.0 - BETA_ONE ** STEP) / (jnp.sqrt(second_new / (1.0 - BETA_TWO ** STEP)) + EPS_ADAM)
    return (weight - step_rate * (corrected + decay_rate * weight), first_new, second_new)

def reference(tokens, segment_ids, cotangent, attn_w, attn_m, attn_v, mlp_w, mlp_m, mlp_v, vectors, vec_m, vec_v):
    input_tokens = tokens.astype(jnp.float32)
    result, pullback = jax.vjp(lambda a_in, b_in, c_in, d_in: forward(a_in, b_in, c_in, d_in, segment_ids), input_tokens, attn_w, mlp_w, vectors)
    block_input_gradient, attn_grad, mlp_grad, vec_grad = pullback(cotangent.astype(jnp.float32))
    attn_new, attn_m_new, attn_v_new = adamw_update(attn_w, attn_m, attn_v, attn_grad, RATE_MATRIX, DECAY_MATRIX)
    mlp_new, mlp_m_new, mlp_v_new = adamw_update(mlp_w, mlp_m, mlp_v, mlp_grad, RATE_MATRIX, DECAY_MATRIX)
    vec_new, vec_m_new, vec_v_new = adamw_update(vectors, vec_m, vec_v, vec_grad, RATE_VECTOR, 0.0)
    return (result.astype(jnp.bfloat16), block_input_gradient, attn_grad, attn_new, attn_m_new, attn_v_new, mlp_grad, mlp_new, mlp_m_new, mlp_v_new, vec_grad, vec_new, vec_m_new, vec_v_new)
```

```python
import functools

import jax
import jax.numpy as jnp
from jax import lax
from jax.experimental import pallas as pl
from jax.experimental.pallas import tpu as pltpu
from jax.sharding import PartitionSpec as P

HEAD_DIM = 64
STEP = 10


EPS_NORM = 1e-06
MASKED_SCORE = -1e30
BETA_ONE = 0.5
BETA_TWO = 0.5
EPS_ADAM = 1e-08
RATE_MATRIX = 0.04
RATE_VECTOR = 0.3
DECAY_MATRIX = 0.05
SCALE = HEAD_DIM ** (-0.5)
TILE = 256
F32 = jnp.float32
BF16 = jnp.bfloat16
AXES = ("wide", "narrow")
VMEM_LIMIT = 48 * 1024 * 1024


def adamw_update(weight, first_mom, second, gradient, step_rate, decay_rate):
    first_new = BETA_ONE * first_mom + (1.0 - BETA_ONE) * gradient
    second_new = BETA_TWO * second + (1.0 - BETA_TWO) * gradient * gradient
    corrected = (
        first_new
        / (1.0 - BETA_ONE**STEP)
        / (jnp.sqrt(second_new / (1.0 - BETA_TWO**STEP)) + EPS_ADAM)
    )
    return (weight - step_rate * (corrected + decay_rate * weight), first_new, second_new)


def nn(a, b):
    return lax.dot_general(a, b, (((1,), (0,)), ((), ())), preferred_element_type=F32)


def nt(a, b):
    return lax.dot_general(a, b, (((1,), (1,)), ((), ())), preferred_element_type=F32)


def tn(a, b):
    return lax.dot_general(a, b, (((0,), (0,)), ((), ())), preferred_element_type=F32)


def standardize(v):
    centred = v - jnp.mean(v, axis=-1, keepdims=True)
    inv = lax.rsqrt(jnp.mean(centred * centred, axis=-1, keepdims=True) + EPS_NORM)
    return centred * inv, inv


def norm_back(grad_out, normed, inv, gain):
    scaled = grad_out * gain
    return inv * (
        scaled
        - jnp.mean(scaled, axis=-1, keepdims=True)
        - normed * jnp.mean(scaled * normed, axis=-1, keepdims=True)
    )


def whole(shape):
    return pl.BlockSpec(shape, lambda *_: (0,) * len(shape))


def params(cost=None):
    return pltpu.CompilerParams(
        dimension_semantics=("arbitrary",), vmem_limit_bytes=VMEM_LIMIT
    )


def call(kernel, grid, in_specs, out_specs, out_shape, scratch=(), flops=0, nbytes=0, trans=0):
    return pl.pallas_call(
        kernel,
        grid=grid,
        in_specs=in_specs,
        out_specs=out_specs,
        out_shape=out_shape,
        scratch_shapes=scratch,
        compiler_params=params(),
        cost_estimate=pl.CostEstimate(flops=flops, bytes_accessed=nbytes, transcendentals=trans),
    )


def qkv_kernel(x_ref, gain_ref, shift_ref, w0_ref, w1_ref, bias_ref, a_ref, qkv_ref):
    normed, _ = standardize(x_ref[...].astype(F32))
    low = (normed * gain_ref[...] + shift_ref[...]).astype(BF16)
    a_ref[...] = low
    cols = qkv_ref.shape[2]
    for j, w_ref in enumerate((w0_ref, w1_ref)):
        qkv_ref[j] = (nn(low, w_ref[:, :cols]) + bias_ref[j : j + 1]).astype(BF16)


def attend_kernel(qkv_q_ref, qkv_ref, seg_col_ref, seg_row_ref, w0_ref, w1_ref,
                  ctx_ref, lse_ref, out_ref):
    cols = ctx_ref.shape[2]
    heads = cols // HEAD_DIM
    same = seg_col_ref[...] == seg_row_ref[...]
    lane = lax.broadcasted_iota(jnp.int32, (TILE, 128), 1)
    totals = jnp.zeros((TILE, 128), F32)
    for j in range(2):
        for h in range(heads):
            lo = h * HEAD_DIM
            q = qkv_q_ref[j, :, lo : lo + HEAD_DIM]
            k = qkv_ref[j, :, cols + lo : cols + lo + HEAD_DIM]
            v = qkv_ref[j, :, 2 * cols + lo : 2 * cols + lo + HEAD_DIM]
            s = jnp.where(same, nt(q, k) * SCALE, MASKED_SCORE)
            top = jnp.max(s, axis=-1, keepdims=True)
            e = jnp.exp(s - top)
            total = jnp.sum(e, axis=-1, keepdims=True)
            o = nn(e.astype(BF16), v) / total
            ctx_ref[j, :, lo : lo + HEAD_DIM] = o.astype(BF16)
            totals = jnp.where(lane == j * heads + h, top + jnp.log(total), totals)
    lse_ref[...] = totals.T[: lse_ref.shape[0]]
    acc = nt(ctx_ref[0], w0_ref[:, 3 * cols :]) + nt(ctx_ref[1], w1_ref[:, 3 * cols :])
    out_ref[...] = acc.astype(BF16)


def mlp_kernel(x_ref, p0_ref, p1_ref, dy_ref, vec_ref, bu_ref, u0_ref, u1_ref, d0_ref, d1_ref,
               a_ref, z_ref, du_ref, down_ref, da_ref, gbu_ref):
    @pl.when(pl.program_id(0) == 0)
    def _():
        gbu_ref[...] = jnp.zeros_like(gbu_ref)

    h = x_ref[...].astype(F32) + (p0_ref[...].astype(F32) + p1_ref[...].astype(F32)) + vec_ref[4:5]
    normed, _ = standardize(h)
    a = (normed * vec_ref[2:3] + vec_ref[3:4]).astype(BF16)
    a_ref[...] = a
    dy = dy_ref[...]
    down = jnp.zeros(down_ref.shape, F32)
    da = jnp.zeros(down_ref.shape, F32)
    for j, (u_ref, d_ref) in enumerate(((u0_ref, d0_ref), (u1_ref, d1_ref))):
        u = nn(a, u_ref[...]) + bu_ref[j : j + 1]
        cdf = 0.5 + 0.5 * lax.erf(u * 0.7071067811865476)
        z = (u * cdf).astype(BF16)
        z_ref[j] = z
        slope = cdf + u * (0.3989422804014327 * jnp.exp(-0.5 * u * u))
        du = (nn(dy, d_ref[...]) * slope).astype(BF16)
        du_ref[j] = du
        gbu_ref[j : j + 1] += jnp.sum(du.astype(F32), axis=0, keepdims=True)
        down += nt(z, d_ref[...])
        da += nt(du, u_ref[...])
    down_ref[...] = down.astype(BF16)
    da_ref[...] = da.astype(BF16)


def mid_kernel(x_ref, p0_ref, p1_ref, dy_ref, da0_ref, da1_ref, ctx_ref, vec_ref, w0_ref, w1_ref,
               dh_ref, dctx_ref, delta_ref, sums_ref):
    @pl.when(pl.program_id(0) == 0)
    def _():
        sums_ref[...] = jnp.zeros_like(sums_ref)

    h = x_ref[...].astype(F32) + (p0_ref[...].astype(F32) + p1_ref[...].astype(F32)) + vec_ref[4:5]
    normed, inv = standardize(h)
    da = da0_ref[...].astype(F32) + da1_ref[...].astype(F32)
    dy = dy_ref[...].astype(F32)
    dh = dy + norm_back(da, normed, inv, vec_ref[2:3])
    low = dh.astype(BF16)
    dh_ref[...] = low
    sums_ref[0:1] += jnp.sum(da * normed, axis=0, keepdims=True)
    sums_ref[1:2] += jnp.sum(da, axis=0, keepdims=True)
    sums_ref[2:3] += jnp.sum(dh, axis=0, keepdims=True)
    sums_ref[3:4] += jnp.sum(dy, axis=0, keepdims=True)
    cols = ctx_ref.shape[2]
    heads = cols // HEAD_DIM
    lane = lax.broadcasted_iota(jnp.int32, (TILE, 128), 1)
    deltas = jnp.zeros((TILE, 128), F32)
    for j, w_ref in enumerate((w0_ref, w1_ref)):
        dctx = nn(low, w_ref[:, 3 * cols :]).astype(BF16)
        dctx_ref[j] = dctx
        prod = dctx.astype(F32) * ctx_ref[j].astype(F32)
        for hd in range(heads):
            part = jnp.sum(prod[:, hd * HEAD_DIM : (hd + 1) * HEAD_DIM], axis=-1, keepdims=True)
            deltas = jnp.where(lane == j * heads + hd, part, deltas)
    delta_ref[...] = deltas.T[: delta_ref.shape[0]]


def attend_back_kernel(qkv_ref, dctx_ref, lse_ref, delta_ref, seg_col_ref, seg_row_ref,
                       dqkv_ref, sums_ref, dk_ref, dv_ref):
    j = pl.program_id(0)
    cols = dctx_ref.shape[2]
    heads = cols // HEAD_DIM
    length = qkv_ref.shape[1]
    for h in range(heads):
        lo = h * HEAD_DIM
        k = qkv_ref[0, :, cols + lo : cols + lo + HEAD_DIM]
        v = qkv_ref[0, :, 2 * cols + lo : 2 * cols + lo + HEAD_DIM]
        for t in range(length // TILE):
            rows = slice(t * TILE, (t + 1) * TILE)
            q = qkv_ref[0, rows, lo : lo + HEAD_DIM]
            dc = dctx_ref[0, rows, lo : lo + HEAD_DIM]
            same = seg_col_ref[...] == seg_row_ref[:, rows]
            s = jnp.where(same, nt(k, q) * SCALE, MASKED_SCORE)
            p = jnp.exp(s - lse_ref[0, h : h + 1, rows])
            ds = (p * (nt(v, dc) - delta_ref[0, h : h + 1, rows])).astype(BF16)
            dv = nn(p.astype(BF16), dc)
            dk = nn(ds, q)
            if t == 0:
                dv_ref[...] = dv
                dk_ref[...] = dk
            else:
                dv_ref[...] += dv
                dk_ref[...] += dk
            dqkv_ref[0, rows, lo : lo + HEAD_DIM] = (tn(ds, k) * SCALE).astype(BF16)
        dqkv_ref[0, :, cols + lo : cols + lo + HEAD_DIM] = (dk_ref[...] * SCALE).astype(BF16)
        dqkv_ref[0, :, 2 * cols + lo : 2 * cols + lo + HEAD_DIM] = dv_ref[...].astype(BF16)
    sums_ref[0] = jnp.sum(dqkv_ref[0].astype(F32), axis=0, keepdims=True)


def final_kernel(x_ref, da0_ref, da1_ref, dh_ref, vec_ref, dx_ref, sums_ref):
    @pl.when(pl.program_id(0) == 0)
    def _():
        sums_ref[...] = jnp.zeros_like(sums_ref)

    normed, inv = standardize(x_ref[...].astype(F32))
    da = da0_ref[...].astype(F32) + da1_ref[...].astype(F32)
    dx_ref[...] = dh_ref[...].astype(F32) + norm_back(da, normed, inv, vec_ref[0:1])
    sums_ref[0:1] += jnp.sum(da * normed, axis=0, keepdims=True)
    sums_ref[1:2] += jnp.sum(da, axis=0, keepdims=True)


def local(
    tokens,
    segment_ids,
    cotangent,
    attn_w,
    attn_m,
    attn_v,
    mlp_w,
    mlp_m,
    mlp_v,
    vectors,
    vec_m,
    vec_v,
):
    wide = lax.axis_size("wide")
    narrow = lax.axis_size("narrow")
    widx = lax.axis_index("wide")
    nidx = lax.axis_index("narrow")
    y = nidx // 2
    c = nidx % 2
    other = (1 - y) * 2 + c
    xbit = widx % 2
    first_core = c == 0
    first_y = y == 0
    _, shard_len, width = tokens.shape
    length = segment_ids.shape[1]
    cols = attn_w.shape[2]
    rows = attn_w.shape[1]
    hidden = mlp_w.shape[2]
    heads = cols // HEAD_DIM
    bits = wide.bit_length() - 1
    upper = wide // 2

    def swap(value, partner):
        pairs = [
            (w * narrow + n, (lambda t: t[0] * narrow + t[1])(partner(w, n)))
            for w in range(wide)
            for n in range(narrow)
        ]
        return lax.ppermute(value, AXES, pairs)

    def over_core(value):
        return swap(value, lambda w, n: (w, n ^ 1))

    def over_y(value):
        return swap(value, lambda w, n: (w, n ^ 2))

    def over_bit(value, b):
        return swap(value, lambda w, n: (w ^ (1 << b), n))

    def mixed_one(value):
        return swap(value, lambda w, n: (w ^ 1, n) if n % 2 == 0 else (w, n ^ 2))

    def mixed_two(value):
        return swap(value, lambda w, n: (w ^ 1, n) if n % 2 == 1 else (w, n ^ 2))

    def pair(flag, first, second, axis):
        return jnp.stack(
            [jnp.where(flag, first, second), jnp.where(flag, second, first)], axis=axis
        )

    def gather(shard):
        held = shard[None]
        for b in range(1, bits):
            came = over_bit(held, b)
            high = ((widx >> b) & 1) == 1
            held = jnp.concatenate(
                [jnp.where(high, came, held), jnp.where(high, held, came)], axis=0
            )
        one = mixed_one(held)
        two = mixed_two(jnp.stack([held, one]))
        from_x = jnp.where(first_core, one, two[0])
        from_y = jnp.where(first_core, two[0], one)
        return (held, from_x, from_y, two[1])

    def arrange(pieces, m):
        held, from_x, from_y, diagonal = (p[:, m] for p in pieces)
        even = xbit == 0
        mine = pair(even, held, from_x, 1).reshape(upper * 2 * rows, -1)
        others = pair(even, from_y, diagonal, 1).reshape(upper * 2 * rows, -1)
        return (mine, others)

    def scatter(grads):
        mine = jnp.stack([g[0].astype(BF16) for g in grads]).reshape(-1, upper, 2, rows, width)
        others = jnp.stack([g[1].astype(BF16) for g in grads]).reshape(-1, upper, 2, rows, width)
        even = xbit == 0
        own = jnp.where(even, mine[:, :, 0], mine[:, :, 1])
        to_x = jnp.where(even, mine[:, :, 1], mine[:, :, 0])
        to_y = jnp.where(even, others[:, :, 0], others[:, :, 1])
        diagonal = jnp.where(even, others[:, :, 1], others[:, :, 0])
        came = mixed_two(jnp.stack([jnp.where(first_core, to_y, to_x), diagonal]))
        left = jnp.where(first_core, to_x, to_y).astype(F32) + came[1].astype(F32)
        last = mixed_one(left.astype(BF16))
        total = own.astype(F32) + came[0].astype(F32) + last.astype(F32)
        for b in reversed(range(1, bits)):
            half = total.shape[1] // 2
            high = ((widx >> b) & 1) == 1
            keep = jnp.where(high, total[:, half:], total[:, :half])
            send = jnp.where(high, total[:, :half], total[:, half:])
            total = keep + over_bit(send.astype(BF16), b).astype(F32)
        return total[:, 0]

    def own_row(value):
        keep = jnp.where(first_y, value[0], value[1])
        came = over_y(jnp.where(first_y, value[1], value[0]))
        mine = pair(first_y, keep, came, 0)
        theirs = over_core(mine)
        return pair(first_core, mine, theirs, 1).reshape(length, width)

    def home(value):
        keep = jnp.where(first_y, value[0], value[1])
        send = jnp.where(first_y, value[1], value[0])
        came = over_y(send.astype(BF16)).astype(value.dtype)
        return pair(first_y, keep, came, 0)

    def by_core(value):
        value = value.reshape(2, 2, shard_len, width)
        return (
            jnp.where(first_core, value[:, 0], value[:, 1]),
            jnp.where(first_core, value[:, 1], value[:, 0]),
        )

    def both(vector, size):
        return jnp.stack(
            [
                lax.dynamic_slice_in_dim(vector, nidx * size, size),
                lax.dynamic_slice_in_dim(vector, other * size, size),
            ]
        )

    x_row = own_row(tokens)
    attn_low = attn_w.astype(BF16)
    attn_shard = jnp.concatenate([attn_low[i] for i in range(4)], axis=-1)[None]
    attn_pieces = gather(attn_shard)
    a_mine, a_others = arrange(attn_pieces, 0)
    mlp_pieces = gather(mlp_w.astype(BF16))
    up_mine, up_others = arrange(mlp_pieces, 0)
    down_mine, down_others = arrange(mlp_pieces, 1)
    dy_row = own_row(cotangent)

    seg_own = lax.dynamic_index_in_dim(segment_ids, y, 0, False)
    seg_row = seg_own[None, :]
    seg_col = seg_own[:, None]
    query_bias = both(vectors[6], cols)
    value_bias = both(vectors[7], cols)
    qkv_bias = jnp.concatenate([query_bias, jnp.zeros_like(query_bias), value_bias], axis=1)
    up_bias = both(vectors[8:].reshape(-1), hidden)

    tiles = length // TILE
    full = (TILE, width)
    tile_spec = pl.BlockSpec(full, lambda t: (t, 0))
    weight_spec = whole((width, 4 * cols))
    qkv_cols = 3 * cols
    matmul = 2 * length * width

    normed_low, qkv = call(
        qkv_kernel,
        (tiles,),
        [tile_spec, whole((1, width)), whole((1, width)), weight_spec, weight_spec,
         whole((2, qkv_cols))],
        [tile_spec, pl.BlockSpec((2, TILE, qkv_cols), lambda t: (0, t, 0))],
        [jax.ShapeDtypeStruct((length, width), BF16),
         jax.ShapeDtypeStruct((2, length, qkv_cols), BF16)],
        flops=matmul * 2 * qkv_cols,
        nbytes=10_000_000,
    )(x_row, vectors[0:1], vectors[1:2], a_mine, a_others, qkv_bias)

    ctx_spec = pl.BlockSpec((2, TILE, cols), lambda t: (0, t, 0))
    context, lse, out_part = call(
        attend_kernel,
        (tiles,),
        [pl.BlockSpec((2, TILE, qkv_cols), lambda t: (0, t, 0)), whole((2, length, qkv_cols)),
         pl.BlockSpec((TILE, 1), lambda t: (t, 0)), whole((1, length)), weight_spec, weight_spec],
        [ctx_spec, pl.BlockSpec((8, TILE), lambda t: (0, t)), tile_spec],
        [jax.ShapeDtypeStruct((2, length, cols), BF16), jax.ShapeDtypeStruct((8, length), F32),
         jax.ShapeDtypeStruct((length, width), BF16)],
        flops=2 * matmul * 2 * cols + 4 * length * length * 2 * cols,
        nbytes=12_000_000,
        trans=2 * heads * length * length,
    )(qkv, qkv, seg_col, seg_row, a_mine, a_others)

    out_came = over_core(out_part)

    pair_spec = pl.BlockSpec((2, TILE, hidden), lambda t: (0, t, 0))
    up_spec = whole((width, hidden))
    second_low, activated, grad_pre, down_part, second_part, up_bias_sums = call(
        mlp_kernel,
        (tiles,),
        [tile_spec] * 4 + [whole(vectors.shape), whole((2, hidden))] + [up_spec] * 4,
        [tile_spec, pair_spec, pair_spec, tile_spec, tile_spec, whole((2, hidden))],
        [jax.ShapeDtypeStruct((length, width), BF16),
         jax.ShapeDtypeStruct((2, length, hidden), BF16),
         jax.ShapeDtypeStruct((2, length, hidden), BF16),
         jax.ShapeDtypeStruct((length, width), BF16),
         jax.ShapeDtypeStruct((length, width), BF16),
         jax.ShapeDtypeStruct((2, hidden), F32)],
        flops=4 * matmul * 2 * hidden,
        nbytes=25_000_000,
        trans=4 * length * hidden,
    )(x_row, out_part, out_came, dy_row, vectors, up_bias, up_mine, up_others, down_mine,
      down_others)

    second_came = over_core(second_part)

    def wgrad(left, right):
        return lax.dot_general(left, right, (((0,), (0,)), ((), ())), preferred_element_type=F32)

    grad_up = [wgrad(second_low, grad_pre[j]) for j in range(2)]
    grad_down = [wgrad(dy_row, activated[j]) for j in range(2)]
    mlp_total = scatter([grad_up, grad_down])

    down_keep, down_send = by_core(down_part)
    down_came = over_core(down_send)
    x_own, _ = by_core(x_row)
    out_own, _ = by_core(out_part)
    came_own, _ = by_core(out_came)
    hidden_own = x_own.astype(F32) + (out_own.astype(F32) + came_own.astype(F32)) + vectors[4]
    block_own = hidden_own + (down_keep.astype(F32) + down_came.astype(F32)) + vectors[5]
    block_out = home(block_own.astype(BF16))

    resid_low, grad_ctx, delta, mid_sums = call(
        mid_kernel,
        (tiles,),
        [tile_spec] * 6 + [ctx_spec, whole(vectors.shape), weight_spec, weight_spec],
        [tile_spec, ctx_spec, pl.BlockSpec((8, TILE), lambda t: (0, t)), whole((8, width))],
        [jax.ShapeDtypeStruct((length, width), BF16),
         jax.ShapeDtypeStruct((2, length, cols), BF16),
         jax.ShapeDtypeStruct((8, length), F32),
         jax.ShapeDtypeStruct((8, width), F32)],
        flops=matmul * 2 * cols,
        nbytes=14_000_000,
    )(x_row, out_part, out_came, dy_row, second_part, second_came, context, vectors, a_mine,
      a_others)

    stat_shape = (2, heads, length)
    grad_qkv, qkv_sums = call(
        attend_back_kernel,
        (2,),
        [pl.BlockSpec((1, length, qkv_cols), lambda j: (j, 0, 0)),
         pl.BlockSpec((1, length, cols), lambda j: (j, 0, 0)),
         pl.BlockSpec((1, heads, length), lambda j: (j, 0, 0)),
         pl.BlockSpec((1, heads, length), lambda j: (j, 0, 0)),
         whole((length, 1)), whole((1, length))],
        [pl.BlockSpec((1, length, qkv_cols), lambda j: (j, 0, 0)),
         pl.BlockSpec((1, 1, qkv_cols), lambda j: (j, 0, 0))],
        [jax.ShapeDtypeStruct((2, length, qkv_cols), BF16),
         jax.ShapeDtypeStruct((2, 1, qkv_cols), F32)],
        scratch=[pltpu.VMEM((length, HEAD_DIM), F32), pltpu.VMEM((length, HEAD_DIM), F32)],
        flops=10 * length * length * 2 * cols,
        nbytes=8_000_000,
        trans=2 * heads * length * length,
    )(qkv, grad_ctx, lse[: 2 * heads].reshape(stat_shape), delta[: 2 * heads].reshape(stat_shape),
      seg_col, seg_row)

    norm_one_part = sum(
        lax.dot_general(
            grad_qkv[j], w[:, :qkv_cols], (((1,), (1,)), ((), ())), preferred_element_type=F32
        )
        for j, w in enumerate((a_mine, a_others))
    ).astype(BF16)
    one_keep, one_send = by_core(norm_one_part)
    one_came = over_core(one_send)
    dh_own, _ = by_core(resid_low)

    half_spec = pl.BlockSpec((shard_len, width), lambda t: (t, 0))
    grad_own, one_sums = call(
        final_kernel,
        (2,),
        [half_spec] * 4 + [whole(vectors.shape)],
        [half_spec, whole((8, width))],
        [jax.ShapeDtypeStruct((2 * shard_len, width), F32),
         jax.ShapeDtypeStruct((8, width), F32)],
        nbytes=6_000_000,
    )(x_own.reshape(-1, width), one_keep.reshape(-1, width), one_came.reshape(-1, width),
      dh_own.reshape(-1, width), vectors)
    block_input_gradient = home(grad_own.reshape(2, shard_len, width))

    grad_attn = [
        jnp.concatenate([wgrad(normed_low, grad_qkv[j]), wgrad(resid_low, context[j])], axis=1)
        for j in range(2)
    ]
    attn_total = scatter([grad_attn])[0]

    def spread(pieces, size):
        empty = jnp.zeros((size * narrow,), F32)
        empty = lax.dynamic_update_slice_in_dim(empty, pieces[0], nidx * size, 0)
        return lax.dynamic_update_slice_in_dim(empty, pieces[1], other * size, 0)

    vec_grad = jnp.concatenate(
        [
            one_sums[:2],
            jnp.where(first_core, mid_sums[:4], 0.0),
            spread(qkv_sums[:, 0, :cols], cols)[None],
            spread(qkv_sums[:, 0, 2 * cols :], cols)[None],
            spread(up_bias_sums, hidden).reshape(-1, width),
        ],
        axis=0,
    )
    vec_grad = vec_grad + over_core(vec_grad)
    vec_grad = vec_grad + over_y(vec_grad)
    for b in range(bits):
        vec_grad = vec_grad + over_bit(vec_grad, b)

    attn_grad = jnp.stack([attn_total[:, i * cols : (i + 1) * cols] for i in range(4)])
    mlp_grad = mlp_total
    attn_new, attn_m_new, attn_v_new = adamw_update(
        attn_w, attn_m, attn_v, attn_grad, RATE_MATRIX, DECAY_MATRIX
    )
    mlp_new, mlp_m_new, mlp_v_new = adamw_update(
        mlp_w, mlp_m, mlp_v, mlp_grad, RATE_MATRIX, DECAY_MATRIX
    )
    vec_new, vec_m_new, vec_v_new = adamw_update(vectors, vec_m, vec_v, vec_grad, RATE_VECTOR, 0.0)
    return (
        block_out,
        block_input_gradient,
        attn_grad,
        attn_new,
        attn_m_new,
        attn_v_new,
        mlp_grad,
        mlp_new,
        mlp_m_new,
        mlp_v_new,
        vec_grad,
        vec_new,
        vec_m_new,
        vec_v_new,
    )


def solution(mesh):
    matrix = P(None, "wide", "narrow")
    rows = P("wide", "narrow", None)
    in_specs = (rows, P("wide", None), rows) + (matrix,) * 6 + (P(),) * 3
    out_specs = (rows, rows) + (matrix,) * 8 + (P(),) * 4
    return jax.shard_map(local, mesh=mesh, in_specs=in_specs, out_specs=out_specs, check_vma=False)
```

```python
import functools

import jax
import jax.numpy as jnp
from jax import lax
from jax.experimental import pallas as pl
from jax.experimental.pallas import tpu as pltpu
from jax.sharding import PartitionSpec as P

HEAD_DIM = 64
STEP = 10


EPS_NORM = 1e-06
MASKED_SCORE = -1e30
BETA_ONE = 0.5
BETA_TWO = 0.5
EPS_ADAM = 1e-08
RATE_MATRIX = 0.04
RATE_VECTOR = 0.3
DECAY_MATRIX = 0.05
SCALE = HEAD_DIM ** (-0.5)
TILE = 256
F32 = jnp.float32
BF16 = jnp.bfloat16
AXES = ("wide", "narrow")
COST_SCALE = 1
VMEM_LIMIT = 48 * 1024 * 1024


def adamw_update(weight, first_mom, second, gradient, step_rate, decay_rate):
    first_new = BETA_ONE * first_mom + (1.0 - BETA_ONE) * gradient
    second_new = BETA_TWO * second + (1.0 - BETA_TWO) * gradient * gradient
    corrected = (
        first_new
        / (1.0 - BETA_ONE**STEP)
        / (jnp.sqrt(second_new / (1.0 - BETA_TWO**STEP)) + EPS_ADAM)
    )
    return (weight - step_rate * (corrected + decay_rate * weight), first_new, second_new)


def nn(a, b):
    return lax.dot_general(a, b, (((1,), (0,)), ((), ())), preferred_element_type=F32)


def nt(a, b):
    return lax.dot_general(a, b, (((1,), (1,)), ((), ())), preferred_element_type=F32)


def tn(a, b):
    return lax.dot_general(a, b, (((0,), (0,)), ((), ())), preferred_element_type=F32)


def standardize(v):
    centred = v - jnp.mean(v, axis=-1, keepdims=True)
    inv = lax.rsqrt(jnp.mean(centred * centred, axis=-1, keepdims=True) + EPS_NORM)
    return centred * inv, inv


def norm_back(grad_out, normed, inv, gain):
    scaled = grad_out * gain
    return inv * (
        scaled
        - jnp.mean(scaled, axis=-1, keepdims=True)
        - normed * jnp.mean(scaled * normed, axis=-1, keepdims=True)
    )


def whole(shape):
    return pl.BlockSpec(shape, lambda *_: (0,) * len(shape))


def params(cost=None):
    return pltpu.CompilerParams(
        dimension_semantics=("arbitrary",), vmem_limit_bytes=VMEM_LIMIT
    )


def call(kernel, grid, in_specs, out_specs, out_shape, scratch=(), flops=0, nbytes=0, trans=0):
    return pl.pallas_call(
        kernel,
        grid=grid,
        in_specs=in_specs,
        out_specs=out_specs,
        out_shape=out_shape,
        scratch_shapes=scratch,
        compiler_params=params(),
        cost_estimate=pl.CostEstimate(
            flops=flops // COST_SCALE,
            bytes_accessed=nbytes // COST_SCALE,
            transcendentals=trans // COST_SCALE,
        ),
    )


def placed(kernel, grid, in_specs, out_specs, out_shape, scratch=(), flops=0, nbytes=0, trans=0):
    return pl.pallas_call(
        kernel,
        grid_spec=pltpu.PrefetchScalarGridSpec(
            num_scalar_prefetch=1,
            grid=grid,
            in_specs=in_specs,
            out_specs=out_specs,
            scratch_shapes=scratch,
        ),
        out_shape=out_shape,
        compiler_params=params(),
        cost_estimate=pl.CostEstimate(
            flops=flops // COST_SCALE,
            bytes_accessed=nbytes // COST_SCALE,
            transcendentals=trans // COST_SCALE,
        ),
    )


def head_columns(h, heads):
    many = (heads - 1) * HEAD_DIM
    if h < heads - 1:
        return tuple(kind * many + h * HEAD_DIM for kind in range(3))
    return tuple(3 * many + kind * HEAD_DIM for kind in range(3))


def natural(place_ref, pieces, targets):
    held_ref, from_x_ref, from_y_ref, diagonal_ref = pieces
    even = place_ref[0] == 0
    upper = place_ref[3]
    count, rows, _ = held_ref.shape
    for u in range(count):
        src = lax.bitwise_xor(upper, jnp.int32(u))
        for x in range(2):
            at = slice((2 * u + x) * rows, (2 * u + x + 1) * rows)
            near = even if x == 0 else jnp.logical_not(even)
            targets(0, at, jnp.where(near, held_ref[src], from_x_ref[src]))
            targets(1, at, jnp.where(near, from_y_ref[src], diagonal_ref[src]))


def pick_row(place_ref, tile, part, refs):
    keep_ref, came_ref, keep_core_ref, came_core_ref = refs
    same_y = tile // 2 == place_ref[2]
    same_core = tile % 2 == place_ref[1]
    return jnp.where(
        same_y,
        jnp.where(same_core, keep_ref[part], keep_core_ref[part]),
        jnp.where(same_core, came_ref[part], came_core_ref[part]),
    )


def qkv_kernel(place_ref, *refs):
    rows = refs[:4]
    pieces = refs[4:8]
    vec_ref, bias_ref, x_ref, dy_ref, a_ref, qkv_ref, w0_ref, w1_ref, o0_ref, o1_ref = refs[8:]
    cols = w0_ref.shape[1]

    @pl.when(pl.program_id(0) == 0)
    def _():
        def store(j, at, value):
            (w0_ref, w1_ref)[j][at] = value[:, :cols]
            (o0_ref, o1_ref)[j][at] = value[:, cols:]

        natural(place_ref, pieces, store)

    x = pick_row(place_ref, pl.program_id(0), 0, rows)
    x_ref[...] = x
    dy_ref[...] = pick_row(place_ref, pl.program_id(0), 1, rows)
    normed, _ = standardize(x.astype(F32))
    low = (normed * vec_ref[0:1] + vec_ref[1:2]).astype(BF16)
    a_ref[...] = low
    for j, w_ref in enumerate((w0_ref, w1_ref)):
        qkv_ref[j] = (nn(low, w_ref[...]) + bias_ref[j : j + 1]).astype(BF16)


def column(row):
    return jnp.broadcast_to(row, (128, row.shape[1])).T[:, :1]


def attend_kernel(last, qkv_q_ref, qkv_ref, seg_tile_ref, seg_row_ref, *refs):
    if last:
        ctx_in_ref, o0_ref, o1_ref, ctx_ref, lse_ref, out_ref = refs
    else:
        ctx_ref, lse_ref = refs
    cols = ctx_ref.shape[1]
    heads = cols // HEAD_DIM
    same = column(seg_tile_ref[...]) == seg_row_ref[...]
    lane = lax.broadcasted_iota(jnp.int32, (TILE, 128), 1)
    totals = jnp.zeros((TILE, 128), F32)
    for h in range(heads):
        lo = h * HEAD_DIM
        at_q, at_k, at_v = head_columns(h, heads)
        q = qkv_q_ref[:, at_q : at_q + HEAD_DIM]
        k = qkv_ref[:, at_k : at_k + HEAD_DIM]
        v = qkv_ref[:, at_v : at_v + HEAD_DIM]
        s = jnp.where(same, nt(q, k) * SCALE, MASKED_SCORE)
        top = jnp.max(s, axis=-1, keepdims=True)
        e = jnp.exp(s - top)
        total = jnp.sum(e, axis=-1, keepdims=True)
        o = nn(e.astype(BF16), v) / total
        ctx_ref[:, lo : lo + HEAD_DIM] = o.astype(BF16)
        totals = jnp.where(lane == h, top + jnp.log(total), totals)
    lse_ref[...] = totals.T[: lse_ref.shape[0]]
    if last:
        out_ref[...] = (nt(ctx_in_ref[...], o0_ref[...]) + nt(ctx_ref[...], o1_ref[...])).astype(BF16)


def sort_grad(place_ref, mine, others, own_ref, send_ref, keep_ref, at):
    even = place_ref[0] == 0
    first = place_ref[1] == 0
    rows = own_ref.shape[1]
    for u in range(own_ref.shape[0]):
        lo = slice(2 * u * rows, (2 * u + 1) * rows)
        hi = slice((2 * u + 1) * rows, (2 * u + 2) * rows)
        own_ref[u, :, at] = jnp.where(even, mine[lo], mine[hi])
        to_x = jnp.where(even, mine[hi], mine[lo])
        to_y = jnp.where(even, others[lo], others[hi])
        send_ref[0, u, :, at] = jnp.where(first, to_y, to_x)
        keep_ref[u, :, at] = jnp.where(first, to_x, to_y)
        send_ref[1, u, :, at] = jnp.where(even, others[hi], others[lo])


def add_grad(total_ref, j, left, right):
    part = tn(left, right)

    @pl.when(pl.program_id(0) == 0)
    def _():
        total_ref[j] = part

    @pl.when(pl.program_id(0) > 0)
    def _():
        total_ref[j] += part


def up_kernel(place_ref, x_ref, p0_ref, p1_ref, dy_ref, vec_ref, bu_ref, *refs):
    pieces = refs[:4]
    (a_ref, normed_ref, inv_ref, z_ref, slope_ref, own_ref, u0_ref, u1_ref,
     g_own_ref, g_send_ref, g_keep_ref, total_ref) = refs[4:]
    tile = pl.program_id(0)

    @pl.when(tile == 0)
    def _():
        def store(j, at, value):
            (u0_ref, u1_ref)[j][at] = value

        natural(place_ref, pieces, store)

    h = x_ref[...].astype(F32) + (p0_ref[...].astype(F32) + p1_ref[...].astype(F32)) + vec_ref[4:5]

    @pl.when(tile % 2 == place_ref[1])
    def _():
        own_ref[...] = h

    normed, inv = standardize(h)
    normed_ref[...] = normed.astype(BF16)
    inv_ref[...] = inv
    a = (normed * vec_ref[2:3] + vec_ref[3:4]).astype(BF16)
    a_ref[...] = a
    dy = dy_ref[...]
    for j, u_ref in enumerate((u0_ref, u1_ref)):
        u = nn(a, u_ref[...]) + bu_ref[j : j + 1]
        cdf = 0.5 + 0.5 * lax.erf(u * 0.7071067811865476)
        z = (u * cdf).astype(BF16)
        z_ref[j] = z
        slope_ref[j] = (cdf + u * (0.3989422804014327 * jnp.exp(-0.5 * u * u))).astype(BF16)
        add_grad(total_ref, j, dy, z)

    @pl.when(tile == pl.num_programs(0) - 1)
    def _():
        sort_grad(place_ref, total_ref[0].astype(BF16), total_ref[1].astype(BF16),
                  g_own_ref, g_send_ref, g_keep_ref, slice(None))


def down_kernel(place_ref, dy_ref, z_ref, slope_ref, u0_ref, u1_ref, *refs):
    pieces = refs[:4]
    du_ref, keep_ref, send_ref, da_ref, gbu_ref, d0_ref, d1_ref = refs[4:]
    tile = pl.program_id(0)

    @pl.when(tile == 0)
    def _():
        gbu_ref[...] = jnp.zeros_like(gbu_ref)

        def store(j, at, value):
            (d0_ref, d1_ref)[j][at] = value

        natural(place_ref, pieces, store)

    dy = dy_ref[...]
    down = jnp.zeros(da_ref.shape, F32)
    da = jnp.zeros(da_ref.shape, F32)
    for j, (u_ref, d_ref) in enumerate(((u0_ref, d0_ref), (u1_ref, d1_ref))):
        du = (nn(dy, d_ref[...]) * slope_ref[j].astype(F32)).astype(BF16)
        du_ref[j] = du
        gbu_ref[j : j + 1] += jnp.sum(du.astype(F32), axis=0, keepdims=True)
        down += nt(z_ref[j], d_ref[...])
        da += nt(du, u_ref[...])
    da_ref[...] = da.astype(BF16)
    down = down.astype(BF16)
    mine = tile % 2 == place_ref[1]

    @pl.when(mine)
    def _():
        keep_ref[...] = down

    @pl.when(jnp.logical_not(mine))
    def _():
        send_ref[...] = down


def grad_kernel(place_ref, left_ref, right_ref, own_ref, send_ref, keep_ref, turned_ref):
    @pl.when(pl.program_id(0) == 0)
    def _():
        turned_ref[...] = left_ref[...].T

    turned = turned_ref[...]
    mine = nn(turned, right_ref[0]).astype(BF16)
    others = nn(turned, right_ref[1]).astype(BF16)
    sort_grad(place_ref, mine, others, own_ref, send_ref, keep_ref, slice(None))


def two_grads_kernel(place_ref, left_ref, right_ref, dh_ref, ctx0_ref, ctx1_ref,
                     own_ref, send_ref, keep_ref):
    many = right_ref.shape[2]
    turned = left_ref[...].T
    mine = nn(turned, right_ref[0]).astype(BF16)
    others = nn(turned, right_ref[1]).astype(BF16)
    sort_grad(place_ref, mine, others, own_ref, send_ref, keep_ref, slice(0, many))
    turned = dh_ref[...].T
    mine = nn(turned, ctx0_ref[...]).astype(BF16)
    others = nn(turned, ctx1_ref[...]).astype(BF16)
    sort_grad(place_ref, mine, others, own_ref, send_ref, keep_ref, slice(many, None))


def mid_kernel(normed_ref, inv_ref, dy_ref, da0_ref, da1_ref, ctx0_ref, ctx1_ref, vec_ref,
               o0_ref, o1_ref, dh_ref, dctx_ref, delta_ref, sums_ref):
    @pl.when(pl.program_id(0) == 0)
    def _():
        sums_ref[...] = jnp.zeros_like(sums_ref)

    normed = normed_ref[...].astype(F32)
    da = da0_ref[...].astype(F32) + da1_ref[...].astype(F32)
    dy = dy_ref[...].astype(F32)
    dh = dy + norm_back(da, normed, inv_ref[...], vec_ref[2:3])
    low = dh.astype(BF16)
    dh_ref[...] = low
    sums_ref[0:1] += jnp.sum(da * normed, axis=0, keepdims=True)
    sums_ref[1:2] += jnp.sum(da, axis=0, keepdims=True)
    sums_ref[2:3] += jnp.sum(dh, axis=0, keepdims=True)
    sums_ref[3:4] += jnp.sum(dy, axis=0, keepdims=True)
    cols = ctx0_ref.shape[1]
    head = lax.broadcasted_iota(jnp.int32, (8, cols), 0)
    owner = lax.broadcasted_iota(jnp.int32, (8, cols), 1) // HEAD_DIM
    member = jnp.where(head == owner, 1.0, 0.0).astype(BF16)
    for j, (o_ref, ctx_ref) in enumerate(((o0_ref, ctx0_ref), (o1_ref, ctx1_ref))):
        dctx = nn(low, o_ref[...]).astype(BF16)
        dctx_ref[j] = dctx
        prod = dctx.astype(F32) * ctx_ref[...].astype(F32)
        high = prod.astype(BF16)
        rest = (prod - high.astype(F32)).astype(BF16)
        delta_ref[j] = nt(member, high) + nt(member, rest)


def attend_back_kernel(which, heads, qkv_ref, dctx_ref, lse0_ref, lse1_ref, delta_ref, seg_row_ref,
                       dqkv_ref, sums_ref, dk_ref, dv_ref):
    length = qkv_ref.shape[1]
    seg_col = column(seg_row_ref[...])
    first = pl.program_id(0) == 0
    many = len(which) * HEAD_DIM
    for i, h in enumerate(which):
        lo = h * HEAD_DIM
        at_q, at_k, at_v = head_columns(h, heads)
        k = qkv_ref[0, :, at_k : at_k + HEAD_DIM]
        v = qkv_ref[0, :, at_v : at_v + HEAD_DIM]
        out = [kind * many + i * HEAD_DIM for kind in range(3)]
        for t in range(length // TILE):
            rows = slice(t * TILE, (t + 1) * TILE)
            q = qkv_ref[0, rows, at_q : at_q + HEAD_DIM]
            dc = dctx_ref[0, rows, lo : lo + HEAD_DIM]
            same = seg_col == seg_row_ref[:, rows]
            lse = jnp.where(first, lse0_ref[h : h + 1, rows], lse1_ref[h : h + 1, rows])
            s = jnp.where(same, nt(k, q) * SCALE, MASKED_SCORE)
            p = jnp.exp(s - lse)
            ds = (p * (nt(v, dc) - delta_ref[0, h : h + 1, rows])).astype(BF16)
            dv = nn(p.astype(BF16), dc)
            dk = nn(ds, q)
            if t == 0:
                dv_ref[...] = dv
                dk_ref[...] = dk
            else:
                dv_ref[...] += dv
                dk_ref[...] += dk
            dqkv_ref[0, rows, out[0] : out[0] + HEAD_DIM] = (tn(ds, k) * SCALE).astype(BF16)
        dqkv_ref[0, :, out[1] : out[1] + HEAD_DIM] = (dk_ref[...] * SCALE).astype(BF16)
        dqkv_ref[0, :, out[2] : out[2] + HEAD_DIM] = dv_ref[...].astype(BF16)
    sums_ref[0] = jnp.sum(dqkv_ref[0].astype(F32), axis=0, keepdims=True)


def input_grad_kernel(place_ref, x_ref, p_ref, q_ref, w0_ref, w1_ref, keep_ref, send_ref, sums_ref):
    tile = pl.program_id(0)

    @pl.when(tile == 0)
    def _():
        sums_ref[...] = jnp.zeros_like(sums_ref)

    many = p_ref.shape[2]
    out = jnp.zeros(keep_ref.shape, F32)
    for j, w_ref in enumerate((w0_ref, w1_ref)):
        out += nt(p_ref[j], w_ref[:, :many]) + nt(q_ref[j], w_ref[:, many:])
    normed, _ = standardize(x_ref[...].astype(F32))
    sums_ref[0:1] += jnp.sum(out * normed, axis=0, keepdims=True)
    sums_ref[1:2] += jnp.sum(out, axis=0, keepdims=True)
    out = out.astype(BF16)
    mine = tile % 2 == place_ref[1]

    @pl.when(mine)
    def _():
        keep_ref[...] = out

    @pl.when(jnp.logical_not(mine))
    def _():
        send_ref[...] = out


def final_kernel(place_ref, x_ref, da0_ref, da1_ref, dh_ref, own_ref, keep_ref, came_ref, vec_ref,
                 dx_ref, out_ref, send_ref):
    normed, inv = standardize(x_ref[...].astype(F32))
    da = da0_ref[...].astype(F32) + da1_ref[...].astype(F32)
    dx = dh_ref[...].astype(F32) + norm_back(da, normed, inv, vec_ref[0:1])
    dx_ref[...] = dx
    out = own_ref[...] + (keep_ref[...].astype(F32) + came_ref[...].astype(F32)) + vec_ref[5:6]
    out = out.astype(BF16)
    out_ref[...] = out

    @pl.when(pl.program_id(0) != place_ref[2])
    def _():
        send_ref[0] = dx.astype(BF16)
        send_ref[1] = out


def local(
    tokens,
    segment_ids,
    cotangent,
    attn_w,
    attn_m,
    attn_v,
    mlp_w,
    mlp_m,
    mlp_v,
    vectors,
    vec_m,
    vec_v,
):
    wide = lax.axis_size("wide")
    narrow = lax.axis_size("narrow")
    widx = lax.axis_index("wide")
    nidx = lax.axis_index("narrow")
    y = nidx // 2
    c = nidx % 2
    other = (1 - y) * 2 + c
    xbit = widx % 2
    even = xbit == 0
    first_core = c == 0
    first_y = y == 0
    _, shard_len, width = tokens.shape
    length = segment_ids.shape[1]
    cols = attn_w.shape[2]
    rows = attn_w.shape[1]
    hidden = mlp_w.shape[2]
    heads = cols // HEAD_DIM
    bits = wide.bit_length() - 1
    upper = wide // 2
    steps = [(b, min(2, bits - b)) for b in range(1, bits, 2)]

    def swap(value, partner):
        pairs = [
            (w * narrow + n, (lambda t: t[0] * narrow + t[1])(partner(w, n)))
            for w in range(wide)
            for n in range(narrow)
        ]
        return lax.ppermute(value, AXES, pairs)

    def over_core(value):
        return swap(value, lambda w, n: (w, n ^ 1))

    def over_y(value):
        return swap(value, lambda w, n: (w, n ^ 2))

    def over_x(value):
        return swap(value, lambda w, n: (w ^ 1, n))

    def over_wide(value, mask):
        return swap(value, lambda w, n: (w ^ mask, n))

    def mixed_one(value):
        return swap(value, lambda w, n: (w ^ 1, n) if n % 2 == 0 else (w, n ^ 2))

    def mixed_two(value):
        return swap(value, lambda w, n: (w ^ 1, n) if n % 2 == 1 else (w, n ^ 2))

    def tie(value, *deps):
        return lax.optimization_barrier((value, *deps))[0]

    def pair(flag, first, second, axis):
        return jnp.stack(
            [jnp.where(flag, first, second), jnp.where(flag, second, first)], axis=axis
        )

    def add_low(keep, came):
        return (keep.astype(F32) + came.astype(F32)).astype(BF16)

    def total_of(own, came, last):
        return own.astype(F32) + came.astype(F32) + last.astype(F32)

    def choose(index, values):
        picked = values[0]
        for i in range(1, len(values)):
            picked = jnp.where(index == i, values[i], picked)
        return picked

    def gather_upper(shard, how, *deps):
        held = shard[None]
        for b, count in how:
            came = [over_wide(held, k << b) for k in range(1, 1 << count)]
            if deps:
                held, *came = lax.optimization_barrier((held, *came, *deps))[: 1 << count]
            held = jnp.concatenate([held, *came], axis=0)
        return held

    def scatter_upper(total, *deps):
        for b, count in reversed(steps):
            size = total.shape[0] >> count
            digit = (widx >> b) & ((1 << count) - 1)
            blocks = [total[i * size : (i + 1) * size] for i in range(1 << count)]
            came = []
            for k in range(1, 1 << count):
                send = choose(digit, [blocks[i ^ k] for i in range(1 << count)])
                came.append(over_wide(send.astype(BF16), k << b))
            if deps:
                came = lax.optimization_barrier((*came, *deps))[: len(came)]
            total = choose(digit, blocks).astype(F32)
            for each in came:
                total = total + each.astype(F32)
        return total[0]

    def both(vector, size):
        return jnp.stack(
            [
                lax.dynamic_slice_in_dim(vector, nidx * size, size),
                lax.dynamic_slice_in_dim(vector, other * size, size),
            ]
        )

    tiles = length // TILE
    tile_spec = pl.BlockSpec((TILE, width), lambda t, *_: (t, 0))
    up_spec = whole((width, hidden))
    qkv_cols = 3 * cols
    matmul = 2 * length * width
    row_shape = jax.ShapeDtypeStruct((length, width), BF16)
    zero = jnp.int32(0)
    place = jnp.stack([xbit, c, y, widx // 2, zero, zero, zero, zero]).astype(jnp.int32)

    def spread_over_plane(held):
        from_x = over_x(held)
        from_y = over_y(held)
        return from_x, from_y

    def turn(from_x, from_y):
        return jnp.where(first_core, from_x, from_y)

    attn_low = attn_w.astype(BF16)
    many = cols - HEAD_DIM
    attn_shard = jnp.concatenate(
        [attn_low[i, :, :many] for i in range(3)]
        + [attn_low[i, :, many:] for i in range(3)]
        + [attn_low[3]],
        axis=-1,
    )
    mlp_low = mlp_w.astype(BF16)
    a_held = gather_upper(attn_shard, steps)

    def row_pair(first):
        return jnp.stack(
            [jnp.where(first, v[0], v[1]) for v in (tokens, cotangent)]
        )

    rows_send = row_pair(jnp.logical_not(first_y))
    rows_came = over_y(tie(rows_send, attn_shard))
    rows_keep = row_pair(first_y)
    rows_keep_core = over_core(rows_keep)

    a_x, a_y = spread_over_plane(a_held)
    rows_came = tie(rows_came, a_held)
    rows_came_core = over_core(rows_came)
    a_turn = turn(a_x, a_y)
    a_diagonal = mixed_two(a_turn)
    u_held = gather_upper(tie(mlp_low[0], a_held, rows_came_core, rows_keep_core), steps, a_turn)
    u_x, u_y = spread_over_plane(u_held)
    d_first = mlp_low[1][None]
    d_first_came = over_wide(tie(d_first, u_held), 2)

    seg_own = lax.dynamic_index_in_dim(segment_ids, y, 0, False)
    seg_row = seg_own[None, :]
    query_bias = both(vectors[6], cols)
    value_bias = both(vectors[7], cols)
    no_bias = jnp.zeros_like(query_bias)
    qkv_bias = jnp.concatenate(
        [bias[:, :many] for bias in (query_bias, no_bias, value_bias)]
        + [bias[:, many:] for bias in (query_bias, no_bias, value_bias)],
        axis=1,
    )
    up_bias = both(vectors[8:].reshape(-1), hidden)

    part_spec = whole((2, shard_len, width))
    piece_spec = whole((upper, rows, width))
    attn_shapes = [(width, qkv_cols), (width, qkv_cols), (width, cols), (width, cols)]
    x_row, dy_row, normed_low, qkv, w_mine, w_others, o_mine, o_others = placed(
        qkv_kernel,
        (tiles,),
        [part_spec] * 4 + [piece_spec] * 4 + [whole(vectors.shape), whole((2, qkv_cols))],
        [tile_spec] * 3 + [pl.BlockSpec((2, TILE, qkv_cols), lambda t, p: (0, t, 0))]
        + [whole(shape) for shape in attn_shapes],
        [row_shape] * 3 + [jax.ShapeDtypeStruct((2, length, qkv_cols), BF16)]
        + [jax.ShapeDtypeStruct(shape, BF16) for shape in attn_shapes],
        flops=matmul * 2 * qkv_cols,
        nbytes=12_000_000,
    )(tie(place, u_held), rows_keep, rows_came, rows_keep_core, rows_came_core, a_held, a_x, a_y,
      a_diagonal, vectors, qkv_bias)

    ctx_spec = pl.BlockSpec((TILE, cols), lambda t: (t, 0))
    lse_spec = pl.BlockSpec((8, TILE), lambda t: (0, t))
    ctx_shape = jax.ShapeDtypeStruct((length, cols), BF16)
    lse_shape = jax.ShapeDtypeStruct((8, length), F32)
    o_spec = whole((width, cols))

    def attend(j, segments, extra):
        last = bool(extra)
        in_specs = [
            pl.BlockSpec((None, TILE, qkv_cols), lambda t: (j, t, 0)),
            pl.BlockSpec((None, length, qkv_cols), lambda t: (j, 0, 0)),
            pl.BlockSpec((1, TILE), lambda t: (0, t)),
            whole((1, length)),
        ]
        out_specs = [ctx_spec, lse_spec]
        out_shape = [ctx_shape, lse_shape]
        if last:
            in_specs += [ctx_spec, o_spec, o_spec]
            out_specs += [tile_spec]
            out_shape += [row_shape]
        return call(
            functools.partial(attend_kernel, last),
            (tiles,),
            in_specs,
            out_specs,
            out_shape,
            flops=4 * length * length * cols,
            nbytes=6_000_000,
            trans=heads * length * length,
        )(qkv, qkv, segments, segments, *extra)

    d_first, d_first_came = lax.optimization_barrier((d_first, d_first_came, qkv))[:2]
    d_second = jnp.concatenate([d_first, d_first_came], axis=0)
    d_second_came = over_wide(d_second, 4)
    ctx_mine, lse_mine = attend(0, tie(seg_row, d_second), ())
    d_second, d_second_came = lax.optimization_barrier((d_second, d_second_came, ctx_mine))[:2]
    d_second = jnp.concatenate([d_second, d_second_came], axis=0)

    def gather_rest(held):
        for b in range(3, bits):
            held = jnp.concatenate([held, over_wide(held, 1 << b)], axis=0)
        return held

    d_held = d_second if bits == 3 else gather_rest(d_second)
    u_turn = turn(*lax.optimization_barrier((u_x, u_y, ctx_mine))[:2])
    u_diagonal = mixed_two(u_turn)
    d_x, d_y = spread_over_plane(tie(d_held, u_turn))
    d_diagonal = swap(tie(d_held, u_turn), lambda w, n: (w ^ 1, n ^ 2))
    ctx_others, lse_others, out_part = attend(
        1, tie(seg_row, u_turn, d_held), (ctx_mine, o_mine, o_others)
    )
    out_part, u_diagonal = lax.optimization_barrier((out_part, u_diagonal))
    out_came = over_core(out_part)

    pair_spec = pl.BlockSpec((2, TILE, hidden), lambda t, *_: (0, t, 0))
    pair_shape = jax.ShapeDtypeStruct((2, length, hidden), BF16)
    half_spec = pl.BlockSpec((None, TILE, width), lambda t, *_: (t // 2, 0, 0))
    up_shape = jax.ShapeDtypeStruct((width, hidden), BF16)

    def half_shape(dtype):
        return jax.ShapeDtypeStruct((2, shard_len, width), dtype)

    grad_specs = [piece_spec, whole((2, upper, rows, width)), piece_spec]
    grad_shapes = [
        jax.ShapeDtypeStruct((upper, rows, hidden), BF16),
        jax.ShapeDtypeStruct((2, upper, rows, hidden), BF16),
        jax.ShapeDtypeStruct((upper, rows, hidden), BF16),
    ]
    (second_low, second_normed, second_inv, activated, slope, hidden_own, u_mine, u_others,
     gd_own, gd_send, gd_keep) = placed(
        up_kernel,
        (tiles,),
        [tile_spec] * 4 + [whole(vectors.shape), whole((2, hidden))] + [piece_spec] * 4,
        [tile_spec, tile_spec, pl.BlockSpec((TILE, 1), lambda t, p: (t, 0)), pair_spec, pair_spec,
         half_spec, up_spec, up_spec] + grad_specs,
        [row_shape, row_shape, jax.ShapeDtypeStruct((length, 1), F32), pair_shape, pair_shape,
         half_shape(F32), up_shape, up_shape] + grad_shapes,
        scratch=[pltpu.VMEM((2, width, hidden), F32)],
        flops=2 * matmul * 2 * hidden,
        nbytes=20_000_000,
        trans=4 * length * hidden,
    )(place, x_row, out_part, out_came, dy_row, vectors, up_bias, u_held, u_x, u_y, u_diagonal)
    gd_came = mixed_two(gd_send)

    def weight_grad(where, left, right, block, extra=()):
        size = right.shape[2]
        out_cols = size + (extra[1].shape[1] if extra else 0)
        in_specs = [
            whole((length, width)),
            pl.BlockSpec((2, length, block), lambda i, p: (0, 0, i)),
        ] + [whole(e.shape) for e in extra]
        out_block = out_cols if extra else block
        spec = pl.BlockSpec((upper, rows, out_block), lambda i, p: (0, 0, i))
        shape = jax.ShapeDtypeStruct((upper, rows, out_cols), BF16)
        return placed(
            two_grads_kernel if extra else grad_kernel,
            (size // block,),
            in_specs,
            [spec, pl.BlockSpec((2, upper, rows, out_block), lambda i, p: (0, 0, 0, i)), spec],
            [shape, jax.ShapeDtypeStruct((2, upper, rows, out_cols), BF16), shape],
            scratch=() if extra else [pltpu.VMEM((width, length), BF16)],
            flops=matmul * 2 * out_cols,
            nbytes=8_000_000,
        )(where, left, right, *extra)

    grad_pre, down_keep, down_send, second_part, up_bias_sums = placed(
        down_kernel,
        (tiles,),
        [tile_spec, pair_spec, pair_spec, up_spec, up_spec] + [piece_spec] * 4,
        [pair_spec, half_spec, half_spec, tile_spec, whole((2, hidden))],
        [pair_shape, half_shape(BF16), half_shape(BF16), row_shape,
         jax.ShapeDtypeStruct((2, hidden), F32)],
        scratch=[pltpu.VMEM((width, hidden), BF16)] * 2,
        flops=3 * matmul * 2 * hidden,
        nbytes=20_000_000,
    )(tie(place, gd_send), dy_row, activated, slope, u_mine, u_others, d_held, d_x, d_y, d_diagonal)
    second_part, gd_came = lax.optimization_barrier((second_part, gd_came))

    down_came = over_core(down_send)
    second_came = over_core(second_part)
    gd_last_send = add_low(gd_keep, gd_came[1])
    gd_last = mixed_one(gd_last_send)
    gu_own, gu_send, gu_keep = weight_grad(
        tie(place, gd_last_send), second_low, grad_pre, 256
    )
    gu_came = mixed_two(gu_send)

    delta_spec = pl.BlockSpec((2, 8, TILE), lambda t: (0, 0, t))
    resid_low, grad_ctx, delta, mid_sums = call(
        mid_kernel,
        (tiles,),
        [tile_spec, pl.BlockSpec((TILE, 1), lambda t: (t, 0))] + [tile_spec] * 3
        + [ctx_spec, ctx_spec, whole(vectors.shape), o_spec, o_spec],
        [tile_spec, pl.BlockSpec((2, TILE, cols), lambda t: (0, t, 0)), delta_spec,
         whole((8, width))],
        [row_shape,
         jax.ShapeDtypeStruct((2, length, cols), BF16),
         jax.ShapeDtypeStruct((2, 8, length), F32),
         jax.ShapeDtypeStruct((8, width), F32)],
        flops=matmul * 2 * cols,
        nbytes=10_000_000,
    )(second_normed, second_inv, dy_row, second_part, second_came, ctx_mine, ctx_others,
      tie(vectors, gu_send), o_mine, o_others)

    def attend_back(which, segments):
        size = 3 * HEAD_DIM * len(which)
        return call(
            functools.partial(attend_back_kernel, which, heads),
            (2,),
            [pl.BlockSpec((1, length, qkv_cols), lambda j: (j, 0, 0)),
             pl.BlockSpec((1, length, cols), lambda j: (j, 0, 0)),
             whole((8, length)),
             whole((8, length)),
             pl.BlockSpec((1, 8, length), lambda j: (j, 0, 0)),
             whole((1, length))],
            [pl.BlockSpec((1, length, size), lambda j: (j, 0, 0)),
             pl.BlockSpec((1, 1, size), lambda j: (j, 0, 0))],
            [jax.ShapeDtypeStruct((2, length, size), BF16),
             jax.ShapeDtypeStruct((2, 1, size), F32)],
            scratch=[pltpu.VMEM((length, HEAD_DIM), F32), pltpu.VMEM((length, HEAD_DIM), F32)],
            flops=20 * length * length * HEAD_DIM * len(which),
            nbytes=8_000_000,
            trans=2 * len(which) * length * length,
        )(qkv, grad_ctx, lse_mine, lse_others, delta, segments)

    gd_sum = total_of(gd_own, gd_came[0], tie(gd_last, grad_ctx))
    dqkv_many, sums_many = attend_back(tuple(range(heads - 1)), tie(seg_row, gd_sum))
    gd_total = scatter_upper(gd_sum, dqkv_many)
    gu_came = tie(gu_came, dqkv_many)
    gu_last_send = add_low(gu_keep, gu_came[1])
    gu_last = mixed_one(gu_last_send)
    gp_own, gp_send, gp_keep = weight_grad(
        tie(place, gu_last_send, gd_total), normed_low, dqkv_many, 3 * many,
        (resid_low, ctx_mine, ctx_others),
    )
    gp_came = mixed_two(gp_send)

    dqkv_last, sums_last = attend_back((heads - 1,), tie(seg_row, gp_send))
    gu_sum = total_of(gu_own, gu_came[0], tie(gu_last, dqkv_last))

    half_out = pl.BlockSpec((None, TILE, width), lambda t, p: (t // 2, 0, 0))
    one_keep, one_send, one_sums = placed(
        input_grad_kernel,
        (tiles,),
        [tile_spec,
         pl.BlockSpec((2, TILE, 3 * many), lambda t, p: (0, t, 0)),
         pl.BlockSpec((2, TILE, 3 * HEAD_DIM), lambda t, p: (0, t, 0))]
        + [whole((width, qkv_cols))] * 2,
        [half_out] * 2 + [whole((8, width))],
        [half_shape(BF16)] * 2 + [jax.ShapeDtypeStruct((8, width), F32)],
        flops=matmul * 2 * qkv_cols,
        nbytes=8_000_000,
    )(tie(place, gu_sum), x_row, dqkv_many, dqkv_last, w_mine, w_others)
    one_came = over_core(one_send)
    gq_own, gq_send, gq_keep = weight_grad(
        tie(place, one_send), normed_low, dqkv_last, 3 * HEAD_DIM
    )

    def spread(mine, others, size):
        empty = jnp.zeros((size * narrow,), F32)
        empty = lax.dynamic_update_slice_in_dim(empty, mine, nidx * size, 0)
        return lax.dynamic_update_slice_in_dim(empty, others, other * size, 0)

    def kind_sums(kind):
        return [
            jnp.concatenate(
                [
                    sums_many[j, 0, kind * many : (kind + 1) * many],
                    sums_last[j, 0, kind * HEAD_DIM : (kind + 1) * HEAD_DIM],
                ]
            )
            for j in range(2)
        ]

    vec_part = jnp.concatenate(
        [
            one_sums[:2],
            jnp.where(first_core, mid_sums[:4], 0.0),
            spread(*kind_sums(0), cols)[None],
            spread(*kind_sums(2), cols)[None],
            spread(up_bias_sums[0], up_bias_sums[1], hidden).reshape(-1, width),
        ],
        axis=0,
    )

    def split(value):
        high = value.astype(BF16)
        rest = (value - high.astype(F32)).astype(BF16)
        return jnp.stack([high, rest])

    def joined(pair_of):
        return pair_of[0].astype(F32) + pair_of[1].astype(F32)

    vec_pair = split(vec_part)
    gq_cols = 3 * HEAD_DIM
    vec_rows = 2 * vec_part.size // gq_cols

    def load(parts, extra):
        return jnp.concatenate([p.reshape(-1, gq_cols) for p in (*parts, extra)], axis=0)

    gq_load = load([gq_send], vec_pair)
    gq_all = mixed_two(gq_load)

    gp_came = tie(gp_came, gq_send)
    gp_last_send = add_low(gp_keep, gp_came[1])
    gp_last = mixed_one(gp_last_send)

    own_block = pl.BlockSpec((TILE, width), lambda t, p: (2 * t + p[1], 0))
    half_in = pl.BlockSpec((None, TILE, width), lambda t, p: (t, 0, 0))
    grad_own, block_own, last_send = placed(
        final_kernel,
        (2,),
        [own_block, half_in, half_in, own_block] + [half_in] * 3 + [whole(vectors.shape)],
        [half_in, half_in, whole((2, shard_len, width))],
        [half_shape(F32), half_shape(BF16), half_shape(BF16)],
        nbytes=9_000_000,
    )(tie(place, gp_last_send, gq_load), x_row, one_keep, one_came, resid_low, hidden_own, down_keep,
      down_came, vectors)
    gu_total = scatter_upper(gu_sum, last_send)
    gp_sum = total_of(gp_own, gp_came[0], tie(gp_last, gu_total))
    gq_all = tie(gq_all, gp_sum)
    count = upper * rows
    gq_came = gq_all[: 2 * count].reshape(2, upper, rows, gq_cols)
    vec_pair = split(joined(vec_pair) + joined(gq_all[2 * count :].reshape(vec_pair.shape)))
    gq_load = load([add_low(gq_keep, gq_came[1])], vec_pair)
    gq_last = mixed_one(gq_load)
    last_came = over_y(tie(last_send, gq_load))
    gp_total = scatter_upper(gp_sum)
    mlp_total = jnp.stack([gu_total, gd_total])

    vec_pair = split(joined(vec_pair) + joined(gq_last[count:].reshape(vec_pair.shape)))
    gq_sum = total_of(gq_own, gq_came[0], gq_last[:count].reshape(upper, rows, gq_cols))
    for b, bits_here in reversed(steps):
        size = gq_sum.shape[0] >> bits_here
        digit = (widx >> b) & ((1 << bits_here) - 1)
        blocks = [gq_sum[i * size : (i + 1) * size] for i in range(1 << bits_here)]
        came = []
        for k in range(1, 1 << bits_here):
            send = choose(digit, [blocks[i ^ k] for i in range(1 << bits_here)])
            came.append(over_wide(load([send.astype(BF16)], vec_pair), k << b))
        gq_sum = choose(digit, blocks)
        vecs = [joined(vec_pair)]
        for each in came:
            gq_sum = gq_sum + each[: size * rows].reshape(gq_sum.shape).astype(F32)
            vecs.append(joined(each[size * rows :].reshape(vec_pair.shape)))
        while len(vecs) > 1:
            vecs = [vecs[i] + vecs[i + 1] for i in range(0, len(vecs), 2)]
        vec_pair = split(vecs[0])
    gq_total = gq_sum[0]
    vec_half = vecs[0]
    vec_grad = vec_half + over_core(vec_half)

    def home(own, came):
        return lax.dynamic_update_slice(own, came[None].astype(own.dtype), (1 - y, 0, 0))

    block_out = home(block_own, last_came[1])
    block_input_gradient = home(grad_own, last_came[0])

    attn_grad = jnp.stack(
        [
            jnp.concatenate(
                [
                    gp_total[:, kind * many : (kind + 1) * many],
                    gq_total[:, kind * HEAD_DIM : (kind + 1) * HEAD_DIM],
                ],
                axis=1,
            )
            for kind in range(3)
        ]
        + [gp_total[:, 3 * many :]]
    )
    mlp_grad = mlp_total
    attn_new, attn_m_new, attn_v_new = adamw_update(
        attn_w, attn_m, attn_v, attn_grad, RATE_MATRIX, DECAY_MATRIX
    )
    mlp_new, mlp_m_new, mlp_v_new = adamw_update(
        mlp_w, mlp_m, mlp_v, mlp_grad, RATE_MATRIX, DECAY_MATRIX
    )
    vec_new, vec_m_new, vec_v_new = adamw_update(vectors, vec_m, vec_v, vec_grad, RATE_VECTOR, 0.0)
    return (
        block_out,
        block_input_gradient,
        attn_grad,
        attn_new,
        attn_m_new,
        attn_v_new,
        mlp_grad,
        mlp_new,
        mlp_m_new,
        mlp_v_new,
        vec_grad,
        vec_new,
        vec_m_new,
        vec_v_new,
    )


def solution(mesh):
    matrix = P(None, "wide", "narrow")
    rows = P("wide", "narrow", None)
    in_specs = (rows, P("wide", None), rows) + (matrix,) * 6 + (P(),) * 3
    out_specs = (rows, rows) + (matrix,) * 8 + (P(),) * 4
    return jax.shard_map(local, mesh=mesh, in_specs=in_specs, out_specs=out_specs, check_vma=False)
```

```python
import functools

import jax
import jax.numpy as jnp
from jax import lax
from jax.experimental import pallas as pl
from jax.experimental.pallas import tpu as pltpu
from jax.sharding import PartitionSpec as P

HEAD_DIM = 64
STEP = 10


EPS_NORM = 1e-06
MASKED_SCORE = -1e30
BETA_ONE = 0.5
BETA_TWO = 0.5
EPS_ADAM = 1e-08
RATE_MATRIX = 0.04
RATE_VECTOR = 0.3
DECAY_MATRIX = 0.05
SCALE = HEAD_DIM ** (-0.5)
TILE = 256
F32 = jnp.float32
BF16 = jnp.bfloat16
AXES = ("wide", "narrow")
COST_SCALE = 1
VMEM_LIMIT = 48 * 1024 * 1024


def adamw_update(weight, first_mom, second, gradient, step_rate, decay_rate):
    first_new = BETA_ONE * first_mom + (1.0 - BETA_ONE) * gradient
    second_new = BETA_TWO * second + (1.0 - BETA_TWO) * gradient * gradient
    corrected = (
        first_new
        / (1.0 - BETA_ONE**STEP)
        / (jnp.sqrt(second_new / (1.0 - BETA_TWO**STEP)) + EPS_ADAM)
    )
    return (weight - step_rate * (corrected + decay_rate * weight), first_new, second_new)


def nn(a, b):
    return lax.dot_general(a, b, (((1,), (0,)), ((), ())), preferred_element_type=F32)


def nt(a, b):
    return lax.dot_general(a, b, (((1,), (1,)), ((), ())), preferred_element_type=F32)


def tn(a, b):
    return lax.dot_general(a, b, (((0,), (0,)), ((), ())), preferred_element_type=F32)


def standardize(v):
    centred = v - jnp.mean(v, axis=-1, keepdims=True)
    inv = lax.rsqrt(jnp.mean(centred * centred, axis=-1, keepdims=True) + EPS_NORM)
    return centred * inv, inv


def norm_back(grad_out, normed, inv, gain):
    scaled = grad_out * gain
    return inv * (
        scaled
        - jnp.mean(scaled, axis=-1, keepdims=True)
        - normed * jnp.mean(scaled * normed, axis=-1, keepdims=True)
    )


def whole(shape):
    return pl.BlockSpec(shape, lambda *_: (0,) * len(shape))


def params(cost=None):
    return pltpu.CompilerParams(
        dimension_semantics=("arbitrary",), vmem_limit_bytes=VMEM_LIMIT
    )


def call(kernel, grid, in_specs, out_specs, out_shape, scratch=(), flops=0, nbytes=0, trans=0):
    return pl.pallas_call(
        kernel,
        grid=grid,
        in_specs=in_specs,
        out_specs=out_specs,
        out_shape=out_shape,
        scratch_shapes=scratch,
        compiler_params=params(),
        cost_estimate=pl.CostEstimate(
            flops=flops // COST_SCALE,
            bytes_accessed=nbytes // COST_SCALE,
            transcendentals=trans // COST_SCALE,
        ),
    )


def placed(kernel, grid, in_specs, out_specs, out_shape, scratch=(), flops=0, nbytes=0, trans=0):
    return pl.pallas_call(
        kernel,
        grid_spec=pltpu.PrefetchScalarGridSpec(
            num_scalar_prefetch=1,
            grid=grid,
            in_specs=in_specs,
            out_specs=out_specs,
            scratch_shapes=scratch,
        ),
        out_shape=out_shape,
        compiler_params=params(),
        cost_estimate=pl.CostEstimate(
            flops=flops // COST_SCALE,
            bytes_accessed=nbytes // COST_SCALE,
            transcendentals=trans // COST_SCALE,
        ),
    )


def head_columns(h, heads):
    return tuple((kind * heads + h) * HEAD_DIM for kind in range(3))


def natural(place_ref, pieces, targets):
    held_ref, from_x_ref, from_y_ref, diagonal_ref = pieces
    even = place_ref[0] == 0
    upper = place_ref[3]
    count, rows, _ = held_ref.shape
    for u in range(count):
        src = lax.bitwise_xor(upper, jnp.int32(u))
        for x in range(2):
            at = slice((2 * u + x) * rows, (2 * u + x + 1) * rows)
            near = even if x == 0 else jnp.logical_not(even)
            targets(0, at, jnp.where(near, held_ref[src], from_x_ref[src]))
            targets(1, at, jnp.where(near, from_y_ref[src], diagonal_ref[src]))


def pick_row(place_ref, tile, part, refs):
    keep_ref, came_ref, keep_core_ref, came_core_ref = refs
    same_y = tile // 2 == place_ref[2]
    same_core = tile % 2 == place_ref[1]
    return jnp.where(
        same_y,
        jnp.where(same_core, keep_ref[part], keep_core_ref[part]),
        jnp.where(same_core, came_ref[part], came_core_ref[part]),
    )


def qkv_kernel(place_ref, *refs):
    rows = refs[:4]
    pieces = refs[4:8]
    vec_ref, bias_ref, x_ref, dy_ref, a_ref, qkv_ref, w0_ref, w1_ref, o0_ref, o1_ref = refs[8:]
    cols = w0_ref.shape[1]

    @pl.when(pl.program_id(0) == 0)
    def _():
        def store(j, at, value):
            (w0_ref, w1_ref)[j][at] = value[:, :cols]
            (o0_ref, o1_ref)[j][at] = value[:, cols:]

        natural(place_ref, pieces, store)

    x = pick_row(place_ref, pl.program_id(0), 0, rows)
    x_ref[...] = x
    dy_ref[...] = pick_row(place_ref, pl.program_id(0), 1, rows)
    normed, _ = standardize(x.astype(F32))
    low = (normed * vec_ref[0:1] + vec_ref[1:2]).astype(BF16)
    a_ref[...] = low
    for j, w_ref in enumerate((w0_ref, w1_ref)):
        qkv_ref[j] = (nn(low, w_ref[...]) + bias_ref[j : j + 1]).astype(BF16)


def column(row):
    return jnp.broadcast_to(row, (128, row.shape[1])).T[:, :1]


def attend_kernel(last, qkv_q_ref, qkv_ref, seg_tile_ref, seg_row_ref, *refs):
    if last:
        ctx_in_ref, o0_ref, o1_ref, ctx_ref, lse_ref, out_ref = refs
    else:
        ctx_ref, lse_ref = refs
    cols = ctx_ref.shape[1]
    heads = cols // HEAD_DIM
    same = column(seg_tile_ref[...]) == seg_row_ref[...]
    lane = lax.broadcasted_iota(jnp.int32, (TILE, 128), 1)
    totals = jnp.zeros((TILE, 128), F32)
    for h in range(heads):
        lo = h * HEAD_DIM
        at_q, at_k, at_v = head_columns(h, heads)
        q = qkv_q_ref[:, at_q : at_q + HEAD_DIM]
        k = qkv_ref[:, at_k : at_k + HEAD_DIM]
        v = qkv_ref[:, at_v : at_v + HEAD_DIM]
        s = jnp.where(same, nt(q, k) * SCALE, MASKED_SCORE)
        top = jnp.max(s, axis=-1, keepdims=True)
        e = jnp.exp(s - top)
        total = jnp.sum(e, axis=-1, keepdims=True)
        o = nn(e.astype(BF16), v) / total
        ctx_ref[:, lo : lo + HEAD_DIM] = o.astype(BF16)
        totals = jnp.where(lane == h, top + jnp.log(total), totals)
    lse_ref[...] = totals.T[: lse_ref.shape[0]]
    if last:
        out_ref[...] = (nt(ctx_in_ref[...], o0_ref[...]) + nt(ctx_ref[...], o1_ref[...])).astype(BF16)


def sort_grad(place_ref, mine, others, own_ref, send_ref, keep_ref, at):
    even = place_ref[0] == 0
    first = place_ref[1] == 0
    rows = own_ref.shape[1]
    for u in range(own_ref.shape[0]):
        lo = slice(2 * u * rows, (2 * u + 1) * rows)
        hi = slice((2 * u + 1) * rows, (2 * u + 2) * rows)
        own_ref[u, :, at] = jnp.where(even, mine[lo], mine[hi])
        to_x = jnp.where(even, mine[hi], mine[lo])
        to_y = jnp.where(even, others[lo], others[hi])
        send_ref[0, u, :, at] = jnp.where(first, to_y, to_x)
        keep_ref[u, :, at] = jnp.where(first, to_x, to_y)
        send_ref[1, u, :, at] = jnp.where(even, others[hi], others[lo])


def add_grad(total_ref, j, left, right):
    part = tn(left, right)

    @pl.when(pl.program_id(0) == 0)
    def _():
        total_ref[j] = part

    @pl.when(pl.program_id(0) > 0)
    def _():
        total_ref[j] += part


def up_kernel(place_ref, x_ref, p0_ref, p1_ref, dy_ref, vec_ref, bu_ref, *refs):
    pieces = refs[:4]
    (a_ref, normed_ref, inv_ref, z_ref, slope_ref, own_ref, u0_ref, u1_ref,
     g_own_ref, g_send_ref, g_keep_ref, total_ref) = refs[4:]
    tile = pl.program_id(0)

    @pl.when(tile == 0)
    def _():
        def store(j, at, value):
            (u0_ref, u1_ref)[j][at] = value

        natural(place_ref, pieces, store)

    h = x_ref[...].astype(F32) + (p0_ref[...].astype(F32) + p1_ref[...].astype(F32)) + vec_ref[4:5]

    @pl.when(tile % 2 == place_ref[1])
    def _():
        own_ref[...] = h

    normed, inv = standardize(h)
    normed_ref[...] = normed.astype(BF16)
    inv_ref[...] = inv
    a = (normed * vec_ref[2:3] + vec_ref[3:4]).astype(BF16)
    a_ref[...] = a
    dy = dy_ref[...]
    for j, u_ref in enumerate((u0_ref, u1_ref)):
        u = nn(a, u_ref[...]) + bu_ref[j : j + 1]
        cdf = 0.5 + 0.5 * lax.erf(u * 0.7071067811865476)
        z = (u * cdf).astype(BF16)
        z_ref[j] = z
        slope_ref[j] = (cdf + u * (0.3989422804014327 * jnp.exp(-0.5 * u * u))).astype(BF16)
        add_grad(total_ref, j, dy, z)

    @pl.when(tile == pl.num_programs(0) - 1)
    def _():
        sort_grad(place_ref, total_ref[0].astype(BF16), total_ref[1].astype(BF16),
                  g_own_ref, g_send_ref, g_keep_ref, slice(None))


def down_kernel(place_ref, dy_ref, z_ref, slope_ref, u0_ref, u1_ref, *refs):
    pieces = refs[:4]
    du_ref, keep_ref, send_ref, da_ref, gbu_ref, d0_ref, d1_ref = refs[4:]
    tile = pl.program_id(0)

    @pl.when(tile == 0)
    def _():
        gbu_ref[...] = jnp.zeros_like(gbu_ref)

        def store(j, at, value):
            (d0_ref, d1_ref)[j][at] = value

        natural(place_ref, pieces, store)

    dy = dy_ref[...]
    down = jnp.zeros(da_ref.shape, F32)
    da = jnp.zeros(da_ref.shape, F32)
    for j, (u_ref, d_ref) in enumerate(((u0_ref, d0_ref), (u1_ref, d1_ref))):
        du = (nn(dy, d_ref[...]) * slope_ref[j].astype(F32)).astype(BF16)
        du_ref[j] = du
        gbu_ref[j : j + 1] += jnp.sum(du.astype(F32), axis=0, keepdims=True)
        down += nt(z_ref[j], d_ref[...])
        da += nt(du, u_ref[...])
    da_ref[...] = da.astype(BF16)
    down = down.astype(BF16)
    mine = tile % 2 == place_ref[1]

    @pl.when(mine)
    def _():
        keep_ref[...] = down

    @pl.when(jnp.logical_not(mine))
    def _():
        send_ref[...] = down


def grad_kernel(place_ref, left_ref, right_ref, own_ref, send_ref, keep_ref, turned_ref):
    @pl.when(pl.program_id(0) == 0)
    def _():
        turned_ref[...] = left_ref[...].T

    turned = turned_ref[...]
    mine = nn(turned, right_ref[0]).astype(BF16)
    others = nn(turned, right_ref[1]).astype(BF16)
    sort_grad(place_ref, mine, others, own_ref, send_ref, keep_ref, slice(None))


def two_grads_kernel(place_ref, left_ref, dh_ref, dqkv0_ref, dqkv1_ref, ctx0_ref, ctx1_ref,
                     own_ref, send_ref, keep_ref):
    many = dqkv0_ref.shape[1]
    turned = left_ref[...].T
    mine = nn(turned, dqkv0_ref[...]).astype(BF16)
    others = nn(turned, dqkv1_ref[...]).astype(BF16)
    sort_grad(place_ref, mine, others, own_ref, send_ref, keep_ref, slice(0, many))
    turned = dh_ref[...].T
    mine = nn(turned, ctx0_ref[...]).astype(BF16)
    others = nn(turned, ctx1_ref[...]).astype(BF16)
    sort_grad(place_ref, mine, others, own_ref, send_ref, keep_ref, slice(many, None))


def mid_kernel(normed_ref, inv_ref, dy_ref, da0_ref, da1_ref, ctx0_ref, ctx1_ref, vec_ref,
               o0_ref, o1_ref, dh_ref, dctx_ref, delta_ref, sums_ref):
    @pl.when(pl.program_id(0) == 0)
    def _():
        sums_ref[...] = jnp.zeros_like(sums_ref)

    normed = normed_ref[...].astype(F32)
    da = da0_ref[...].astype(F32) + da1_ref[...].astype(F32)
    dy = dy_ref[...].astype(F32)
    dh = dy + norm_back(da, normed, inv_ref[...], vec_ref[2:3])
    low = dh.astype(BF16)
    dh_ref[...] = low
    sums_ref[0:1] += jnp.sum(da * normed, axis=0, keepdims=True)
    sums_ref[1:2] += jnp.sum(da, axis=0, keepdims=True)
    sums_ref[2:3] += jnp.sum(dh, axis=0, keepdims=True)
    sums_ref[3:4] += jnp.sum(dy, axis=0, keepdims=True)
    cols = ctx0_ref.shape[1]
    head = lax.broadcasted_iota(jnp.int32, (8, cols), 0)
    owner = lax.broadcasted_iota(jnp.int32, (8, cols), 1) // HEAD_DIM
    member = jnp.where(head == owner, 1.0, 0.0).astype(BF16)
    for j, (o_ref, ctx_ref) in enumerate(((o0_ref, ctx0_ref), (o1_ref, ctx1_ref))):
        dctx = nn(low, o_ref[...]).astype(BF16)
        dctx_ref[j] = dctx
        prod = dctx.astype(F32) * ctx_ref[...].astype(F32)
        high = prod.astype(BF16)
        rest = (prod - high.astype(F32)).astype(BF16)
        delta_ref[j] = nt(member, high) + nt(member, rest)


def attend_back_kernel(heads, qkv_ref, dctx_ref, lse_ref, delta_ref, seg_row_ref,
                       dqkv_ref, sums_ref, dk_ref, dv_ref):
    length = qkv_ref.shape[0]
    seg_col = column(seg_row_ref[...])
    for h in range(heads):
        lo = h * HEAD_DIM
        at_q, at_k, at_v = head_columns(h, heads)
        k = qkv_ref[:, at_k : at_k + HEAD_DIM]
        v = qkv_ref[:, at_v : at_v + HEAD_DIM]
        for t in range(length // TILE):
            rows = slice(t * TILE, (t + 1) * TILE)
            q = qkv_ref[rows, at_q : at_q + HEAD_DIM]
            dc = dctx_ref[rows, lo : lo + HEAD_DIM]
            same = seg_col == seg_row_ref[:, rows]
            s = jnp.where(same, nt(k, q) * SCALE, MASKED_SCORE)
            p = jnp.exp(s - lse_ref[h : h + 1, rows])
            ds = (p * (nt(v, dc) - delta_ref[h : h + 1, rows])).astype(BF16)
            dv = nn(p.astype(BF16), dc)
            dk = nn(ds, q)
            if t == 0:
                dv_ref[...] = dv
                dk_ref[...] = dk
            else:
                dv_ref[...] += dv
                dk_ref[...] += dk
            dqkv_ref[rows, at_q : at_q + HEAD_DIM] = (tn(ds, k) * SCALE).astype(BF16)
        dqkv_ref[:, at_k : at_k + HEAD_DIM] = (dk_ref[...] * SCALE).astype(BF16)
        dqkv_ref[:, at_v : at_v + HEAD_DIM] = dv_ref[...].astype(BF16)
    sums_ref[...] = jnp.sum(dqkv_ref[...].astype(F32), axis=0, keepdims=True)


def input_grad_kernel(place_ref, x_ref, g0_ref, g1_ref, w0_ref, w1_ref, keep_ref, send_ref,
                      sums_ref):
    tile = pl.program_id(0)

    @pl.when(tile == 0)
    def _():
        sums_ref[...] = jnp.zeros_like(sums_ref)

    out = nt(g0_ref[...], w0_ref[...]) + nt(g1_ref[...], w1_ref[...])
    normed, _ = standardize(x_ref[...].astype(F32))
    sums_ref[0:1] += jnp.sum(out * normed, axis=0, keepdims=True)
    sums_ref[1:2] += jnp.sum(out, axis=0, keepdims=True)
    out = out.astype(BF16)
    mine = tile % 2 == place_ref[1]

    @pl.when(mine)
    def _():
        keep_ref[...] = out

    @pl.when(jnp.logical_not(mine))
    def _():
        send_ref[...] = out


def final_kernel(place_ref, x_ref, da0_ref, da1_ref, dh_ref, own_ref, keep_ref, came_ref, vec_ref,
                 dx_ref, out_ref, send_ref):
    normed, inv = standardize(x_ref[...].astype(F32))
    da = da0_ref[...].astype(F32) + da1_ref[...].astype(F32)
    dx = dh_ref[...].astype(F32) + norm_back(da, normed, inv, vec_ref[0:1])
    dx_ref[...] = dx
    out = own_ref[...] + (keep_ref[...].astype(F32) + came_ref[...].astype(F32)) + vec_ref[5:6]
    out = out.astype(BF16)
    out_ref[...] = out

    @pl.when(pl.program_id(0) != place_ref[2])
    def _():
        send_ref[0] = dx.astype(BF16)
        send_ref[1] = out


def local(
    tokens,
    segment_ids,
    cotangent,
    attn_w,
    attn_m,
    attn_v,
    mlp_w,
    mlp_m,
    mlp_v,
    vectors,
    vec_m,
    vec_v,
):
    wide = lax.axis_size("wide")
    narrow = lax.axis_size("narrow")
    widx = lax.axis_index("wide")
    nidx = lax.axis_index("narrow")
    y = nidx // 2
    c = nidx % 2
    other = (1 - y) * 2 + c
    xbit = widx % 2
    even = xbit == 0
    first_core = c == 0
    first_y = y == 0
    _, shard_len, width = tokens.shape
    length = segment_ids.shape[1]
    cols = attn_w.shape[2]
    rows = attn_w.shape[1]
    hidden = mlp_w.shape[2]
    heads = cols // HEAD_DIM
    bits = wide.bit_length() - 1
    upper = wide // 2
    steps = [(b, min(2, bits - b)) for b in range(1, bits, 2)]

    def swap(value, partner):
        pairs = [
            (w * narrow + n, (lambda t: t[0] * narrow + t[1])(partner(w, n)))
            for w in range(wide)
            for n in range(narrow)
        ]
        return lax.ppermute(value, AXES, pairs)

    def over_core(value):
        return swap(value, lambda w, n: (w, n ^ 1))

    def over_y(value):
        return swap(value, lambda w, n: (w, n ^ 2))

    def over_x(value):
        return swap(value, lambda w, n: (w ^ 1, n))

    def over_wide(value, mask):
        return swap(value, lambda w, n: (w ^ mask, n))

    def mixed_one(value):
        return swap(value, lambda w, n: (w ^ 1, n) if n % 2 == 0 else (w, n ^ 2))

    def mixed_two(value):
        return swap(value, lambda w, n: (w ^ 1, n) if n % 2 == 1 else (w, n ^ 2))

    def tie(value, *deps):
        return lax.optimization_barrier((value, *deps))[0]

    def pair(flag, first, second, axis):
        return jnp.stack(
            [jnp.where(flag, first, second), jnp.where(flag, second, first)], axis=axis
        )

    def add_low(keep, came):
        return (keep.astype(F32) + came.astype(F32)).astype(BF16)

    def total_of(own, came, last):
        return own.astype(F32) + came.astype(F32) + last.astype(F32)

    def choose(index, values):
        picked = values[0]
        for i in range(1, len(values)):
            picked = jnp.where(index == i, values[i], picked)
        return picked

    def gather_upper(shard):
        held = shard[None]
        for b, count in steps:
            came = [over_wide(held, k << b) for k in range(1, 1 << count)]
            held = jnp.concatenate([held, *came], axis=0)
        return held

    def scatter_upper(total, *deps):
        for b, count in reversed(steps):
            size = total.shape[0] >> count
            digit = (widx >> b) & ((1 << count) - 1)
            blocks = [total[i * size : (i + 1) * size] for i in range(1 << count)]
            came = []
            for k in range(1, 1 << count):
                send = choose(digit, [blocks[i ^ k] for i in range(1 << count)])
                came.append(over_wide(send.astype(BF16), k << b))
            if deps:
                came = lax.optimization_barrier((*came, *deps))[: len(came)]
            total = choose(digit, blocks).astype(F32)
            for each in came:
                total = total + each.astype(F32)
        return total

    def both(vector, size):
        return jnp.stack(
            [
                lax.dynamic_slice_in_dim(vector, nidx * size, size),
                lax.dynamic_slice_in_dim(vector, other * size, size),
            ]
        )

    tiles = length // TILE
    tile_spec = pl.BlockSpec((TILE, width), lambda t, *_: (t, 0))
    up_spec = whole((width, hidden))
    qkv_cols = 3 * cols
    matmul = 2 * length * width
    row_shape = jax.ShapeDtypeStruct((length, width), BF16)
    zero = jnp.int32(0)
    place = jnp.stack([xbit, c, y, widx // 2, zero, zero, zero, zero]).astype(jnp.int32)

    def spread_over_plane(held):
        from_x = over_x(held)
        from_y = over_y(held)
        return from_x, from_y

    def turn(from_x, from_y):
        return jnp.where(first_core, from_x, from_y)

    attn_low = attn_w.astype(BF16)
    attn_shard = jnp.concatenate([attn_low[i] for i in range(4)], axis=-1)

    mlp_low = mlp_w.astype(BF16)
    a_held = gather_upper(attn_shard)

    def row_pair(first):
        return jnp.stack(
            [jnp.where(first, v[0], v[1]) for v in (tokens, cotangent)]
        )

    rows_send = row_pair(jnp.logical_not(first_y))
    rows_came = over_y(tie(rows_send, attn_shard))
    rows_keep = row_pair(first_y)
    rows_keep_core = over_core(rows_keep)

    a_held, rows_came = lax.optimization_barrier((a_held, rows_came))
    a_x, a_y = spread_over_plane(a_held)
    rows_came_core = over_core(rows_came)
    u_held = gather_upper(tie(mlp_low[0], a_held, rows_came_core, rows_keep_core))
    a_turn = turn(*lax.optimization_barrier((a_x, a_y, rows_came_core, rows_keep_core))[:2])
    a_diagonal = mixed_two(a_turn)
    u_x, u_y = spread_over_plane(u_held)
    d_first = mlp_low[1][None]
    d_first_came = over_wide(tie(d_first, u_held), 2)

    seg_own = lax.dynamic_index_in_dim(segment_ids, y, 0, False)
    seg_row = seg_own[None, :]
    query_bias = both(vectors[6], cols)
    value_bias = both(vectors[7], cols)
    no_bias = jnp.zeros_like(query_bias)
    qkv_bias = jnp.concatenate([query_bias, no_bias, value_bias], axis=1)
    up_bias = both(vectors[8:].reshape(-1), hidden)

    part_spec = whole((2, shard_len, width))
    piece_spec = whole((upper, rows, width))
    attn_shapes = [(width, qkv_cols), (width, qkv_cols), (width, cols), (width, cols)]
    x_row, dy_row, normed_low, qkv, w_mine, w_others, o_mine, o_others = placed(
        qkv_kernel,
        (tiles,),
        [part_spec] * 4 + [piece_spec] * 4 + [whole(vectors.shape), whole((2, qkv_cols))],
        [tile_spec] * 3 + [pl.BlockSpec((2, TILE, qkv_cols), lambda t, p: (0, t, 0))]
        + [whole(shape) for shape in attn_shapes],
        [row_shape] * 3 + [jax.ShapeDtypeStruct((2, length, qkv_cols), BF16)]
        + [jax.ShapeDtypeStruct(shape, BF16) for shape in attn_shapes],
    )(tie(place, u_held), rows_keep, rows_came, rows_keep_core, rows_came_core, a_held, a_x, a_y,
      a_diagonal, vectors, qkv_bias)

    ctx_spec = pl.BlockSpec((TILE, cols), lambda t: (t, 0))
    lse_spec = pl.BlockSpec((8, TILE), lambda t: (0, t))
    ctx_shape = jax.ShapeDtypeStruct((length, cols), BF16)
    lse_shape = jax.ShapeDtypeStruct((8, length), F32)
    o_spec = whole((width, cols))

    def attend(j, segments, extra):
        last = bool(extra)
        in_specs = [
            pl.BlockSpec((None, TILE, qkv_cols), lambda t: (j, t, 0)),
            pl.BlockSpec((None, length, qkv_cols), lambda t: (j, 0, 0)),
            pl.BlockSpec((1, TILE), lambda t: (0, t)),
            whole((1, length)),
        ]
        out_specs = [ctx_spec, lse_spec]
        out_shape = [ctx_shape, lse_shape]
        if last:
            in_specs += [ctx_spec, o_spec, o_spec]
            out_specs += [tile_spec]
            out_shape += [row_shape]
        return call(
            functools.partial(attend_kernel, last),
            (tiles,),
            in_specs,
            out_specs,
            out_shape,
            flops=4 * length * length * cols,
            nbytes=6_000_000,
            trans=heads * length * length,
        )(qkv, qkv, segments, segments, *extra)

    d_first, d_first_came = lax.optimization_barrier((d_first, d_first_came, qkv))[:2]
    d_second = jnp.concatenate([d_first, d_first_came], axis=0)
    d_second_came = over_wide(d_second, 4)
    ctx_mine, lse_mine = attend(0, tie(seg_row, d_second), ())
    d_second, d_second_came = lax.optimization_barrier((d_second, d_second_came, ctx_mine))[:2]
    d_second = jnp.concatenate([d_second, d_second_came], axis=0)

    def gather_rest(held):
        for b in range(3, bits):
            held = jnp.concatenate([held, over_wide(held, 1 << b)], axis=0)
        return held

    d_held = d_second if bits == 3 else gather_rest(d_second)
    u_turn = turn(*lax.optimization_barrier((u_x, u_y, ctx_mine))[:2])
    u_diagonal = mixed_two(u_turn)
    d_x, d_y = spread_over_plane(tie(d_held, u_turn))
    d_diagonal = swap(tie(d_held, u_turn), lambda w, n: (w ^ 1, n ^ 2))
    ctx_others, lse_others, out_part = attend(
        1, tie(seg_row, u_turn, d_held), (ctx_mine, o_mine, o_others)
    )
    out_part, u_diagonal = lax.optimization_barrier((out_part, u_diagonal))
    out_came = over_core(out_part)

    pair_spec = pl.BlockSpec((2, TILE, hidden), lambda t, *_: (0, t, 0))
    pair_shape = jax.ShapeDtypeStruct((2, length, hidden), BF16)
    half_spec = pl.BlockSpec((None, TILE, width), lambda t, *_: (t // 2, 0, 0))
    up_shape = jax.ShapeDtypeStruct((width, hidden), BF16)

    def half_shape(dtype):
        return jax.ShapeDtypeStruct((2, shard_len, width), dtype)

    grad_specs = [piece_spec, whole((2, upper, rows, width)), piece_spec]
    grad_shapes = [
        jax.ShapeDtypeStruct((upper, rows, hidden), BF16),
        jax.ShapeDtypeStruct((2, upper, rows, hidden), BF16),
        jax.ShapeDtypeStruct((upper, rows, hidden), BF16),
    ]
    (second_low, second_normed, second_inv, activated, slope, hidden_own, u_mine, u_others,
     gd_own, gd_send, gd_keep) = placed(
        up_kernel,
        (tiles,),
        [tile_spec] * 4 + [whole(vectors.shape), whole((2, hidden))] + [piece_spec] * 4,
        [tile_spec, tile_spec, pl.BlockSpec((TILE, 1), lambda t, p: (t, 0)), pair_spec, pair_spec,
         half_spec, up_spec, up_spec] + grad_specs,
        [row_shape, row_shape, jax.ShapeDtypeStruct((length, 1), F32), pair_shape, pair_shape,
         half_shape(F32), up_shape, up_shape] + grad_shapes,
        scratch=[pltpu.VMEM((2, width, hidden), F32)],
        flops=2 * matmul * 2 * hidden,
        nbytes=20_000_000,
        trans=4 * length * hidden,
    )(place, x_row, out_part, out_came, dy_row, vectors, up_bias, u_held, u_x, u_y, u_diagonal)
    gd_came = mixed_two(gd_send)

    def weight_grad(where, left, right, block):
        spec = pl.BlockSpec((upper, rows, block), lambda i, p: (0, 0, i))
        return placed(
            grad_kernel,
            (hidden // block,),
            [whole((length, width)), pl.BlockSpec((2, length, block), lambda i, p: (0, 0, i))],
            [spec, pl.BlockSpec((2, upper, rows, block), lambda i, p: (0, 0, 0, i)), spec],
            grad_shapes,
            scratch=[pltpu.VMEM((width, length), BF16)],
            flops=matmul * 2 * hidden,
            nbytes=8_000_000,
        )(where, left, right)

    def attn_weight_grad(dqkv_first, dqkv_second):
        return placed(
            two_grads_kernel,
            (1,),
            [whole((length, width))] * 2 + [whole((length, qkv_cols))] * 2
            + [whole((length, cols))] * 2,
            grad_specs,
            grad_shapes,
            flops=matmul * 2 * hidden,
            nbytes=8_000_000,
        )(place, normed_low, resid_low, dqkv_first, dqkv_second, ctx_mine, ctx_others)

    grad_pre, down_keep, down_send, second_part, up_bias_sums = placed(
        down_kernel,
        (tiles,),
        [tile_spec, pair_spec, pair_spec, up_spec, up_spec] + [piece_spec] * 4,
        [pair_spec, half_spec, half_spec, tile_spec, whole((2, hidden))],
        [pair_shape, half_shape(BF16), half_shape(BF16), row_shape,
         jax.ShapeDtypeStruct((2, hidden), F32)],
        scratch=[pltpu.VMEM((width, hidden), BF16)] * 2,
        flops=3 * matmul * 2 * hidden,
        nbytes=20_000_000,
    )(tie(place, gd_send), dy_row, activated, slope, u_mine, u_others, d_held, d_x, d_y, d_diagonal)
    second_part, gd_came = lax.optimization_barrier((second_part, gd_came))

    down_came = over_core(down_send)
    second_came = over_core(second_part)
    gd_last_send = add_low(gd_keep, gd_came[1])
    gd_last = mixed_one(gd_last_send)
    gu_own, gu_send, gu_keep = weight_grad(
        tie(place, gd_last_send), second_low, grad_pre, 256
    )
    gu_came = mixed_two(gu_send)

    delta_spec = pl.BlockSpec((2, 8, TILE), lambda t: (0, 0, t))
    resid_low, grad_ctx, delta, mid_sums = call(
        mid_kernel,
        (tiles,),
        [tile_spec, pl.BlockSpec((TILE, 1), lambda t: (t, 0))] + [tile_spec] * 3
        + [ctx_spec, ctx_spec, whole(vectors.shape), o_spec, o_spec],
        [tile_spec, pl.BlockSpec((2, TILE, cols), lambda t: (0, t, 0)), delta_spec,
         whole((8, width))],
        [row_shape,
         jax.ShapeDtypeStruct((2, length, cols), BF16),
         jax.ShapeDtypeStruct((2, 8, length), F32),
         jax.ShapeDtypeStruct((8, width), F32)],
        flops=matmul * 2 * cols,
        nbytes=10_000_000,
    )(second_normed, second_inv, dy_row, second_part, second_came, ctx_mine, ctx_others,
      tie(vectors, gu_send, down_came), o_mine, o_others)

    gd_sum = total_of(gd_own, gd_came[0], tie(gd_last, grad_ctx))
    def attend_back(j, lse, segments):
        return call(
            functools.partial(attend_back_kernel, heads),
            (1,),
            [pl.BlockSpec((None, length, qkv_cols), lambda i: (j, 0, 0)),
             pl.BlockSpec((None, length, cols), lambda i: (j, 0, 0)),
             whole((8, length)),
             pl.BlockSpec((None, 8, length), lambda i: (j, 0, 0)),
             whole((1, length))],
            [whole((length, qkv_cols)), whole((1, qkv_cols))],
            [jax.ShapeDtypeStruct((length, qkv_cols), BF16),
             jax.ShapeDtypeStruct((1, qkv_cols), F32)],
            scratch=[pltpu.VMEM((length, HEAD_DIM), F32), pltpu.VMEM((length, HEAD_DIM), F32)],
            flops=10 * length * length * cols,
            nbytes=8_000_000,
            trans=heads * length * length,
        )(qkv, grad_ctx, lse, delta, segments)

    dqkv_mine, sums_mine = attend_back(0, lse_mine, tie(seg_row, gd_sum))
    gd_total = scatter_upper(gd_sum, dqkv_mine)
    gu_came = tie(gu_came, dqkv_mine)
    gu_last_send = add_low(gu_keep, gu_came[1])
    gu_last = mixed_one(gu_last_send)
    dqkv_others, sums_others = attend_back(1, lse_others, tie(seg_row, gu_last_send, gd_total))
    ga_own, ga_send, ga_keep = attn_weight_grad(dqkv_mine, dqkv_others)
    ga_came = mixed_two(ga_send)
    gu_sum = total_of(gu_own, gu_came[0], tie(gu_last, ga_send))

    half_out = pl.BlockSpec((None, TILE, width), lambda t, p: (t // 2, 0, 0))
    one_keep, one_send, one_sums = placed(
        input_grad_kernel,
        (tiles,),
        [tile_spec] + [pl.BlockSpec((TILE, qkv_cols), lambda t, p: (t, 0))] * 2
        + [whole((width, qkv_cols))] * 2,
        [half_out] * 2 + [whole((8, width))],
        [half_shape(BF16)] * 2 + [jax.ShapeDtypeStruct((8, width), F32)],
        flops=matmul * 2 * qkv_cols,
        nbytes=8_000_000,
    )(tie(place, gu_sum), x_row, dqkv_mine, dqkv_others, w_mine, w_others)
    one_came = over_core(one_send)

    def spread(mine, others, size):
        empty = jnp.zeros((size * narrow,), F32)
        empty = lax.dynamic_update_slice_in_dim(empty, mine, nidx * size, 0)
        return lax.dynamic_update_slice_in_dim(empty, others, other * size, 0)

    vec_part = jnp.concatenate(
        [
            one_sums[:2],
            jnp.where(first_core, mid_sums[:4], 0.0),
            spread(sums_mine[0, :cols], sums_others[0, :cols], cols)[None],
            spread(sums_mine[0, 2 * cols :], sums_others[0, 2 * cols :], cols)[None],
            spread(up_bias_sums[0], up_bias_sums[1], hidden).reshape(-1, width),
        ],
        axis=0,
    )

    vec_came = mixed_two(vec_part)

    own_block = pl.BlockSpec((TILE, width), lambda t, p: (2 * t + p[1], 0))
    half_in = pl.BlockSpec((None, TILE, width), lambda t, p: (t, 0, 0))
    grad_own, block_own, last_send = placed(
        final_kernel,
        (2,),
        [own_block, half_in, half_in, own_block] + [half_in] * 3 + [whole(vectors.shape)],
        [half_in, half_in, whole((2, shard_len, width))],
        [half_shape(F32), half_shape(BF16), half_shape(BF16)],
        nbytes=9_000_000,
    )(tie(place, vec_part), x_row, one_keep, one_came, resid_low, hidden_own, down_keep,
      down_came, vectors)

    ga_came, vec_came, last_send = lax.optimization_barrier((ga_came, vec_came, last_send))
    ga_send = add_low(ga_keep, ga_came[1])
    ga_last = mixed_one(ga_send)
    vec_grad = tie(vec_part + vec_came, ga_send)
    vec_came = mixed_one(vec_grad)
    last_came = over_y(tie(last_send, ga_send))
    gu_total = scatter_upper(gu_sum, ga_send)
    vec_grad = tie(vec_grad + vec_came, gu_total)
    for b, count in steps:
        terms = [vec_grad] + [over_wide(vec_grad, k << b) for k in range(1, 1 << count)]
        while len(terms) > 1:
            terms = [terms[i] + terms[i + 1] for i in range(0, len(terms), 2)]
        vec_grad = terms[0]
    ga_last = tie(ga_last, gu_total)
    ga_sum = scatter_upper(total_of(ga_own, ga_came[0], ga_last))
    vec_grad = vec_grad + over_core(vec_grad)
    attn_total = ga_sum[0]
    mlp_total = jnp.concatenate([gu_total, gd_total], axis=0)

    def home(own, came):
        return lax.dynamic_update_slice(own, came[None].astype(own.dtype), (1 - y, 0, 0))

    block_out = home(block_own, last_came[1])
    block_input_gradient = home(grad_own, last_came[0])

    attn_grad = jnp.stack([attn_total[:, i * cols : (i + 1) * cols] for i in range(4)])
    mlp_grad = mlp_total
    attn_new, attn_m_new, attn_v_new = adamw_update(
        attn_w, attn_m, attn_v, attn_grad, RATE_MATRIX, DECAY_MATRIX
    )
    mlp_new, mlp_m_new, mlp_v_new = adamw_update(
        mlp_w, mlp_m, mlp_v, mlp_grad, RATE_MATRIX, DECAY_MATRIX
    )
    vec_new, vec_m_new, vec_v_new = adamw_update(vectors, vec_m, vec_v, vec_grad, RATE_VECTOR, 0.0)
    return (
        block_out,
        block_input_gradient,
        attn_grad,
        attn_new,
        attn_m_new,
        attn_v_new,
        mlp_grad,
        mlp_new,
        mlp_m_new,
        mlp_v_new,
        vec_grad,
        vec_new,
        vec_m_new,
        vec_v_new,
    )


def solution(mesh):
    matrix = P(None, "wide", "narrow")
    rows = P("wide", "narrow", None)
    in_specs = (rows, P("wide", None), rows) + (matrix,) * 6 + (P(),) * 3
    out_specs = (rows, rows) + (matrix,) * 8 + (P(),) * 4
    return jax.shard_map(local, mesh=mesh, in_specs=in_specs, out_specs=out_specs, check_vma=False)
```

```python
import functools

import jax
import jax.numpy as jnp
from jax import lax
from jax.experimental import pallas as pl
from jax.experimental.pallas import tpu as pltpu
from jax.sharding import PartitionSpec as P

HEAD_DIM = 64
STEP = 10


EPS_NORM = 1e-06
MASKED_SCORE = -1e30
BETA_ONE = 0.5
BETA_TWO = 0.5
EPS_ADAM = 1e-08
RATE_MATRIX = 0.04
RATE_VECTOR = 0.3
DECAY_MATRIX = 0.05
SCALE = HEAD_DIM ** (-0.5)
TILE = 256
F32 = jnp.float32
BF16 = jnp.bfloat16
AXES = ("wide", "narrow")
COST_SCALE = 1
VMEM_LIMIT = 48 * 1024 * 1024


def adamw_update(weight, first_mom, second, gradient, step_rate, decay_rate):
    first_new = BETA_ONE * first_mom + (1.0 - BETA_ONE) * gradient
    second_new = BETA_TWO * second + (1.0 - BETA_TWO) * gradient * gradient
    corrected = (
        first_new
        / (1.0 - BETA_ONE**STEP)
        / (jnp.sqrt(second_new / (1.0 - BETA_TWO**STEP)) + EPS_ADAM)
    )
    return (weight - step_rate * (corrected + decay_rate * weight), first_new, second_new)


def nn(a, b):
    return lax.dot_general(a, b, (((1,), (0,)), ((), ())), preferred_element_type=F32)


def nt(a, b):
    return lax.dot_general(a, b, (((1,), (1,)), ((), ())), preferred_element_type=F32)


def tn(a, b):
    return lax.dot_general(a, b, (((0,), (0,)), ((), ())), preferred_element_type=F32)


def standardize(v):
    centred = v - jnp.mean(v, axis=-1, keepdims=True)
    inv = lax.rsqrt(jnp.mean(centred * centred, axis=-1, keepdims=True) + EPS_NORM)
    return centred * inv, inv


def norm_back(grad_out, normed, inv, gain):
    scaled = grad_out * gain
    return inv * (
        scaled
        - jnp.mean(scaled, axis=-1, keepdims=True)
        - normed * jnp.mean(scaled * normed, axis=-1, keepdims=True)
    )


def whole(shape):
    return pl.BlockSpec(shape, lambda *_: (0,) * len(shape))


def params(cost=None):
    return pltpu.CompilerParams(
        dimension_semantics=("arbitrary",), vmem_limit_bytes=VMEM_LIMIT
    )


def call(kernel, grid, in_specs, out_specs, out_shape, scratch=(), flops=0, nbytes=0, trans=0):
    return pl.pallas_call(
        kernel,
        grid=grid,
        in_specs=in_specs,
        out_specs=out_specs,
        out_shape=out_shape,
        scratch_shapes=scratch,
        compiler_params=params(),
        cost_estimate=pl.CostEstimate(
            flops=flops // COST_SCALE,
            bytes_accessed=nbytes // COST_SCALE,
            transcendentals=trans // COST_SCALE,
        ),
    )


def placed(kernel, grid, in_specs, out_specs, out_shape, scratch=(), flops=0, nbytes=0, trans=0):
    return pl.pallas_call(
        kernel,
        grid_spec=pltpu.PrefetchScalarGridSpec(
            num_scalar_prefetch=1,
            grid=grid,
            in_specs=in_specs,
            out_specs=out_specs,
            scratch_shapes=scratch,
        ),
        out_shape=out_shape,
        compiler_params=params(),
        cost_estimate=pl.CostEstimate(
            flops=flops // COST_SCALE,
            bytes_accessed=nbytes // COST_SCALE,
            transcendentals=trans // COST_SCALE,
        ),
    )


def head_columns(h, heads):
    return tuple((kind * heads + h) * HEAD_DIM for kind in range(3))


def block_rows(place_ref, near_ref, far_ref, store):
    even = place_ref[0] == 0
    upper = place_ref[3]
    count, rows, _ = near_ref.shape
    for u in range(count):
        src = lax.bitwise_xor(upper, jnp.int32(u))
        for x in range(2):
            at = slice((2 * u + x) * rows, (2 * u + x + 1) * rows)
            same = even if x == 0 else jnp.logical_not(even)
            store(at, jnp.where(same, near_ref[src], far_ref[src]))


def natural(place_ref, pieces, targets):
    held_ref, from_x_ref, from_y_ref, diagonal_ref = pieces
    block_rows(place_ref, held_ref, from_x_ref, functools.partial(targets, 0))
    block_rows(place_ref, from_y_ref, diagonal_ref, functools.partial(targets, 1))


def pick_row(place_ref, tile, part, refs):
    keep_ref, came_ref, keep_core_ref, came_core_ref = refs
    same_y = tile // 2 == place_ref[2]
    same_core = tile % 2 == place_ref[1]
    return jnp.where(
        same_y,
        jnp.where(same_core, keep_ref[part], keep_core_ref[part]),
        jnp.where(same_core, came_ref[part], came_core_ref[part]),
    )


def project(place_ref, near_ref, far_ref, low, bias_ref, qkv_ref, w_ref, o_ref):
    cols = w_ref.shape[1]

    @pl.when(pl.program_id(0) == 0)
    def _():
        def store(at, value):
            w_ref[at] = value[:, :cols]
            o_ref[at] = value[:, cols:]

        block_rows(place_ref, near_ref, far_ref, store)

    qkv_ref[...] = (nn(low, w_ref[...]) + bias_ref[...]).astype(BF16)


def first_qkv_kernel(place_ref, *refs):
    rows = refs[:4]
    near_ref, far_ref, vec_ref, bias_ref, x_ref, dy_ref, a_ref, *outs = refs[4:]
    x = pick_row(place_ref, pl.program_id(0), 0, rows)
    x_ref[...] = x
    dy_ref[...] = pick_row(place_ref, pl.program_id(0), 1, rows)
    normed, _ = standardize(x.astype(F32))
    low = (normed * vec_ref[0:1] + vec_ref[1:2]).astype(BF16)
    a_ref[...] = low
    project(place_ref, near_ref, far_ref, low, bias_ref, *outs)


def second_qkv_kernel(place_ref, a_ref, near_ref, far_ref, bias_ref, *outs):
    project(place_ref, near_ref, far_ref, a_ref[...], bias_ref, *outs)


def column(row):
    return jnp.broadcast_to(row, (128, row.shape[1])).T[:, :1]


def attend_kernel(last, qkv_q_ref, qkv_ref, seg_tile_ref, seg_row_ref, *refs):
    if last:
        ctx_in_ref, o0_ref, o1_ref, ctx_ref, lse_ref, out_ref = refs
    else:
        ctx_ref, lse_ref = refs
    cols = ctx_ref.shape[1]
    heads = cols // HEAD_DIM
    same = column(seg_tile_ref[...]) == seg_row_ref[...]
    lane = lax.broadcasted_iota(jnp.int32, (TILE, 128), 1)
    totals = jnp.zeros((TILE, 128), F32)
    for h in range(heads):
        lo = h * HEAD_DIM
        at_q, at_k, at_v = head_columns(h, heads)
        q = qkv_q_ref[:, at_q : at_q + HEAD_DIM]
        k = qkv_ref[:, at_k : at_k + HEAD_DIM]
        v = qkv_ref[:, at_v : at_v + HEAD_DIM]
        s = jnp.where(same, nt(q, k) * SCALE, MASKED_SCORE)
        top = jnp.max(s, axis=-1, keepdims=True)
        e = jnp.exp(s - top)
        total = jnp.sum(e, axis=-1, keepdims=True)
        o = nn(e.astype(BF16), v) / total
        ctx_ref[:, lo : lo + HEAD_DIM] = o.astype(BF16)
        totals = jnp.where(lane == h, top + jnp.log(total), totals)
    lse_ref[...] = totals.T[: lse_ref.shape[0]]
    if last:
        out_ref[...] = (nt(ctx_in_ref[...], o0_ref[...]) + nt(ctx_ref[...], o1_ref[...])).astype(BF16)


def sort_grad(place_ref, mine, others, own_ref, send_ref, keep_ref, at):
    even = place_ref[0] == 0
    first = place_ref[1] == 0
    rows = own_ref.shape[1]
    for u in range(own_ref.shape[0]):
        lo = slice(2 * u * rows, (2 * u + 1) * rows)
        hi = slice((2 * u + 1) * rows, (2 * u + 2) * rows)
        own_ref[u, :, at] = jnp.where(even, mine[lo], mine[hi])
        to_x = jnp.where(even, mine[hi], mine[lo])
        to_y = jnp.where(even, others[lo], others[hi])
        send_ref[0, u, :, at] = jnp.where(first, to_y, to_x)
        keep_ref[u, :, at] = jnp.where(first, to_x, to_y)
        send_ref[1, u, :, at] = jnp.where(even, others[hi], others[lo])


def add_grad(total_ref, j, left, right):
    part = tn(left, right)

    @pl.when(pl.program_id(0) == 0)
    def _():
        total_ref[j] = part

    @pl.when(pl.program_id(0) > 0)
    def _():
        total_ref[j] += part


def up_kernel(place_ref, x_ref, p0_ref, p1_ref, dy_ref, vec_ref, bu_ref, *refs):
    pieces = refs[:4]
    (a_ref, normed_ref, inv_ref, z_ref, slope_ref, own_ref, u0_ref, u1_ref,
     g_own_ref, g_send_ref, g_keep_ref, total_ref) = refs[4:]
    tile = pl.program_id(0)

    @pl.when(tile == 0)
    def _():
        def store(j, at, value):
            (u0_ref, u1_ref)[j][at] = value

        natural(place_ref, pieces, store)

    h = x_ref[...].astype(F32) + (p0_ref[...].astype(F32) + p1_ref[...].astype(F32)) + vec_ref[4:5]

    @pl.when(tile % 2 == place_ref[1])
    def _():
        own_ref[...] = h

    normed, inv = standardize(h)
    normed_ref[...] = normed.astype(BF16)
    inv_ref[...] = inv
    a = (normed * vec_ref[2:3] + vec_ref[3:4]).astype(BF16)
    a_ref[...] = a
    dy = dy_ref[...]
    for j, u_ref in enumerate((u0_ref, u1_ref)):
        u = nn(a, u_ref[...]) + bu_ref[j : j + 1]
        cdf = 0.5 + 0.5 * lax.erf(u * 0.7071067811865476)
        z = (u * cdf).astype(BF16)
        z_ref[j] = z
        slope_ref[j] = (cdf + u * (0.3989422804014327 * jnp.exp(-0.5 * u * u))).astype(BF16)
        add_grad(total_ref, j, dy, z)

    @pl.when(tile == pl.num_programs(0) - 1)
    def _():
        sort_grad(place_ref, total_ref[0].astype(BF16), total_ref[1].astype(BF16),
                  g_own_ref, g_send_ref, g_keep_ref, slice(None))


def down_kernel(place_ref, dy_ref, z_ref, slope_ref, u0_ref, u1_ref, *refs):
    pieces = refs[:4]
    du_ref, keep_ref, send_ref, da_ref, gbu_ref, d0_ref, d1_ref = refs[4:]
    tile = pl.program_id(0)

    @pl.when(tile == 0)
    def _():
        gbu_ref[...] = jnp.zeros_like(gbu_ref)

        def store(j, at, value):
            (d0_ref, d1_ref)[j][at] = value

        natural(place_ref, pieces, store)

    dy = dy_ref[...]
    down = jnp.zeros(da_ref.shape, F32)
    da = jnp.zeros(da_ref.shape, F32)
    for j, (u_ref, d_ref) in enumerate(((u0_ref, d0_ref), (u1_ref, d1_ref))):
        du = (nn(dy, d_ref[...]) * slope_ref[j].astype(F32)).astype(BF16)
        du_ref[j] = du
        gbu_ref[j : j + 1] += jnp.sum(du.astype(F32), axis=0, keepdims=True)
        down += nt(z_ref[j], d_ref[...])
        da += nt(du, u_ref[...])
    da_ref[...] = da.astype(BF16)
    down = down.astype(BF16)
    mine = tile % 2 == place_ref[1]

    @pl.when(mine)
    def _():
        keep_ref[...] = down

    @pl.when(jnp.logical_not(mine))
    def _():
        send_ref[...] = down


def grad_kernel(place_ref, left_ref, right_ref, own_ref, send_ref, keep_ref, turned_ref):
    @pl.when(pl.program_id(0) == 0)
    def _():
        turned_ref[...] = left_ref[...].T

    turned = turned_ref[...]
    mine = nn(turned, right_ref[0]).astype(BF16)
    others = nn(turned, right_ref[1]).astype(BF16)
    sort_grad(place_ref, mine, others, own_ref, send_ref, keep_ref, slice(None))


def two_grads_kernel(place_ref, left_ref, dh_ref, dqkv0_ref, dqkv1_ref, ctx0_ref, ctx1_ref,
                     own_ref, send_ref, keep_ref):
    many = dqkv0_ref.shape[1]
    turned = left_ref[...].T
    mine = nn(turned, dqkv0_ref[...]).astype(BF16)
    others = nn(turned, dqkv1_ref[...]).astype(BF16)
    sort_grad(place_ref, mine, others, own_ref, send_ref, keep_ref, slice(0, many))
    turned = dh_ref[...].T
    mine = nn(turned, ctx0_ref[...]).astype(BF16)
    others = nn(turned, ctx1_ref[...]).astype(BF16)
    sort_grad(place_ref, mine, others, own_ref, send_ref, keep_ref, slice(many, None))


def mid_kernel(normed_ref, inv_ref, dy_ref, da0_ref, da1_ref, ctx0_ref, ctx1_ref, vec_ref,
               o0_ref, o1_ref, dh_ref, dctx_ref, delta_ref, sums_ref):
    @pl.when(pl.program_id(0) == 0)
    def _():
        sums_ref[...] = jnp.zeros_like(sums_ref)

    normed = normed_ref[...].astype(F32)
    da = da0_ref[...].astype(F32) + da1_ref[...].astype(F32)
    dy = dy_ref[...].astype(F32)
    dh = dy + norm_back(da, normed, inv_ref[...], vec_ref[2:3])
    low = dh.astype(BF16)
    dh_ref[...] = low
    sums_ref[0:1] += jnp.sum(da * normed, axis=0, keepdims=True)
    sums_ref[1:2] += jnp.sum(da, axis=0, keepdims=True)
    sums_ref[2:3] += jnp.sum(dh, axis=0, keepdims=True)
    sums_ref[3:4] += jnp.sum(dy, axis=0, keepdims=True)
    cols = ctx0_ref.shape[1]
    head = lax.broadcasted_iota(jnp.int32, (8, cols), 0)
    owner = lax.broadcasted_iota(jnp.int32, (8, cols), 1) // HEAD_DIM
    member = jnp.where(head == owner, 1.0, 0.0).astype(BF16)
    for j, (o_ref, ctx_ref) in enumerate(((o0_ref, ctx0_ref), (o1_ref, ctx1_ref))):
        dctx = nn(low, o_ref[...]).astype(BF16)
        dctx_ref[j] = dctx
        prod = dctx.astype(F32) * ctx_ref[...].astype(F32)
        high = prod.astype(BF16)
        rest = (prod - high.astype(F32)).astype(BF16)
        delta_ref[j] = nt(member, high) + nt(member, rest)


def attend_back_kernel(heads, qkv_ref, dctx_ref, lse_ref, delta_ref, seg_row_ref,
                       dqkv_ref, sums_ref, dk_ref, dv_ref):
    length = qkv_ref.shape[0]
    seg_col = column(seg_row_ref[...])
    for h in range(heads):
        lo = h * HEAD_DIM
        at_q, at_k, at_v = head_columns(h, heads)
        k = qkv_ref[:, at_k : at_k + HEAD_DIM]
        v = qkv_ref[:, at_v : at_v + HEAD_DIM]
        for t in range(length // TILE):
            rows = slice(t * TILE, (t + 1) * TILE)
            q = qkv_ref[rows, at_q : at_q + HEAD_DIM]
            dc = dctx_ref[rows, lo : lo + HEAD_DIM]
            same = seg_col == seg_row_ref[:, rows]
            s = jnp.where(same, nt(k, q) * SCALE, MASKED_SCORE)
            p = jnp.exp(s - lse_ref[h : h + 1, rows])
            ds = (p * (nt(v, dc) - delta_ref[h : h + 1, rows])).astype(BF16)
            dv = nn(p.astype(BF16), dc)
            dk = nn(ds, q)
            if t == 0:
                dv_ref[...] = dv
                dk_ref[...] = dk
            else:
                dv_ref[...] += dv
                dk_ref[...] += dk
            dqkv_ref[rows, at_q : at_q + HEAD_DIM] = (tn(ds, k) * SCALE).astype(BF16)
        dqkv_ref[:, at_k : at_k + HEAD_DIM] = (dk_ref[...] * SCALE).astype(BF16)
        dqkv_ref[:, at_v : at_v + HEAD_DIM] = dv_ref[...].astype(BF16)
    sums_ref[...] = jnp.sum(dqkv_ref[...].astype(F32), axis=0, keepdims=True)


def input_grad_kernel(place_ref, x_ref, g0_ref, g1_ref, w0_ref, w1_ref, keep_ref, send_ref,
                      sums_ref):
    tile = pl.program_id(0)

    @pl.when(tile == 0)
    def _():
        sums_ref[...] = jnp.zeros_like(sums_ref)

    out = nt(g0_ref[...], w0_ref[...]) + nt(g1_ref[...], w1_ref[...])
    normed, _ = standardize(x_ref[...].astype(F32))
    sums_ref[0:1] += jnp.sum(out * normed, axis=0, keepdims=True)
    sums_ref[1:2] += jnp.sum(out, axis=0, keepdims=True)
    out = out.astype(BF16)
    mine = tile % 2 == place_ref[1]

    @pl.when(mine)
    def _():
        keep_ref[...] = out

    @pl.when(jnp.logical_not(mine))
    def _():
        send_ref[...] = out


def final_kernel(place_ref, x_ref, da0_ref, da1_ref, dh_ref, own_ref, keep_ref, came_ref, vec_ref,
                 dx_ref, out_ref, send_ref):
    normed, inv = standardize(x_ref[...].astype(F32))
    da = da0_ref[...].astype(F32) + da1_ref[...].astype(F32)
    dx = dh_ref[...].astype(F32) + norm_back(da, normed, inv, vec_ref[0:1])
    dx_ref[...] = dx
    out = own_ref[...] + (keep_ref[...].astype(F32) + came_ref[...].astype(F32)) + vec_ref[5:6]
    out = out.astype(BF16)
    out_ref[...] = out

    @pl.when(pl.program_id(0) != place_ref[2])
    def _():
        send_ref[0] = dx.astype(BF16)
        send_ref[1] = out


def local(
    tokens,
    segment_ids,
    cotangent,
    attn_w,
    attn_m,
    attn_v,
    mlp_w,
    mlp_m,
    mlp_v,
    vectors,
    vec_m,
    vec_v,
):
    wide = lax.axis_size("wide")
    narrow = lax.axis_size("narrow")
    widx = lax.axis_index("wide")
    nidx = lax.axis_index("narrow")
    y = nidx // 2
    c = nidx % 2
    other = (1 - y) * 2 + c
    xbit = widx % 2
    even = xbit == 0
    first_core = c == 0
    first_y = y == 0
    _, shard_len, width = tokens.shape
    length = segment_ids.shape[1]
    cols = attn_w.shape[2]
    rows = attn_w.shape[1]
    hidden = mlp_w.shape[2]
    heads = cols // HEAD_DIM
    bits = wide.bit_length() - 1
    upper = wide // 2
    steps = [(b, min(2, bits - b)) for b in range(1, bits, 2)]

    def swap(value, partner):
        pairs = [
            (w * narrow + n, (lambda t: t[0] * narrow + t[1])(partner(w, n)))
            for w in range(wide)
            for n in range(narrow)
        ]
        return lax.ppermute(value, AXES, pairs)

    def over_core(value):
        return swap(value, lambda w, n: (w, n ^ 1))

    def over_y(value):
        return swap(value, lambda w, n: (w, n ^ 2))

    def over_x(value):
        return swap(value, lambda w, n: (w ^ 1, n))

    def over_wide(value, mask):
        return swap(value, lambda w, n: (w ^ mask, n))

    def mixed_one(value):
        return swap(value, lambda w, n: (w ^ 1, n) if n % 2 == 0 else (w, n ^ 2))

    def mixed_two(value):
        return swap(value, lambda w, n: (w ^ 1, n) if n % 2 == 1 else (w, n ^ 2))

    def tie(value, *deps):
        return lax.optimization_barrier((value, *deps))[0]

    def pair(flag, first, second, axis):
        return jnp.stack(
            [jnp.where(flag, first, second), jnp.where(flag, second, first)], axis=axis
        )

    def add_low(keep, came):
        return (keep.astype(F32) + came.astype(F32)).astype(BF16)

    def total_of(own, came, last):
        return own.astype(F32) + came.astype(F32) + last.astype(F32)

    def choose(index, values):
        picked = values[0]
        for i in range(1, len(values)):
            picked = jnp.where(index == i, values[i], picked)
        return picked

    def gather_upper(shard):
        held = shard[None]
        for b, count in steps:
            came = [over_wide(held, k << b) for k in range(1, 1 << count)]
            held = jnp.concatenate([held, *came], axis=0)
        return held

    def scatter_upper(total):
        for b, count in reversed(steps):
            size = total.shape[0] >> count
            digit = (widx >> b) & ((1 << count) - 1)
            blocks = [total[i * size : (i + 1) * size] for i in range(1 << count)]
            came = []
            for k in range(1, 1 << count):
                send = choose(digit, [blocks[i ^ k] for i in range(1 << count)])
                came.append(over_wide(send.astype(BF16), k << b))
            total = choose(digit, blocks).astype(F32)
            for each in came:
                total = total + each.astype(F32)
        return total, came

    def both(vector, size):
        return jnp.stack(
            [
                lax.dynamic_slice_in_dim(vector, nidx * size, size),
                lax.dynamic_slice_in_dim(vector, other * size, size),
            ]
        )

    tiles = length // TILE
    tile_spec = pl.BlockSpec((TILE, width), lambda t, *_: (t, 0))
    up_spec = whole((width, hidden))
    qkv_cols = 3 * cols
    matmul = 2 * length * width
    row_shape = jax.ShapeDtypeStruct((length, width), BF16)
    zero = jnp.int32(0)
    place = jnp.stack([xbit, c, y, widx // 2, zero, zero, zero, zero]).astype(jnp.int32)

    def spread_over_plane(held):
        from_x = over_x(held)
        from_y = over_y(held)
        return from_x, from_y

    def turn(from_x, from_y):
        return jnp.where(first_core, from_x, from_y)

    attn_low = attn_w.astype(BF16)
    attn_shard = jnp.concatenate([attn_low[i] for i in range(4)], axis=-1)

    mlp_low = mlp_w.astype(BF16)
    a_held = gather_upper(attn_shard)

    def row_pair(first):
        return jnp.stack(
            [jnp.where(first, v[0], v[1]) for v in (tokens, cotangent)]
        )

    rows_send = row_pair(jnp.logical_not(first_y))
    rows_came = over_y(tie(rows_send, attn_shard))
    rows_keep = row_pair(first_y)
    rows_keep_core = over_core(rows_keep)

    a_held, rows_came = lax.optimization_barrier((a_held, rows_came))
    a_x, a_y = spread_over_plane(a_held)
    rows_came_core = over_core(rows_came)
    u_held = gather_upper(tie(mlp_low[0], a_held, rows_came_core, rows_keep_core))
    query_bias = both(vectors[6], cols)
    value_bias = both(vectors[7], cols)
    no_bias = jnp.zeros_like(query_bias)
    qkv_bias = jnp.concatenate([query_bias, no_bias, value_bias], axis=1)
    up_bias = both(vectors[8:].reshape(-1), hidden)

    a_turn = turn(*lax.optimization_barrier((a_x, a_y, rows_came_core, rows_keep_core, qkv_bias, up_bias))[:2])
    a_diagonal = mixed_two(a_turn)
    u_x, u_y = None, None
    d_first = mlp_low[1][None]

    seg_own = lax.dynamic_index_in_dim(segment_ids, y, 0, False)
    seg_row = seg_own[None, :]
    part_spec = whole((2, shard_len, width))
    piece_spec = whole((upper, rows, width))
    qkv_shape = jax.ShapeDtypeStruct((length, qkv_cols), BF16)
    qkv_spec = pl.BlockSpec((TILE, qkv_cols), lambda t, *_: (t, 0))
    block_shapes = [
        qkv_shape,
        jax.ShapeDtypeStruct((width, qkv_cols), BF16),
        jax.ShapeDtypeStruct((width, cols), BF16),
    ]
    block_specs = [qkv_spec, whole((width, qkv_cols)), whole((width, cols))]
    x_row, dy_row, normed_low, qkv_mine, w_mine, o_mine = placed(
        first_qkv_kernel,
        (tiles,),
        [part_spec] * 4 + [piece_spec] * 2 + [whole(vectors.shape), whole((1, qkv_cols))],
        [tile_spec] * 3 + block_specs,
        [row_shape] * 3 + block_shapes,
    )(tie(place, a_turn), rows_keep, rows_came, rows_keep_core, rows_came_core, a_held, a_x,
      vectors, qkv_bias[0:1])

    d_first_came = over_wide(tie(d_first, a_turn), 2)
    d_first, d_first_came = lax.optimization_barrier((d_first, d_first_came, qkv_mine))[:2]
    d_second = jnp.concatenate([d_first, d_first_came], axis=0)
    d_second_came = over_wide(d_second, 4)
    u_x, u_y = spread_over_plane(tie(u_held, qkv_mine, d_first_came))
    ctx_spec = pl.BlockSpec((TILE, cols), lambda t: (t, 0))
    lse_spec = pl.BlockSpec((8, TILE), lambda t: (0, t))
    ctx_shape = jax.ShapeDtypeStruct((length, cols), BF16)
    lse_shape = jax.ShapeDtypeStruct((8, length), F32)
    o_spec = whole((width, cols))

    def attend(qkv, segments, extra):
        last = bool(extra)
        in_specs = [
            qkv_spec,
            whole((length, qkv_cols)),
            pl.BlockSpec((1, TILE), lambda t: (0, t)),
            whole((1, length)),
        ]
        out_specs = [ctx_spec, lse_spec]
        out_shape = [ctx_shape, lse_shape]
        if last:
            in_specs += [ctx_spec, o_spec, o_spec]
            out_specs += [tile_spec]
            out_shape += [row_shape]
        return call(
            functools.partial(attend_kernel, last),
            (tiles,),
            in_specs,
            out_specs,
            out_shape,
            flops=4 * length * length * cols if last else 0,
        )(qkv, qkv, segments, segments, *extra)

    ctx_mine, lse_mine = attend(qkv_mine, tie(seg_row, d_second), ())
    a_y, a_diagonal = lax.optimization_barrier((a_y, a_diagonal, ctx_mine))[:2]
    qkv_others, w_others, o_others = placed(
        second_qkv_kernel,
        (tiles,),
        [tile_spec] + [piece_spec] * 2 + [whole((1, qkv_cols))],
        block_specs,
        block_shapes,
    )(place, normed_low, a_y, a_diagonal, qkv_bias[1:2])
    u_turn = turn(*lax.optimization_barrier((u_x, u_y, qkv_others))[:2])
    u_diagonal = mixed_two(u_turn)
    d_second, d_second_came = lax.optimization_barrier((d_second, d_second_came, qkv_others))[:2]
    d_second = jnp.concatenate([d_second, d_second_came], axis=0)

    def gather_rest(held):
        for b in range(3, bits):
            held = jnp.concatenate([held, over_wide(held, 1 << b)], axis=0)
        return held

    d_held = d_second if bits == 3 else gather_rest(d_second)
    ctx_others, lse_others, out_part = attend(
        qkv_others, tie(seg_row, u_turn, d_held), (ctx_mine, o_mine, o_others)
    )
    out_part, u_diagonal = lax.optimization_barrier((out_part, u_diagonal))
    out_came = over_core(out_part)
    d_x, d_y = spread_over_plane(tie(d_held, u_turn))
    d_diagonal = swap(tie(d_held, u_turn), lambda w, n: (w ^ 1, n ^ 2))

    pair_spec = pl.BlockSpec((2, TILE, hidden), lambda t, *_: (0, t, 0))
    pair_shape = jax.ShapeDtypeStruct((2, length, hidden), BF16)
    half_spec = pl.BlockSpec((None, TILE, width), lambda t, *_: (t // 2, 0, 0))
    up_shape = jax.ShapeDtypeStruct((width, hidden), BF16)

    def half_shape(dtype):
        return jax.ShapeDtypeStruct((2, shard_len, width), dtype)

    grad_specs = [piece_spec, whole((2, upper, rows, width)), piece_spec]
    grad_shapes = [
        jax.ShapeDtypeStruct((upper, rows, hidden), BF16),
        jax.ShapeDtypeStruct((2, upper, rows, hidden), BF16),
        jax.ShapeDtypeStruct((upper, rows, hidden), BF16),
    ]
    (second_low, second_normed, second_inv, activated, slope, hidden_own, u_mine, u_others,
     gd_own, gd_send, gd_keep) = placed(
        up_kernel,
        (tiles,),
        [tile_spec] * 4 + [whole(vectors.shape), whole((2, hidden))] + [piece_spec] * 4,
        [tile_spec, tile_spec, pl.BlockSpec((TILE, 1), lambda t, p: (t, 0)), pair_spec, pair_spec,
         half_spec, up_spec, up_spec] + grad_specs,
        [row_shape, row_shape, jax.ShapeDtypeStruct((length, 1), F32), pair_shape, pair_shape,
         half_shape(F32), up_shape, up_shape] + grad_shapes,
        scratch=[pltpu.VMEM((2, width, hidden), F32)],
        flops=2 * matmul * 2 * hidden,
        nbytes=20_000_000,
        trans=4 * length * hidden,
    )(place, x_row, out_part, out_came, dy_row, vectors, up_bias, u_held, u_x, u_y, u_diagonal)
    gd_came = mixed_two(gd_send)

    def weight_grad(where, left, right, block):
        spec = pl.BlockSpec((upper, rows, block), lambda i, p: (0, 0, i))
        return placed(
            grad_kernel,
            (hidden // block,),
            [whole((length, width)), pl.BlockSpec((2, length, block), lambda i, p: (0, 0, i))],
            [spec, pl.BlockSpec((2, upper, rows, block), lambda i, p: (0, 0, 0, i)), spec],
            grad_shapes,
            scratch=[pltpu.VMEM((width, length), BF16)],
            flops=matmul * 2 * hidden,
            nbytes=8_000_000,
        )(where, left, right)

    def attn_weight_grad(dqkv_first, dqkv_second):
        return placed(
            two_grads_kernel,
            (1,),
            [whole((length, width))] * 2 + [whole((length, qkv_cols))] * 2
            + [whole((length, cols))] * 2,
            grad_specs,
            grad_shapes,
        )(place, normed_low, resid_low, dqkv_first, dqkv_second, ctx_mine, ctx_others)

    grad_pre, down_keep, down_send, second_part, up_bias_sums = placed(
        down_kernel,
        (tiles,),
        [tile_spec, pair_spec, pair_spec, up_spec, up_spec] + [piece_spec] * 4,
        [pair_spec, half_spec, half_spec, tile_spec, whole((2, hidden))],
        [pair_shape, half_shape(BF16), half_shape(BF16), row_shape,
         jax.ShapeDtypeStruct((2, hidden), F32)],
        scratch=[pltpu.VMEM((width, hidden), BF16)] * 2,
        flops=3 * matmul * 2 * hidden,
        nbytes=20_000_000,
    )(tie(place, gd_send), dy_row, activated, slope, u_mine, u_others, d_held, d_x, d_y, d_diagonal)
    second_part, gd_came = lax.optimization_barrier((second_part, gd_came))

    down_came = over_core(down_send)
    second_came = over_core(second_part)
    gu_own, gu_send, gu_keep = weight_grad(
        tie(place, second_part), second_low, grad_pre, 256
    )
    gu_came = mixed_two(gu_send)

    delta_spec = pl.BlockSpec((2, 8, TILE), lambda t: (0, 0, t))
    resid_low, grad_ctx, delta, mid_sums = call(
        mid_kernel,
        (tiles,),
        [tile_spec, pl.BlockSpec((TILE, 1), lambda t: (t, 0))] + [tile_spec] * 3
        + [ctx_spec, ctx_spec, whole(vectors.shape), o_spec, o_spec],
        [tile_spec, pl.BlockSpec((2, TILE, cols), lambda t: (0, t, 0)), delta_spec,
         whole((8, width))],
        [row_shape,
         jax.ShapeDtypeStruct((2, length, cols), BF16),
         jax.ShapeDtypeStruct((2, 8, length), F32),
         jax.ShapeDtypeStruct((8, width), F32)],
        flops=matmul * 2 * cols,
        nbytes=10_000_000,
    )(second_normed, second_inv, dy_row, second_part, second_came, ctx_mine, ctx_others,
      tie(vectors, gu_send), o_mine, o_others)

    def attend_back(j, qkv, lse, segments):
        return call(
            functools.partial(attend_back_kernel, heads),
            (1,),
            [whole((length, qkv_cols)),
             pl.BlockSpec((None, length, cols), lambda i: (j, 0, 0)),
             whole((8, length)),
             pl.BlockSpec((None, 8, length), lambda i: (j, 0, 0)),
             whole((1, length))],
            [whole((length, qkv_cols)), whole((1, qkv_cols))],
            [jax.ShapeDtypeStruct((length, qkv_cols), BF16),
             jax.ShapeDtypeStruct((1, qkv_cols), F32)],
            scratch=[pltpu.VMEM((length, HEAD_DIM), F32), pltpu.VMEM((length, HEAD_DIM), F32)],
        )(qkv, grad_ctx, lse, delta, segments)

    dqkv_mine, sums_mine = attend_back(0, qkv_mine, lse_mine, tie(seg_row, down_came))
    gu_came = tie(gu_came, dqkv_mine)
    mlp_last_send = jnp.stack([add_low(gu_keep, gu_came[1]), add_low(gd_keep, gd_came[1])], axis=1)
    mlp_last = mixed_one(mlp_last_send)
    dqkv_others, sums_others = attend_back(1, qkv_others, lse_others, tie(seg_row, mlp_last_send))
    ga_own, ga_send, ga_keep = attn_weight_grad(dqkv_mine, dqkv_others)
    ga_came = mixed_two(ga_send)
    mlp_last = tie(mlp_last, ga_send)
    gu_sum = total_of(gu_own, gu_came[0], mlp_last[:, 0])
    gd_sum = total_of(gd_own, gd_came[0], mlp_last[:, 1])

    def halves(total, b):
        size = total.shape[0] // 2
        total = total.reshape(size, 2, *total.shape[1:])
        high = ((widx >> b) & 1) == 1
        return (
            jnp.where(high, total[:, 1], total[:, 0]),
            jnp.where(high, total[:, 0], total[:, 1]),
        )

    gu_keep, gu_send = halves(gu_sum, 1)
    gd_keep, gd_send = halves(gd_sum, 1)
    mlp_came = over_wide(jnp.stack([gu_send, gd_send], axis=1).astype(BF16), 2)

    half_out = pl.BlockSpec((None, TILE, width), lambda t, p: (t // 2, 0, 0))
    one_keep, one_send, one_sums = placed(
        input_grad_kernel,
        (tiles,),
        [tile_spec] + [pl.BlockSpec((TILE, qkv_cols), lambda t, p: (t, 0))] * 2
        + [whole((width, qkv_cols))] * 2,
        [half_out] * 2 + [whole((8, width))],
        [half_shape(BF16)] * 2 + [jax.ShapeDtypeStruct((8, width), F32)],
        flops=matmul * 2 * qkv_cols,
        nbytes=8_000_000,
    )(tie(place, gu_sum, gd_sum), x_row, dqkv_mine, dqkv_others, w_mine, w_others)
    one_came = over_core(one_send)

    def spread(mine, others, size):
        empty = jnp.zeros((size * narrow,), F32)
        empty = lax.dynamic_update_slice_in_dim(empty, mine, nidx * size, 0)
        return lax.dynamic_update_slice_in_dim(empty, others, other * size, 0)

    vec_part = jnp.concatenate(
        [
            one_sums[:2],
            jnp.where(first_core, mid_sums[:4], 0.0),
            spread(sums_mine[0, :cols], sums_others[0, :cols], cols)[None],
            spread(sums_mine[0, 2 * cols :], sums_others[0, 2 * cols :], cols)[None],
            spread(up_bias_sums[0], up_bias_sums[1], hidden).reshape(-1, width),
        ],
        axis=0,
    )

    vec_came = mixed_two(vec_part)

    own_block = pl.BlockSpec((TILE, width), lambda t, p: (2 * t + p[1], 0))
    half_in = pl.BlockSpec((None, TILE, width), lambda t, p: (t, 0, 0))
    grad_own, block_own, last_send = placed(
        final_kernel,
        (2,),
        [own_block, half_in, half_in, own_block] + [half_in] * 3 + [whole(vectors.shape)],
        [half_in, half_in, whole((2, shard_len, width))],
        [half_shape(F32), half_shape(BF16), half_shape(BF16)],
        nbytes=9_000_000,
    )(tie(place, vec_part), x_row, one_keep, one_came, resid_low, hidden_own, down_keep,
      down_came, vectors)

    ga_came, vec_came, last_send = lax.optimization_barrier((ga_came, vec_came, last_send))
    ga_send = add_low(ga_keep, ga_came[1])
    ga_last = mixed_one(ga_send)
    vec_grad = tie(vec_part + vec_came, ga_send)
    vec_grad = vec_grad + mixed_one(vec_grad)
    last_came = over_y(tie(last_send, ga_send))

    mlp_came = tie(mlp_came, ga_send)
    mlp_parts = [
        keep + mlp_came[:, i].astype(F32) for i, keep in enumerate((gu_keep, gd_keep))
    ]
    mlp_sends = []
    for b in range(2, bits):
        split = [halves(part, b) for part in mlp_parts]
        mlp_sends = [send.astype(BF16) for _, send in split]
        mlp_came = over_wide(jnp.stack(mlp_sends, axis=1), 1 << b)
        mlp_parts = [(keep, mlp_came[:, i]) for i, (keep, _) in enumerate(split)]
        if b < bits - 1:
            mlp_parts = [keep + came.astype(F32) for keep, came in mlp_parts]

    vec_here = vec_grad
    for b in range(1, bits - 1):
        vec_here = vec_here + over_wide(vec_here, 1 << b)
    ga_last = tie(ga_last, vec_grad, *mlp_sends)
    ga_sum = total_of(ga_own, ga_came[0], ga_last)
    ga_sum, vec_here = lax.optimization_barrier((ga_sum, vec_here))
    ga_sum, came = scatter_upper(ga_sum)
    vec_here = tie(vec_here, came[0])
    vec_grad = vec_here + over_wide(vec_here, 1 << (bits - 1))
    vec_grad = vec_grad + over_core(vec_grad)
    mlp_total = jnp.concatenate(
        [keep + tie(last, came[-1]).astype(F32) for keep, last in mlp_parts], axis=0
    )
    attn_total = ga_sum[0]

    def home(own, came):
        return lax.dynamic_update_slice(own, came[None].astype(own.dtype), (1 - y, 0, 0))

    block_out = home(block_own, last_came[1])
    block_input_gradient = home(grad_own, last_came[0])

    attn_grad = jnp.stack([attn_total[:, i * cols : (i + 1) * cols] for i in range(4)])
    mlp_grad = mlp_total
    attn_new, attn_m_new, attn_v_new = adamw_update(
        attn_w, attn_m, attn_v, attn_grad, RATE_MATRIX, DECAY_MATRIX
    )
    mlp_new, mlp_m_new, mlp_v_new = adamw_update(
        mlp_w, mlp_m, mlp_v, mlp_grad, RATE_MATRIX, DECAY_MATRIX
    )
    vec_new, vec_m_new, vec_v_new = adamw_update(vectors, vec_m, vec_v, vec_grad, RATE_VECTOR, 0.0)
    return (
        block_out,
        block_input_gradient,
        attn_grad,
        attn_new,
        attn_m_new,
        attn_v_new,
        mlp_grad,
        mlp_new,
        mlp_m_new,
        mlp_v_new,
        vec_grad,
        vec_new,
        vec_m_new,
        vec_v_new,
    )


def solution(mesh):
    matrix = P(None, "wide", "narrow")
    rows = P("wide", "narrow", None)
    in_specs = (rows, P("wide", None), rows) + (matrix,) * 6 + (P(),) * 3
    out_specs = (rows, rows) + (matrix,) * 8 + (P(),) * 4
    return jax.shard_map(local, mesh=mesh, in_specs=in_specs, out_specs=out_specs, check_vma=False)
```

```python
import functools

import jax
import jax.numpy as jnp
from jax import lax
from jax.experimental import pallas as pl
from jax.experimental.pallas import tpu as pltpu
from jax.sharding import PartitionSpec as P

HEAD_DIM = 64
STEP = 10


EPS_NORM = 1e-06
MASKED_SCORE = -1e30
BETA_ONE = 0.5
BETA_TWO = 0.5
EPS_ADAM = 1e-08
RATE_MATRIX = 0.04
RATE_VECTOR = 0.3
DECAY_MATRIX = 0.05
SCALE = HEAD_DIM ** (-0.5)
TILE = 256
F32 = jnp.float32
BF16 = jnp.bfloat16
AXES = ("wide", "narrow")
COST_SCALE = 1
VMEM_LIMIT = 48 * 1024 * 1024


def adamw_update(weight, first_mom, second, gradient, step_rate, decay_rate):
    first_new = BETA_ONE * first_mom + (1.0 - BETA_ONE) * gradient
    second_new = BETA_TWO * second + (1.0 - BETA_TWO) * gradient * gradient
    corrected = (
        first_new
        / (1.0 - BETA_ONE**STEP)
        / (jnp.sqrt(second_new / (1.0 - BETA_TWO**STEP)) + EPS_ADAM)
    )
    return (weight - step_rate * (corrected + decay_rate * weight), first_new, second_new)


def nn(a, b):
    return lax.dot_general(a, b, (((1,), (0,)), ((), ())), preferred_element_type=F32)


def nt(a, b):
    return lax.dot_general(a, b, (((1,), (1,)), ((), ())), preferred_element_type=F32)


def tn(a, b):
    return lax.dot_general(a, b, (((0,), (0,)), ((), ())), preferred_element_type=F32)


def standardize(v):
    centred = v - jnp.mean(v, axis=-1, keepdims=True)
    inv = lax.rsqrt(jnp.mean(centred * centred, axis=-1, keepdims=True) + EPS_NORM)
    return centred * inv, inv


def norm_back(grad_out, normed, inv, gain):
    scaled = grad_out * gain
    return inv * (
        scaled
        - jnp.mean(scaled, axis=-1, keepdims=True)
        - normed * jnp.mean(scaled * normed, axis=-1, keepdims=True)
    )


def whole(shape):
    return pl.BlockSpec(shape, lambda *_: (0,) * len(shape))


def params(cost=None):
    return pltpu.CompilerParams(
        dimension_semantics=("arbitrary",), vmem_limit_bytes=VMEM_LIMIT
    )


def call(kernel, grid, in_specs, out_specs, out_shape, scratch=(), flops=0, nbytes=0, trans=0):
    return pl.pallas_call(
        kernel,
        grid=grid,
        in_specs=in_specs,
        out_specs=out_specs,
        out_shape=out_shape,
        scratch_shapes=scratch,
        compiler_params=params(),
        cost_estimate=pl.CostEstimate(
            flops=flops // COST_SCALE,
            bytes_accessed=nbytes // COST_SCALE,
            transcendentals=trans // COST_SCALE,
        ),
    )


def placed(kernel, grid, in_specs, out_specs, out_shape, scratch=(), flops=0, nbytes=0, trans=0):
    return pl.pallas_call(
        kernel,
        grid_spec=pltpu.PrefetchScalarGridSpec(
            num_scalar_prefetch=1,
            grid=grid,
            in_specs=in_specs,
            out_specs=out_specs,
            scratch_shapes=scratch,
        ),
        out_shape=out_shape,
        compiler_params=params(),
        cost_estimate=pl.CostEstimate(
            flops=flops // COST_SCALE,
            bytes_accessed=nbytes // COST_SCALE,
            transcendentals=trans // COST_SCALE,
        ),
    )


def head_columns(h, heads):
    return tuple((kind * heads + h) * HEAD_DIM for kind in range(3))


def block_rows(place_ref, near_ref, far_ref, store):
    even = place_ref[0] == 0
    upper = place_ref[3]
    count, rows, _ = near_ref.shape
    for u in range(count):
        src = lax.bitwise_xor(upper, jnp.int32(u))
        for x in range(2):
            at = slice((2 * u + x) * rows, (2 * u + x + 1) * rows)
            same = even if x == 0 else jnp.logical_not(even)
            store(at, jnp.where(same, near_ref[src], far_ref[src]))


def natural(place_ref, pieces, targets):
    held_ref, from_x_ref, from_y_ref, diagonal_ref = pieces
    block_rows(place_ref, held_ref, from_x_ref, functools.partial(targets, 0))
    block_rows(place_ref, from_y_ref, diagonal_ref, functools.partial(targets, 1))


def pick_row(place_ref, tile, part, refs):
    keep_ref, came_ref, keep_core_ref, came_core_ref = refs
    same_y = tile // 2 == place_ref[2]
    same_core = tile % 2 == place_ref[1]
    return jnp.where(
        same_y,
        jnp.where(same_core, keep_ref[part], keep_core_ref[part]),
        jnp.where(same_core, came_ref[part], came_core_ref[part]),
    )


def project(place_ref, near_ref, far_ref, low, bias_ref, qkv_ref, w_ref, o_ref):
    cols = w_ref.shape[1]

    @pl.when(pl.program_id(0) == 0)
    def _():
        def store(at, value):
            w_ref[at] = value[:, :cols]
            o_ref[at] = value[:, cols:]

        block_rows(place_ref, near_ref, far_ref, store)

    qkv_ref[...] = (nn(low, w_ref[...]) + bias_ref[...]).astype(BF16)


def first_qkv_kernel(place_ref, *refs):
    rows = refs[:4]
    near_ref, far_ref, vec_ref, bias_ref, x_ref, dy_ref, a_ref, *outs = refs[4:]
    x = pick_row(place_ref, pl.program_id(0), 0, rows)
    x_ref[...] = x
    dy_ref[...] = pick_row(place_ref, pl.program_id(0), 1, rows)
    normed, _ = standardize(x.astype(F32))
    low = (normed * vec_ref[0:1] + vec_ref[1:2]).astype(BF16)
    a_ref[...] = low
    project(place_ref, near_ref, far_ref, low, bias_ref, *outs)


def second_qkv_kernel(place_ref, a_ref, near_ref, far_ref, bias_ref, *outs):
    project(place_ref, near_ref, far_ref, a_ref[...], bias_ref, *outs)


def column(row):
    return jnp.broadcast_to(row, (128, row.shape[1])).T[:, :1]


def attend_kernel(last, qkv_q_ref, qkv_ref, seg_tile_ref, seg_row_ref, *refs):
    if last:
        ctx_in_ref, o0_ref, o1_ref, ctx_ref, lse_ref, out_ref = refs
    else:
        ctx_ref, lse_ref = refs
    cols = ctx_ref.shape[1]
    heads = cols // HEAD_DIM
    same = column(seg_tile_ref[...]) == seg_row_ref[...]
    lane = lax.broadcasted_iota(jnp.int32, (TILE, 128), 1)
    totals = jnp.zeros((TILE, 128), F32)
    for h in range(heads):
        lo = h * HEAD_DIM
        at_q, at_k, at_v = head_columns(h, heads)
        q = qkv_q_ref[:, at_q : at_q + HEAD_DIM]
        k = qkv_ref[:, at_k : at_k + HEAD_DIM]
        v = qkv_ref[:, at_v : at_v + HEAD_DIM]
        s = jnp.where(same, nt(q, k) * SCALE, MASKED_SCORE)
        top = jnp.max(s, axis=-1, keepdims=True)
        e = jnp.exp(s - top)
        total = jnp.sum(e, axis=-1, keepdims=True)
        o = nn(e.astype(BF16), v) / total
        ctx_ref[:, lo : lo + HEAD_DIM] = o.astype(BF16)
        totals = jnp.where(lane == h, top + jnp.log(total), totals)
    lse_ref[...] = totals.T[: lse_ref.shape[0]]
    if last:
        out_ref[...] = (nt(ctx_in_ref[...], o0_ref[...]) + nt(ctx_ref[...], o1_ref[...])).astype(BF16)


def sort_grad(place_ref, mine, others, own_ref, send_ref, keep_ref, at):
    even = place_ref[0] == 0
    first = place_ref[1] == 0
    rows = own_ref.shape[1]
    for u in range(own_ref.shape[0]):
        lo = slice(2 * u * rows, (2 * u + 1) * rows)
        hi = slice((2 * u + 1) * rows, (2 * u + 2) * rows)
        own_ref[u, :, at] = jnp.where(even, mine[lo], mine[hi])
        to_x = jnp.where(even, mine[hi], mine[lo])
        to_y = jnp.where(even, others[lo], others[hi])
        send_ref[0, u, :, at] = jnp.where(first, to_y, to_x)
        keep_ref[u, :, at] = jnp.where(first, to_x, to_y)
        send_ref[1, u, :, at] = jnp.where(even, others[hi], others[lo])


def add_grad(total_ref, j, left, right):
    part = tn(left, right)

    @pl.when(pl.program_id(0) == 0)
    def _():
        total_ref[j] = part

    @pl.when(pl.program_id(0) > 0)
    def _():
        total_ref[j] += part


def up_kernel(place_ref, x_ref, p0_ref, p1_ref, dy_ref, vec_ref, bu_ref, *refs):
    pieces = refs[:4]
    (a_ref, h_ref, z_ref, slope_ref,
     g_own_ref, g_send_ref, g_keep_ref, total_ref, u0_ref, u1_ref) = refs[4:]
    tile = pl.program_id(0)

    @pl.when(tile == 0)
    def _():
        def store(j, at, value):
            (u0_ref, u1_ref)[j][at] = value

        natural(place_ref, pieces, store)

    h = x_ref[...].astype(F32) + (p0_ref[...].astype(F32) + p1_ref[...].astype(F32)) + vec_ref[4:5]

    h_ref[...] = h.astype(BF16)
    normed, _ = standardize(h)
    a = (normed * vec_ref[2:3] + vec_ref[3:4]).astype(BF16)
    a_ref[...] = a
    dy = dy_ref[...]
    for j, u_ref in enumerate((u0_ref, u1_ref)):
        u = nn(a, u_ref[...]) + bu_ref[j : j + 1]
        cdf = 0.5 + 0.5 * lax.erf(u * 0.7071067811865476)
        z = (u * cdf).astype(BF16)
        z_ref[j] = z
        slope_ref[j] = (cdf + u * (0.3989422804014327 * jnp.exp(-0.5 * u * u))).astype(BF16)
        add_grad(total_ref, j, dy, z)

    @pl.when(tile == pl.num_programs(0) - 1)
    def _():
        sort_grad(place_ref, total_ref[0].astype(BF16), total_ref[1].astype(BF16),
                  g_own_ref, g_send_ref, g_keep_ref, slice(None))


def down_kernel(place_ref, dy_ref, z_ref, slope_ref, *refs):
    up_pieces = refs[:4]
    pieces = refs[4:8]
    du_ref, keep_ref, send_ref, da_ref, gbu_ref, d0_ref, d1_ref, u0_ref, u1_ref = refs[8:]
    tile = pl.program_id(0)

    @pl.when(tile == 0)
    def _():
        gbu_ref[...] = jnp.zeros_like(gbu_ref)

        def store_up(j, at, value):
            (u0_ref, u1_ref)[j][at] = value

        def store(j, at, value):
            (d0_ref, d1_ref)[j][at] = value

        natural(place_ref, up_pieces, store_up)
        natural(place_ref, pieces, store)

    dy = dy_ref[...]
    down = jnp.zeros(da_ref.shape, F32)
    da = jnp.zeros(da_ref.shape, F32)
    for j, (u_ref, d_ref) in enumerate(((u0_ref, d0_ref), (u1_ref, d1_ref))):
        du = (nn(dy, d_ref[...]) * slope_ref[j].astype(F32)).astype(BF16)
        du_ref[j] = du
        gbu_ref[j : j + 1] += jnp.sum(du.astype(F32), axis=0, keepdims=True)
        down += nt(z_ref[j], d_ref[...])
        da += nt(du, u_ref[...])
    da_ref[...] = da.astype(BF16)
    down = down.astype(BF16)
    mine = tile % 2 == place_ref[1]

    @pl.when(mine)
    def _():
        keep_ref[...] = down

    @pl.when(jnp.logical_not(mine))
    def _():
        send_ref[...] = down


def grad_kernel(place_ref, left_ref, right_ref, own_ref, send_ref, keep_ref, turned_ref):
    @pl.when(pl.program_id(0) == 0)
    def _():
        turned_ref[...] = left_ref[...].T

    turned = turned_ref[...]
    mine = nn(turned, right_ref[0]).astype(BF16)
    others = nn(turned, right_ref[1]).astype(BF16)
    sort_grad(place_ref, mine, others, own_ref, send_ref, keep_ref, slice(None))


def two_grads_kernel(place_ref, left_ref, dh_ref, dqkv0_ref, dqkv1_ref, ctx0_ref, ctx1_ref,
                     own_ref, send_ref, keep_ref):
    many = dqkv0_ref.shape[1]
    turned = left_ref[...].T
    mine = nn(turned, dqkv0_ref[...]).astype(BF16)
    others = nn(turned, dqkv1_ref[...]).astype(BF16)
    sort_grad(place_ref, mine, others, own_ref, send_ref, keep_ref, slice(0, many))
    turned = dh_ref[...].T
    mine = nn(turned, ctx0_ref[...]).astype(BF16)
    others = nn(turned, ctx1_ref[...]).astype(BF16)
    sort_grad(place_ref, mine, others, own_ref, send_ref, keep_ref, slice(many, None))


def mid_kernel(place_ref, h_ref, dy_ref, da0_ref, da1_ref, ctx0_ref, ctx1_ref, keep_ref, came_ref,
               vec_ref, o0_ref, o1_ref, dh_ref, dctx_ref, delta_ref, sums_ref, out_ref, send_ref):
    tile = pl.program_id(0)

    @pl.when(tile % 2 == place_ref[1])
    def _():
        out = h_ref[...].astype(F32) + (keep_ref[...].astype(F32) + came_ref[...].astype(F32))
        out = (out + vec_ref[5:6]).astype(BF16)
        out_ref[...] = out

        @pl.when(tile // 2 != place_ref[2])
        def _():
            send_ref[...] = out

    @pl.when(pl.program_id(0) == 0)
    def _():
        sums_ref[...] = jnp.zeros_like(sums_ref)

    normed, inv = standardize(h_ref[...].astype(F32))
    da = da0_ref[...].astype(F32) + da1_ref[...].astype(F32)
    dy = dy_ref[...].astype(F32)
    dh = dy + norm_back(da, normed, inv, vec_ref[2:3])
    low = dh.astype(BF16)
    dh_ref[...] = low
    sums_ref[0:1] += jnp.sum(da * normed, axis=0, keepdims=True)
    sums_ref[1:2] += jnp.sum(da, axis=0, keepdims=True)
    sums_ref[2:3] += jnp.sum(dh, axis=0, keepdims=True)
    sums_ref[3:4] += jnp.sum(dy, axis=0, keepdims=True)
    cols = ctx0_ref.shape[1]
    head = lax.broadcasted_iota(jnp.int32, (8, cols), 0)
    owner = lax.broadcasted_iota(jnp.int32, (8, cols), 1) // HEAD_DIM
    member = jnp.where(head == owner, 1.0, 0.0).astype(BF16)
    for j, (o_ref, ctx_ref) in enumerate(((o0_ref, ctx0_ref), (o1_ref, ctx1_ref))):
        dctx = nn(low, o_ref[...]).astype(BF16)
        dctx_ref[j] = dctx
        prod = dctx.astype(F32) * ctx_ref[...].astype(F32)
        high = prod.astype(BF16)
        rest = (prod - high.astype(F32)).astype(BF16)
        delta_ref[j] = nt(member, high) + nt(member, rest)


def attend_back_kernel(heads, qkv_ref, dctx_ref, lse_ref, delta_ref, seg_row_ref,
                       dqkv_ref, sums_ref, dk_ref, dv_ref):
    length = qkv_ref.shape[0]
    seg_col = column(seg_row_ref[...])
    for h in range(heads):
        lo = h * HEAD_DIM
        at_q, at_k, at_v = head_columns(h, heads)
        k = qkv_ref[:, at_k : at_k + HEAD_DIM]
        v = qkv_ref[:, at_v : at_v + HEAD_DIM]
        for t in range(length // TILE):
            rows = slice(t * TILE, (t + 1) * TILE)
            q = qkv_ref[rows, at_q : at_q + HEAD_DIM]
            dc = dctx_ref[rows, lo : lo + HEAD_DIM]
            same = seg_col == seg_row_ref[:, rows]
            s = jnp.where(same, nt(k, q) * SCALE, MASKED_SCORE)
            p = jnp.exp(s - lse_ref[h : h + 1, rows])
            ds = (p * (nt(v, dc) - delta_ref[h : h + 1, rows])).astype(BF16)
            dv = nn(p.astype(BF16), dc)
            dk = nn(ds, q)
            if t == 0:
                dv_ref[...] = dv
                dk_ref[...] = dk
            else:
                dv_ref[...] += dv
                dk_ref[...] += dk
            dqkv_ref[rows, at_q : at_q + HEAD_DIM] = (tn(ds, k) * SCALE).astype(BF16)
        dqkv_ref[:, at_k : at_k + HEAD_DIM] = (dk_ref[...] * SCALE).astype(BF16)
        dqkv_ref[:, at_v : at_v + HEAD_DIM] = dv_ref[...].astype(BF16)
    sums_ref[...] = jnp.sum(dqkv_ref[...].astype(F32), axis=0, keepdims=True)


def input_grad_kernel(place_ref, x_ref, g0_ref, g1_ref, w0_ref, w1_ref, keep_ref, send_ref,
                      sums_ref):
    tile = pl.program_id(0)

    @pl.when(tile == 0)
    def _():
        sums_ref[...] = jnp.zeros_like(sums_ref)

    out = nt(g0_ref[...], w0_ref[...]) + nt(g1_ref[...], w1_ref[...])
    normed, _ = standardize(x_ref[...].astype(F32))
    sums_ref[0:1] += jnp.sum(out * normed, axis=0, keepdims=True)
    sums_ref[1:2] += jnp.sum(out, axis=0, keepdims=True)
    out = out.astype(BF16)
    mine = tile % 2 == place_ref[1]

    @pl.when(mine)
    def _():
        keep_ref[...] = out

    @pl.when(jnp.logical_not(mine))
    def _():
        send_ref[...] = out


def final_kernel(place_ref, x_ref, da0_ref, da1_ref, dh_ref, vec_ref, dx_ref, send_ref):
    normed, inv = standardize(x_ref[...].astype(F32))
    da = da0_ref[...].astype(F32) + da1_ref[...].astype(F32)
    dx = dh_ref[...].astype(F32) + norm_back(da, normed, inv, vec_ref[0:1])
    dx_ref[...] = dx

    @pl.when(pl.program_id(0) != place_ref[2])
    def _():
        send_ref[...] = dx.astype(BF16)


def local(
    tokens,
    segment_ids,
    cotangent,
    attn_w,
    attn_m,
    attn_v,
    mlp_w,
    mlp_m,
    mlp_v,
    vectors,
    vec_m,
    vec_v,
):
    wide = lax.axis_size("wide")
    narrow = lax.axis_size("narrow")
    widx = lax.axis_index("wide")
    nidx = lax.axis_index("narrow")
    y = nidx // 2
    c = nidx % 2
    other = (1 - y) * 2 + c
    xbit = widx % 2
    even = xbit == 0
    first_core = c == 0
    first_y = y == 0
    _, shard_len, width = tokens.shape
    length = segment_ids.shape[1]
    cols = attn_w.shape[2]
    rows = attn_w.shape[1]
    hidden = mlp_w.shape[2]
    heads = cols // HEAD_DIM
    bits = wide.bit_length() - 1
    upper = wide // 2
    steps = [(b, min(2, bits - b)) for b in range(1, bits, 2)]

    def swap(value, partner):
        pairs = [
            (w * narrow + n, (lambda t: t[0] * narrow + t[1])(partner(w, n)))
            for w in range(wide)
            for n in range(narrow)
        ]
        return lax.ppermute(value, AXES, pairs)

    def over_core(value):
        return swap(value, lambda w, n: (w, n ^ 1))

    def over_y(value):
        return swap(value, lambda w, n: (w, n ^ 2))

    def over_x(value):
        return swap(value, lambda w, n: (w ^ 1, n))

    def over_wide(value, mask):
        return swap(value, lambda w, n: (w ^ mask, n))

    def mixed_one(value):
        return swap(value, lambda w, n: (w ^ 1, n) if n % 2 == 0 else (w, n ^ 2))

    def mixed_two(value):
        return swap(value, lambda w, n: (w ^ 1, n) if n % 2 == 1 else (w, n ^ 2))

    def tie(value, *deps):
        return lax.optimization_barrier((value, *deps))[0]

    def pair(flag, first, second, axis):
        return jnp.stack(
            [jnp.where(flag, first, second), jnp.where(flag, second, first)], axis=axis
        )

    def add_low(keep, came):
        return (keep.astype(F32) + came.astype(F32)).astype(BF16)

    def total_of(own, came, last):
        return own.astype(F32) + came.astype(F32) + last.astype(F32)

    def choose(index, values):
        picked = values[0]
        for i in range(1, len(values)):
            picked = jnp.where(index == i, values[i], picked)
        return picked

    def gather_upper(shard):
        held = shard[None]
        for b, count in steps:
            came = [over_wide(held, k << b) for k in range(1, 1 << count)]
            held = jnp.concatenate([held, *came], axis=0)
        return held

    def scatter_upper(total):
        for b, count in reversed(steps):
            size = total.shape[0] >> count
            digit = (widx >> b) & ((1 << count) - 1)
            blocks = [total[i * size : (i + 1) * size] for i in range(1 << count)]
            came = []
            for k in range(1, 1 << count):
                send = choose(digit, [blocks[i ^ k] for i in range(1 << count)])
                came.append(over_wide(send.astype(BF16), k << b))
            total = choose(digit, blocks).astype(F32)
            for each in came:
                total = total + each.astype(F32)
        return total, came

    def both(vector, size):
        return jnp.stack(
            [
                lax.dynamic_slice_in_dim(vector, nidx * size, size),
                lax.dynamic_slice_in_dim(vector, other * size, size),
            ]
        )

    tiles = length // TILE
    tile_spec = pl.BlockSpec((TILE, width), lambda t, *_: (t, 0))
    qkv_cols = 3 * cols
    matmul = 2 * length * width
    row_shape = jax.ShapeDtypeStruct((length, width), BF16)
    zero = jnp.int32(0)
    place = jnp.stack([xbit, c, y, widx // 2, zero, zero, zero, zero]).astype(jnp.int32)

    def spread_over_plane(held):
        from_x = over_x(held)
        from_y = over_y(held)
        return from_x, from_y

    def turn(from_x, from_y):
        return jnp.where(first_core, from_x, from_y)

    attn_low = attn_w.astype(BF16)
    attn_shard = jnp.concatenate([attn_low[i] for i in range(4)], axis=-1)

    mlp_low = mlp_w.astype(BF16)
    a_held = gather_upper(attn_shard)

    def row_pair(first):
        return jnp.stack(
            [jnp.where(first, v[0], v[1]) for v in (tokens, cotangent)]
        )

    rows_send = row_pair(jnp.logical_not(first_y))
    rows_came = over_y(tie(rows_send, attn_shard))
    rows_keep = row_pair(first_y)
    rows_keep_core = over_core(rows_keep)

    a_held, rows_came = lax.optimization_barrier((a_held, rows_came))
    a_x, a_y = spread_over_plane(a_held)
    rows_came_core = over_core(rows_came)
    u_held = gather_upper(tie(mlp_low[0], a_held, rows_came_core, rows_keep_core))
    query_bias = both(vectors[6], cols)
    value_bias = both(vectors[7], cols)
    no_bias = jnp.zeros_like(query_bias)
    qkv_bias = jnp.concatenate([query_bias, no_bias, value_bias], axis=1)
    up_bias = both(vectors[8:].reshape(-1), hidden)

    a_turn = turn(*lax.optimization_barrier((a_x, a_y, rows_came_core, rows_keep_core, qkv_bias, up_bias))[:2])
    a_diagonal = mixed_two(a_turn)
    u_x, u_y = None, None
    d_first = mlp_low[1][None]

    seg_own = lax.dynamic_index_in_dim(segment_ids, y, 0, False)
    seg_row = seg_own[None, :]
    part_spec = whole((2, shard_len, width))
    piece_spec = whole((upper, rows, width))
    qkv_shape = jax.ShapeDtypeStruct((length, qkv_cols), BF16)
    qkv_spec = pl.BlockSpec((TILE, qkv_cols), lambda t, *_: (t, 0))
    block_shapes = [
        qkv_shape,
        jax.ShapeDtypeStruct((width, qkv_cols), BF16),
        jax.ShapeDtypeStruct((width, cols), BF16),
    ]
    block_specs = [qkv_spec, whole((width, qkv_cols)), whole((width, cols))]
    x_row, dy_row, normed_low, qkv_mine, w_mine, o_mine = placed(
        first_qkv_kernel,
        (tiles,),
        [part_spec] * 4 + [piece_spec] * 2 + [whole(vectors.shape), whole((1, qkv_cols))],
        [tile_spec] * 3 + block_specs,
        [row_shape] * 3 + block_shapes,
    )(tie(place, a_turn), rows_keep, rows_came, rows_keep_core, rows_came_core, a_held, a_x,
      vectors, qkv_bias[0:1])

    d_first_came = over_wide(tie(d_first, a_turn), 2)
    d_first, d_first_came = lax.optimization_barrier((d_first, d_first_came, qkv_mine))[:2]
    d_second = jnp.concatenate([d_first, d_first_came], axis=0)
    d_second_came = over_wide(d_second, 4)
    u_x, u_y = spread_over_plane(tie(u_held, qkv_mine, d_first_came))
    ctx_spec = pl.BlockSpec((TILE, cols), lambda t, *_: (t, 0))
    lse_spec = pl.BlockSpec((8, TILE), lambda t: (0, t))
    ctx_shape = jax.ShapeDtypeStruct((length, cols), BF16)
    lse_shape = jax.ShapeDtypeStruct((8, length), F32)
    o_spec = whole((width, cols))

    def attend(qkv, segments, extra):
        last = bool(extra)
        in_specs = [
            qkv_spec,
            whole((length, qkv_cols)),
            pl.BlockSpec((1, TILE), lambda t: (0, t)),
            whole((1, length)),
        ]
        out_specs = [ctx_spec, lse_spec]
        out_shape = [ctx_shape, lse_shape]
        if last:
            in_specs += [ctx_spec, o_spec, o_spec]
            out_specs += [tile_spec]
            out_shape += [row_shape]
        return call(
            functools.partial(attend_kernel, last),
            (tiles,),
            in_specs,
            out_specs,
            out_shape,
            flops=4 * length * length * cols if last else 0,
        )(qkv, qkv, segments, segments, *extra)

    ctx_mine, lse_mine = attend(qkv_mine, tie(seg_row, d_second), ())
    a_y, a_diagonal = lax.optimization_barrier((a_y, a_diagonal, ctx_mine))[:2]
    qkv_others, w_others, o_others = placed(
        second_qkv_kernel,
        (tiles,),
        [tile_spec] + [piece_spec] * 2 + [whole((1, qkv_cols))],
        block_specs,
        block_shapes,
    )(place, normed_low, a_y, a_diagonal, qkv_bias[1:2])
    u_turn = turn(*lax.optimization_barrier((u_x, u_y, qkv_others))[:2])
    u_diagonal = mixed_two(u_turn)
    d_second, d_second_came = lax.optimization_barrier((d_second, d_second_came, qkv_others))[:2]
    d_second = jnp.concatenate([d_second, d_second_came], axis=0)

    def gather_rest(held):
        for b in range(3, bits):
            held = jnp.concatenate([held, over_wide(held, 1 << b)], axis=0)
        return held

    d_held = d_second if bits == 3 else gather_rest(d_second)
    ctx_others, lse_others, out_part = attend(
        qkv_others, tie(seg_row, u_turn, d_held), (ctx_mine, o_mine, o_others)
    )
    out_part, u_diagonal = lax.optimization_barrier((out_part, u_diagonal))
    out_came = over_core(out_part)
    d_x, d_y = spread_over_plane(tie(d_held, u_turn))
    d_diagonal = swap(tie(d_held, u_turn), lambda w, n: (w ^ 1, n ^ 2))

    pair_spec = pl.BlockSpec((2, TILE, hidden), lambda t, *_: (0, t, 0))
    pair_shape = jax.ShapeDtypeStruct((2, length, hidden), BF16)
    half_spec = pl.BlockSpec((None, TILE, width), lambda t, *_: (t // 2, 0, 0))

    def half_shape(dtype):
        return jax.ShapeDtypeStruct((2, shard_len, width), dtype)

    grad_specs = [piece_spec, whole((2, upper, rows, width)), piece_spec]
    grad_shapes = [
        jax.ShapeDtypeStruct((upper, rows, hidden), BF16),
        jax.ShapeDtypeStruct((2, upper, rows, hidden), BF16),
        jax.ShapeDtypeStruct((upper, rows, hidden), BF16),
    ]
    (second_low, hidden_row, activated, slope,
     gd_own, gd_send, gd_keep) = placed(
        up_kernel,
        (tiles,),
        [tile_spec] * 4 + [whole(vectors.shape), whole((2, hidden))] + [piece_spec] * 4,
        [tile_spec, tile_spec, pair_spec, pair_spec] + grad_specs,
        [row_shape, row_shape, pair_shape, pair_shape] + grad_shapes,
        scratch=[pltpu.VMEM((2, width, hidden), F32)] + [pltpu.VMEM((width, hidden), BF16)] * 2,
        flops=2 * matmul * 2 * hidden,
        nbytes=20_000_000,
        trans=4 * length * hidden,
    )(place, x_row, out_part, out_came, dy_row, vectors, up_bias, u_held, u_x, u_y, u_diagonal)
    gd_came = mixed_two(gd_send)

    def weight_grad(where, left, right, block):
        spec = pl.BlockSpec((upper, rows, block), lambda i, p: (0, 0, i))
        return placed(
            grad_kernel,
            (hidden // block,),
            [whole((length, width)), pl.BlockSpec((2, length, block), lambda i, p: (0, 0, i))],
            [spec, pl.BlockSpec((2, upper, rows, block), lambda i, p: (0, 0, 0, i)), spec],
            grad_shapes,
            scratch=[pltpu.VMEM((width, length), BF16)],
            flops=matmul * 2 * hidden,
            nbytes=8_000_000,
        )(where, left, right)

    def attn_weight_grad(dqkv_first, dqkv_second):
        part = width // 2
        left = pl.BlockSpec((length, part), lambda i, p: (0, i))
        spec = pl.BlockSpec((upper // 2, rows, width), lambda i, p: (i, 0, 0))
        return placed(
            two_grads_kernel,
            (2,),
            [left] * 2 + [whole((length, qkv_cols))] * 2 + [whole((length, cols))] * 2,
            [spec, pl.BlockSpec((2, upper // 2, rows, width), lambda i, p: (0, i, 0, 0)), spec],
            grad_shapes,
        )(place, normed_low, resid_low, dqkv_first, dqkv_second, ctx_mine, ctx_others)

    grad_pre, down_keep, down_send, second_part, up_bias_sums = placed(
        down_kernel,
        (tiles,),
        [tile_spec, pair_spec, pair_spec] + [piece_spec] * 8,
        [pair_spec, half_spec, half_spec, tile_spec, whole((2, hidden))],
        [pair_shape, half_shape(BF16), half_shape(BF16), row_shape,
         jax.ShapeDtypeStruct((2, hidden), F32)],
        scratch=[pltpu.VMEM((width, hidden), BF16)] * 4,
        flops=3 * matmul * 2 * hidden,
        nbytes=20_000_000,
    )(tie(place, gd_send), dy_row, activated, slope, u_held, u_x, u_y, u_diagonal, d_held, d_x,
      d_y, d_diagonal)
    second_part, gd_came = lax.optimization_barrier((second_part, gd_came))

    down_came = over_core(down_send)
    second_came = over_core(second_part)
    gu_own, gu_send, gu_keep = weight_grad(
        tie(place, second_part), second_low, grad_pre, 256
    )
    gu_came = mixed_two(gu_send)

    delta_spec = pl.BlockSpec((2, 8, TILE), lambda t, *_: (0, 0, t))
    resid_low, grad_ctx, delta, mid_sums, block_own, block_send = placed(
        mid_kernel,
        (tiles,),
        [tile_spec] * 4
        + [ctx_spec, ctx_spec, half_spec, half_spec, whole(vectors.shape), o_spec, o_spec],
        [tile_spec, pl.BlockSpec((2, TILE, cols), lambda t, *_: (0, t, 0)), delta_spec,
         whole((8, width)), half_spec, whole((shard_len, width))],
        [row_shape,
         jax.ShapeDtypeStruct((2, length, cols), BF16),
         jax.ShapeDtypeStruct((2, 8, length), F32),
         jax.ShapeDtypeStruct((8, width), F32), half_shape(BF16),
         jax.ShapeDtypeStruct((shard_len, width), BF16)],
        flops=matmul * 2 * cols,
        nbytes=10_000_000,
    )(place, hidden_row, dy_row, second_part, second_came, ctx_mine, ctx_others,
      down_keep, down_came, tie(vectors, gu_send), o_mine, o_others)

    block_came = over_y(block_send)

    def attend_back(j, qkv, lse, segments):
        return call(
            functools.partial(attend_back_kernel, heads),
            (1,),
            [whole((length, qkv_cols)),
             pl.BlockSpec((None, length, cols), lambda i: (j, 0, 0)),
             whole((8, length)),
             pl.BlockSpec((None, 8, length), lambda i: (j, 0, 0)),
             whole((1, length))],
            [whole((length, qkv_cols)), whole((1, qkv_cols))],
            [jax.ShapeDtypeStruct((length, qkv_cols), BF16),
             jax.ShapeDtypeStruct((1, qkv_cols), F32)],
            scratch=[pltpu.VMEM((length, HEAD_DIM), F32), pltpu.VMEM((length, HEAD_DIM), F32)],
        )(qkv, grad_ctx, lse, delta, segments)

    dqkv_mine, sums_mine = attend_back(0, qkv_mine, lse_mine, seg_row)
    gu_came = tie(gu_came, dqkv_mine)
    mlp_last_send = jnp.stack([add_low(gu_keep, gu_came[1]), add_low(gd_keep, gd_came[1])], axis=1)
    mlp_last = mixed_one(mlp_last_send)
    dqkv_others, sums_others = attend_back(1, qkv_others, lse_others, tie(seg_row, mlp_last_send))
    ga_own, ga_send, ga_keep = attn_weight_grad(dqkv_mine, dqkv_others)
    ga_came = mixed_two(ga_send)
    mlp_last = tie(mlp_last, ga_send)
    gu_sum = total_of(gu_own, gu_came[0], mlp_last[:, 0])
    gd_sum = total_of(gd_own, gd_came[0], mlp_last[:, 1])

    def halves(total, b):
        size = total.shape[0] // 2
        total = total.reshape(size, 2, *total.shape[1:])
        high = ((widx >> b) & 1) == 1
        return (
            jnp.where(high, total[:, 1], total[:, 0]),
            jnp.where(high, total[:, 0], total[:, 1]),
        )

    gu_keep, gu_send = halves(gu_sum, 1)
    gd_keep, gd_send = halves(gd_sum, 1)
    mlp_came = over_wide(jnp.stack([gu_send, gd_send], axis=1).astype(BF16), 2)

    half_out = pl.BlockSpec((None, TILE, width), lambda t, p: (t // 2, 0, 0))
    one_keep, one_send, one_sums = placed(
        input_grad_kernel,
        (tiles,),
        [tile_spec] + [pl.BlockSpec((TILE, qkv_cols), lambda t, p: (t, 0))] * 2
        + [whole((width, qkv_cols))] * 2,
        [half_out] * 2 + [whole((8, width))],
        [half_shape(BF16)] * 2 + [jax.ShapeDtypeStruct((8, width), F32)],
        flops=matmul * 2 * qkv_cols,
        nbytes=8_000_000,
    )(tie(place, gu_sum, gd_sum, block_came), x_row, dqkv_mine, dqkv_others, w_mine, w_others)
    one_send, mlp_came, ga_came = lax.optimization_barrier((one_send, mlp_came, ga_came))
    ga_send = add_low(ga_keep, ga_came[1])
    ga_last = mixed_one(ga_send)
    mlp_parts = [
        keep + mlp_came[:, i].astype(F32) for i, keep in enumerate((gu_keep, gd_keep))
    ]
    mlp_sends = []
    for b in range(2, bits):
        split = [halves(part, b) for part in mlp_parts]
        mlp_sends = [send.astype(BF16) for _, send in split]
        mlp_came = over_wide(jnp.stack(mlp_sends, axis=1), 1 << b)
        mlp_parts = [(keep, mlp_came[:, i]) for i, (keep, _) in enumerate(split)]
        if b < bits - 1:
            mlp_parts = [keep + came.astype(F32) for keep, came in mlp_parts]

    one_came = over_core(one_send)

    def spread(mine, others, size):
        empty = jnp.zeros((size * narrow,), F32)
        empty = lax.dynamic_update_slice_in_dim(empty, mine, nidx * size, 0)
        return lax.dynamic_update_slice_in_dim(empty, others, other * size, 0)

    vec_part = jnp.concatenate(
        [
            one_sums[:2],
            jnp.where(first_core, mid_sums[:4], 0.0),
            spread(sums_mine[0, :cols], sums_others[0, :cols], cols)[None],
            spread(sums_mine[0, 2 * cols :], sums_others[0, 2 * cols :], cols)[None],
            spread(up_bias_sums[0], up_bias_sums[1], hidden).reshape(-1, width),
        ],
        axis=0,
    )

    vec_came = mixed_two(vec_part)

    own_block = pl.BlockSpec((TILE, width), lambda t, p: (2 * t + p[1], 0))
    half_in = pl.BlockSpec((None, TILE, width), lambda t, p: (t, 0, 0))
    grad_own, last_send = placed(
        final_kernel,
        (2,),
        [own_block, half_in, half_in, own_block, whole(vectors.shape)],
        [half_in, whole((shard_len, width))],
        [half_shape(F32), jax.ShapeDtypeStruct((shard_len, width), BF16)],
        nbytes=9_000_000,
    )(tie(place, vec_part, ga_send, *mlp_sends), x_row, one_keep, one_came, resid_low, vectors)

    vec_came, last_send = lax.optimization_barrier((vec_came, last_send))
    vec_grad = vec_part + vec_came
    vec_grad = vec_grad + mixed_one(vec_grad)
    last_came = over_y(last_send)

    vec_here = vec_grad
    for b in range(1, bits - 1):
        vec_here = vec_here + over_wide(vec_here, 1 << b)
    ga_last = tie(ga_last, vec_grad, *mlp_sends)
    ga_sum = total_of(ga_own, ga_came[0], ga_last)
    ga_sum, vec_here = lax.optimization_barrier((ga_sum, vec_here))
    ga_sum, came = scatter_upper(ga_sum)
    vec_here = tie(vec_here, came[0])
    vec_grad = vec_here + over_wide(vec_here, 1 << (bits - 1))
    vec_grad = vec_grad + over_core(vec_grad)
    mlp_total = jnp.concatenate(
        [keep + tie(last, came[-1]).astype(F32) for keep, last in mlp_parts], axis=0
    )
    attn_total = ga_sum[0]

    def home(own, came):
        return lax.dynamic_update_slice(own, came[None].astype(own.dtype), (1 - y, 0, 0))

    block_out = home(block_own, block_came)
    block_input_gradient = home(grad_own, last_came)

    attn_grad = jnp.stack([attn_total[:, i * cols : (i + 1) * cols] for i in range(4)])
    mlp_grad = mlp_total
    attn_new, attn_m_new, attn_v_new = adamw_update(
        attn_w, attn_m, attn_v, attn_grad, RATE_MATRIX, DECAY_MATRIX
    )
    mlp_new, mlp_m_new, mlp_v_new = adamw_update(
        mlp_w, mlp_m, mlp_v, mlp_grad, RATE_MATRIX, DECAY_MATRIX
    )
    vec_new, vec_m_new, vec_v_new = adamw_update(vectors, vec_m, vec_v, vec_grad, RATE_VECTOR, 0.0)
    return (
        block_out,
        block_input_gradient,
        attn_grad,
        attn_new,
        attn_m_new,
        attn_v_new,
        mlp_grad,
        mlp_new,
        mlp_m_new,
        mlp_v_new,
        vec_grad,
        vec_new,
        vec_m_new,
        vec_v_new,
    )


def solution(mesh):
    matrix = P(None, "wide", "narrow")
    rows = P("wide", "narrow", None)
    in_specs = (rows, P("wide", None), rows) + (matrix,) * 6 + (P(),) * 3
    out_specs = (rows, rows) + (matrix,) * 8 + (P(),) * 4
    return jax.shard_map(local, mesh=mesh, in_specs=in_specs, out_specs=out_specs, check_vma=False)
```

```python
import functools

import jax
import jax.numpy as jnp
from jax import lax
from jax.experimental import pallas as pl
from jax.experimental.pallas import tpu as pltpu
from jax.sharding import PartitionSpec as P

HEAD_DIM = 64
STEP = 10


EPS_NORM = 1e-06
MASKED_SCORE = -1e30
BETA_ONE = 0.5
BETA_TWO = 0.5
EPS_ADAM = 1e-08
RATE_MATRIX = 0.04
RATE_VECTOR = 0.3
DECAY_MATRIX = 0.05
SCALE = HEAD_DIM ** (-0.5)
TILE = 256
F32 = jnp.float32
BF16 = jnp.bfloat16
AXES = ("wide", "narrow")
COST_SCALE = 1
VMEM_LIMIT = 48 * 1024 * 1024


def adamw_update(weight, first_mom, second, gradient, step_rate, decay_rate):
    first_new = BETA_ONE * first_mom + (1.0 - BETA_ONE) * gradient
    second_new = BETA_TWO * second + (1.0 - BETA_TWO) * gradient * gradient
    corrected = (
        first_new
        / (1.0 - BETA_ONE**STEP)
        / (jnp.sqrt(second_new / (1.0 - BETA_TWO**STEP)) + EPS_ADAM)
    )
    return (weight - step_rate * (corrected + decay_rate * weight), first_new, second_new)


def nn(a, b):
    return lax.dot_general(a, b, (((1,), (0,)), ((), ())), preferred_element_type=F32)


def nt(a, b):
    return lax.dot_general(a, b, (((1,), (1,)), ((), ())), preferred_element_type=F32)


def tn(a, b):
    return lax.dot_general(a, b, (((0,), (0,)), ((), ())), preferred_element_type=F32)


def standardize(v):
    centred = v - jnp.mean(v, axis=-1, keepdims=True)
    inv = lax.rsqrt(jnp.mean(centred * centred, axis=-1, keepdims=True) + EPS_NORM)
    return centred * inv, inv


def norm_back(grad_out, normed, inv, gain):
    scaled = grad_out * gain
    return inv * (
        scaled
        - jnp.mean(scaled, axis=-1, keepdims=True)
        - normed * jnp.mean(scaled * normed, axis=-1, keepdims=True)
    )


def whole(shape):
    return pl.BlockSpec(shape, lambda *_: (0,) * len(shape))


def params(cost=None):
    return pltpu.CompilerParams(
        dimension_semantics=("arbitrary",), vmem_limit_bytes=VMEM_LIMIT
    )


def call(kernel, grid, in_specs, out_specs, out_shape, scratch=(), flops=0, nbytes=0, trans=0):
    return pl.pallas_call(
        kernel,
        grid=grid,
        in_specs=in_specs,
        out_specs=out_specs,
        out_shape=out_shape,
        scratch_shapes=scratch,
        compiler_params=params(),
        cost_estimate=pl.CostEstimate(
            flops=flops // COST_SCALE,
            bytes_accessed=nbytes // COST_SCALE,
            transcendentals=trans // COST_SCALE,
        ),
    )


def placed(kernel, grid, in_specs, out_specs, out_shape, scratch=(), flops=0, nbytes=0, trans=0):
    return pl.pallas_call(
        kernel,
        grid_spec=pltpu.PrefetchScalarGridSpec(
            num_scalar_prefetch=1,
            grid=grid,
            in_specs=in_specs,
            out_specs=out_specs,
            scratch_shapes=scratch,
        ),
        out_shape=out_shape,
        compiler_params=params(),
        cost_estimate=pl.CostEstimate(
            flops=flops // COST_SCALE,
            bytes_accessed=nbytes // COST_SCALE,
            transcendentals=trans // COST_SCALE,
        ),
    )


def head_columns(h, heads):
    return tuple((kind * heads + h) * HEAD_DIM for kind in range(3))


def block_rows(place_ref, near_ref, far_ref, store):
    even = place_ref[0] == 0
    upper = place_ref[3]
    count, rows, _ = near_ref.shape
    for u in range(count):
        src = lax.bitwise_xor(upper, jnp.int32(u))
        for x in range(2):
            at = slice((2 * u + x) * rows, (2 * u + x + 1) * rows)
            same = even if x == 0 else jnp.logical_not(even)
            store(at, jnp.where(same, near_ref[src], far_ref[src]))


def natural(place_ref, pieces, targets):
    held_ref, from_x_ref, from_y_ref, diagonal_ref = pieces
    block_rows(place_ref, held_ref, from_x_ref, functools.partial(targets, 0))
    block_rows(place_ref, from_y_ref, diagonal_ref, functools.partial(targets, 1))


def pick_row(place_ref, tile, part, refs):
    keep_ref, came_ref, keep_core_ref, came_core_ref = refs
    same_y = tile // 2 == place_ref[2]
    same_core = tile % 2 == place_ref[1]
    return jnp.where(
        same_y,
        jnp.where(same_core, keep_ref[part], keep_core_ref[part]),
        jnp.where(same_core, came_ref[part], came_core_ref[part]),
    )


def project(place_ref, near_ref, far_ref, low, bias_ref, qkv_ref, w_ref, o_ref):
    cols = w_ref.shape[1]

    @pl.when(pl.program_id(0) == 0)
    def _():
        def store(at, value):
            w_ref[at] = value[:, :cols]
            o_ref[at] = value[:, cols:]

        block_rows(place_ref, near_ref, far_ref, store)

    qkv_ref[...] = (nn(low, w_ref[...]) + bias_ref[...]).astype(BF16)


def first_qkv_kernel(place_ref, *refs):
    rows = refs[:4]
    near_ref, far_ref, vec_ref, bias_ref, x_ref, dy_ref, a_ref, *outs = refs[4:]
    x = pick_row(place_ref, pl.program_id(0), 0, rows)
    x_ref[...] = x
    dy_ref[...] = pick_row(place_ref, pl.program_id(0), 1, rows)
    normed, _ = standardize(x.astype(F32))
    low = (normed * vec_ref[0:1] + vec_ref[1:2]).astype(BF16)
    a_ref[...] = low
    project(place_ref, near_ref, far_ref, low, bias_ref, *outs)


def second_qkv_kernel(place_ref, a_ref, near_ref, far_ref, bias_ref, *outs):
    project(place_ref, near_ref, far_ref, a_ref[...], bias_ref, *outs)


def column(row):
    return jnp.broadcast_to(row, (128, row.shape[1])).T[:, :1]


def attend_kernel(last, qkv_q_ref, qkv_ref, seg_tile_ref, seg_row_ref, *refs):
    if last:
        ctx_in_ref, o0_ref, o1_ref, ctx_ref, lse_ref, out_ref = refs
    else:
        ctx_ref, lse_ref = refs
    cols = ctx_ref.shape[1]
    heads = cols // HEAD_DIM
    same = column(seg_tile_ref[...]) == seg_row_ref[...]
    lane = lax.broadcasted_iota(jnp.int32, (TILE, 128), 1)
    totals = jnp.zeros((TILE, 128), F32)
    for h in range(heads):
        lo = h * HEAD_DIM
        at_q, at_k, at_v = head_columns(h, heads)
        q = qkv_q_ref[:, at_q : at_q + HEAD_DIM]
        k = qkv_ref[:, at_k : at_k + HEAD_DIM]
        v = qkv_ref[:, at_v : at_v + HEAD_DIM]
        s = jnp.where(same, nt(q, k) * SCALE, MASKED_SCORE)
        top = jnp.max(s, axis=-1, keepdims=True)
        e = jnp.exp(s - top)
        total = jnp.sum(e, axis=-1, keepdims=True)
        o = nn(e.astype(BF16), v) / total
        ctx_ref[:, lo : lo + HEAD_DIM] = o.astype(BF16)
        totals = jnp.where(lane == h, top + jnp.log(total), totals)
    lse_ref[...] = totals.T[: lse_ref.shape[0]]
    if last:
        out_ref[...] = (nt(ctx_in_ref[...], o0_ref[...]) + nt(ctx_ref[...], o1_ref[...])).astype(BF16)


def sort_grad(place_ref, mine, others, own_ref, send_ref, keep_ref, at):
    even = place_ref[0] == 0
    first = place_ref[1] == 0
    rows = own_ref.shape[1]
    for u in range(own_ref.shape[0]):
        lo = slice(2 * u * rows, (2 * u + 1) * rows)
        hi = slice((2 * u + 1) * rows, (2 * u + 2) * rows)
        own_ref[u, :, at] = jnp.where(even, mine[lo], mine[hi])
        to_x = jnp.where(even, mine[hi], mine[lo])
        to_y = jnp.where(even, others[lo], others[hi])
        send_ref[0, u, :, at] = jnp.where(first, to_y, to_x)
        keep_ref[u, :, at] = jnp.where(first, to_x, to_y)
        send_ref[1, u, :, at] = jnp.where(even, others[hi], others[lo])


def add_grad(total_ref, j, left, right):
    part = tn(left, right)

    @pl.when(pl.program_id(0) == 0)
    def _():
        total_ref[j] = part

    @pl.when(pl.program_id(0) > 0)
    def _():
        total_ref[j] += part


def up_kernel(place_ref, x_ref, p0_ref, p1_ref, dy_ref, vec_ref, bu_ref, *refs):
    pieces = refs[:4]
    (a_ref, h_ref, z_ref, slope_ref,
     g_own_ref, g_send_ref, g_keep_ref, total_ref, u0_ref, u1_ref) = refs[4:]
    tile = pl.program_id(0)

    @pl.when(tile == 0)
    def _():
        def store(j, at, value):
            (u0_ref, u1_ref)[j][at] = value

        natural(place_ref, pieces, store)

    h = x_ref[...].astype(F32) + (p0_ref[...].astype(F32) + p1_ref[...].astype(F32)) + vec_ref[4:5]

    h_ref[...] = h.astype(BF16)
    normed, _ = standardize(h)
    a = (normed * vec_ref[2:3] + vec_ref[3:4]).astype(BF16)
    a_ref[...] = a
    dy = dy_ref[...]
    for j, u_ref in enumerate((u0_ref, u1_ref)):
        u = nn(a, u_ref[...]) + bu_ref[j : j + 1]
        cdf = 0.5 + 0.5 * lax.erf(u * 0.7071067811865476)
        z = (u * cdf).astype(BF16)
        z_ref[j] = z
        slope_ref[j] = (cdf + u * (0.3989422804014327 * jnp.exp(-0.5 * u * u))).astype(BF16)
        add_grad(total_ref, j, dy, z)

    @pl.when(tile == pl.num_programs(0) - 1)
    def _():
        sort_grad(place_ref, total_ref[0].astype(BF16), total_ref[1].astype(BF16),
                  g_own_ref, g_send_ref, g_keep_ref, slice(None))


def down_kernel(place_ref, dy_ref, z_ref, slope_ref, *refs):
    up_pieces = refs[:4]
    pieces = refs[4:8]
    du_ref, keep_ref, send_ref, da_ref, gbu_ref, d0_ref, d1_ref, u0_ref, u1_ref = refs[8:]
    tile = pl.program_id(0)

    @pl.when(tile == 0)
    def _():
        gbu_ref[...] = jnp.zeros_like(gbu_ref)

        def store_up(j, at, value):
            (u0_ref, u1_ref)[j][at] = value

        def store(j, at, value):
            (d0_ref, d1_ref)[j][at] = value

        natural(place_ref, up_pieces, store_up)
        natural(place_ref, pieces, store)

    dy = dy_ref[...]
    down = jnp.zeros(da_ref.shape, F32)
    da = jnp.zeros(da_ref.shape, F32)
    for j, (u_ref, d_ref) in enumerate(((u0_ref, d0_ref), (u1_ref, d1_ref))):
        du = (nn(dy, d_ref[...]) * slope_ref[j].astype(F32)).astype(BF16)
        du_ref[j] = du
        gbu_ref[j : j + 1] += jnp.sum(du.astype(F32), axis=0, keepdims=True)
        down += nt(z_ref[j], d_ref[...])
        da += nt(du, u_ref[...])
    da_ref[...] = da.astype(BF16)
    down = down.astype(BF16)
    mine = tile % 2 == place_ref[1]

    @pl.when(mine)
    def _():
        keep_ref[...] = down

    @pl.when(jnp.logical_not(mine))
    def _():
        send_ref[...] = down


def grad_kernel(place_ref, left_ref, right_ref, own_ref, send_ref, keep_ref, turned_ref):
    @pl.when(pl.program_id(0) == 0)
    def _():
        turned_ref[...] = left_ref[...].T

    turned = turned_ref[...]
    mine = nn(turned, right_ref[0]).astype(BF16)
    others = nn(turned, right_ref[1]).astype(BF16)
    sort_grad(place_ref, mine, others, own_ref, send_ref, keep_ref, slice(None))


def two_grads_kernel(place_ref, left_ref, dh_ref, dqkv0_ref, dqkv1_ref, ctx0_ref, ctx1_ref,
                     own_ref, send_ref, keep_ref):
    many = dqkv0_ref.shape[1]
    turned = left_ref[...].T
    mine = nn(turned, dqkv0_ref[...]).astype(BF16)
    others = nn(turned, dqkv1_ref[...]).astype(BF16)
    sort_grad(place_ref, mine, others, own_ref, send_ref, keep_ref, slice(0, many))
    turned = dh_ref[...].T
    mine = nn(turned, ctx0_ref[...]).astype(BF16)
    others = nn(turned, ctx1_ref[...]).astype(BF16)
    sort_grad(place_ref, mine, others, own_ref, send_ref, keep_ref, slice(many, None))


def mid_kernel(place_ref, h_ref, dy_ref, da0_ref, da1_ref, ctx0_ref, ctx1_ref, keep_ref, came_ref,
               vec_ref, o0_ref, o1_ref, dh_ref, dctx_ref, delta_ref, sums_ref, out_ref, send_ref):
    tile = pl.program_id(0)

    @pl.when(tile % 2 == place_ref[1])
    def _():
        out = h_ref[...].astype(F32) + (keep_ref[...].astype(F32) + came_ref[...].astype(F32))
        out = (out + vec_ref[5:6]).astype(BF16)
        out_ref[...] = out

        @pl.when(tile // 2 != place_ref[2])
        def _():
            send_ref[...] = out

    @pl.when(pl.program_id(0) == 0)
    def _():
        sums_ref[...] = jnp.zeros_like(sums_ref)

    normed, inv = standardize(h_ref[...].astype(F32))
    da = da0_ref[...].astype(F32) + da1_ref[...].astype(F32)
    dy = dy_ref[...].astype(F32)
    dh = dy + norm_back(da, normed, inv, vec_ref[2:3])
    low = dh.astype(BF16)
    dh_ref[...] = low
    sums_ref[0:1] += jnp.sum(da * normed, axis=0, keepdims=True)
    sums_ref[1:2] += jnp.sum(da, axis=0, keepdims=True)
    sums_ref[2:3] += jnp.sum(dh, axis=0, keepdims=True)
    sums_ref[3:4] += jnp.sum(dy, axis=0, keepdims=True)
    cols = ctx0_ref.shape[1]
    head = lax.broadcasted_iota(jnp.int32, (8, cols), 0)
    owner = lax.broadcasted_iota(jnp.int32, (8, cols), 1) // HEAD_DIM
    member = jnp.where(head == owner, 1.0, 0.0).astype(BF16)
    for j, (o_ref, ctx_ref) in enumerate(((o0_ref, ctx0_ref), (o1_ref, ctx1_ref))):
        dctx = nn(low, o_ref[...]).astype(BF16)
        dctx_ref[j] = dctx
        prod = dctx.astype(F32) * ctx_ref[...].astype(F32)
        high = prod.astype(BF16)
        rest = (prod - high.astype(F32)).astype(BF16)
        delta_ref[j] = nt(member, high) + nt(member, rest)


def attend_back_kernel(heads, qkv_ref, dctx_ref, lse_ref, delta_ref, seg_row_ref,
                       dqkv_ref, sums_ref, dk_ref, dv_ref):
    length = qkv_ref.shape[0]
    seg_col = column(seg_row_ref[...])
    for h in range(heads):
        lo = h * HEAD_DIM
        at_q, at_k, at_v = head_columns(h, heads)
        k = qkv_ref[:, at_k : at_k + HEAD_DIM]
        v = qkv_ref[:, at_v : at_v + HEAD_DIM]
        for t in range(length // TILE):
            rows = slice(t * TILE, (t + 1) * TILE)
            q = qkv_ref[rows, at_q : at_q + HEAD_DIM]
            dc = dctx_ref[rows, lo : lo + HEAD_DIM]
            same = seg_col == seg_row_ref[:, rows]
            s = jnp.where(same, nt(k, q) * SCALE, MASKED_SCORE)
            p = jnp.exp(s - lse_ref[h : h + 1, rows])
            ds = (p * (nt(v, dc) - delta_ref[h : h + 1, rows])).astype(BF16)
            dv = nn(p.astype(BF16), dc)
            dk = nn(ds, q)
            if t == 0:
                dv_ref[...] = dv
                dk_ref[...] = dk
            else:
                dv_ref[...] += dv
                dk_ref[...] += dk
            dqkv_ref[rows, at_q : at_q + HEAD_DIM] = (tn(ds, k) * SCALE).astype(BF16)
        dqkv_ref[:, at_k : at_k + HEAD_DIM] = (dk_ref[...] * SCALE).astype(BF16)
        dqkv_ref[:, at_v : at_v + HEAD_DIM] = dv_ref[...].astype(BF16)
    sums_ref[...] = jnp.sum(dqkv_ref[...].astype(F32), axis=0, keepdims=True)


def input_grad_kernel(place_ref, x_ref, g0_ref, g1_ref, w0_ref, w1_ref, keep_ref, send_ref,
                      sums_ref):
    tile = pl.program_id(0)

    @pl.when(tile == 0)
    def _():
        sums_ref[...] = jnp.zeros_like(sums_ref)

    out = nt(g0_ref[...], w0_ref[...]) + nt(g1_ref[...], w1_ref[...])
    normed, _ = standardize(x_ref[...].astype(F32))
    sums_ref[0:1] += jnp.sum(out * normed, axis=0, keepdims=True)
    sums_ref[1:2] += jnp.sum(out, axis=0, keepdims=True)
    out = out.astype(BF16)
    mine = tile % 2 == place_ref[1]

    @pl.when(mine)
    def _():
        keep_ref[...] = out

    @pl.when(jnp.logical_not(mine))
    def _():
        send_ref[...] = out


def final_kernel(place_ref, x_ref, da0_ref, da1_ref, dh_ref, vec_ref, dx_ref, send_ref):
    normed, inv = standardize(x_ref[...].astype(F32))
    da = da0_ref[...].astype(F32) + da1_ref[...].astype(F32)
    dx = dh_ref[...].astype(F32) + norm_back(da, normed, inv, vec_ref[0:1])
    dx_ref[...] = dx

    @pl.when(pl.program_id(0) != place_ref[2])
    def _():
        send_ref[...] = dx.astype(BF16)


def local(
    tokens,
    segment_ids,
    cotangent,
    attn_w,
    attn_m,
    attn_v,
    mlp_w,
    mlp_m,
    mlp_v,
    vectors,
    vec_m,
    vec_v,
):
    wide = lax.axis_size("wide")
    narrow = lax.axis_size("narrow")
    widx = lax.axis_index("wide")
    nidx = lax.axis_index("narrow")
    y = nidx // 2
    c = nidx % 2
    other = (1 - y) * 2 + c
    xbit = widx % 2
    even = xbit == 0
    first_core = c == 0
    first_y = y == 0
    _, shard_len, width = tokens.shape
    length = segment_ids.shape[1]
    cols = attn_w.shape[2]
    rows = attn_w.shape[1]
    hidden = mlp_w.shape[2]
    heads = cols // HEAD_DIM
    bits = wide.bit_length() - 1
    upper = wide // 2
    steps = [(b, min(2, bits - b)) for b in range(1, bits, 2)]

    def swap(value, partner):
        pairs = [
            (w * narrow + n, (lambda t: t[0] * narrow + t[1])(partner(w, n)))
            for w in range(wide)
            for n in range(narrow)
        ]
        return lax.ppermute(value, AXES, pairs)

    def over_core(value):
        return swap(value, lambda w, n: (w, n ^ 1))

    def over_y(value):
        return swap(value, lambda w, n: (w, n ^ 2))

    def over_x(value):
        return swap(value, lambda w, n: (w ^ 1, n))

    def over_wide(value, mask):
        return swap(value, lambda w, n: (w ^ mask, n))

    def mixed_one(value):
        return swap(value, lambda w, n: (w ^ 1, n) if n % 2 == 0 else (w, n ^ 2))

    def mixed_two(value):
        return swap(value, lambda w, n: (w ^ 1, n) if n % 2 == 1 else (w, n ^ 2))

    def tie(value, *deps):
        return lax.optimization_barrier((value, *deps))[0]

    def pair(flag, first, second, axis):
        return jnp.stack(
            [jnp.where(flag, first, second), jnp.where(flag, second, first)], axis=axis
        )

    def add_low(keep, came):
        return (keep.astype(F32) + came.astype(F32)).astype(BF16)

    def total_of(own, came, last):
        return own.astype(F32) + came.astype(F32) + last.astype(F32)

    def choose(index, values):
        picked = values[0]
        for i in range(1, len(values)):
            picked = jnp.where(index == i, values[i], picked)
        return picked

    def gather_upper(shard):
        held = shard[None]
        for b, count in steps:
            came = [over_wide(held, k << b) for k in range(1, 1 << count)]
            held = jnp.concatenate([held, *came], axis=0)
        return held

    def scatter_upper(total):
        for b, count in reversed(steps):
            size = total.shape[0] >> count
            digit = (widx >> b) & ((1 << count) - 1)
            blocks = [total[i * size : (i + 1) * size] for i in range(1 << count)]
            came = []
            for k in range(1, 1 << count):
                send = choose(digit, [blocks[i ^ k] for i in range(1 << count)])
                came.append(over_wide(send.astype(BF16), k << b))
            total = choose(digit, blocks).astype(F32)
            for each in came:
                total = total + each.astype(F32)
        return total, came

    def both(vector, size):
        return jnp.stack(
            [
                lax.dynamic_slice_in_dim(vector, nidx * size, size),
                lax.dynamic_slice_in_dim(vector, other * size, size),
            ]
        )

    tiles = length // TILE
    tile_spec = pl.BlockSpec((TILE, width), lambda t, *_: (t, 0))
    qkv_cols = 3 * cols
    matmul = 2 * length * width
    row_shape = jax.ShapeDtypeStruct((length, width), BF16)
    zero = jnp.int32(0)
    place = jnp.stack([xbit, c, y, widx // 2, zero, zero, zero, zero]).astype(jnp.int32)

    def spread_over_plane(held):
        from_x = over_x(held)
        from_y = over_y(held)
        return from_x, from_y

    def turn(from_x, from_y):
        return jnp.where(first_core, from_x, from_y)

    attn_low = attn_w.astype(BF16)
    attn_shard = jnp.concatenate([attn_low[i] for i in range(4)], axis=-1)

    mlp_low = mlp_w.astype(BF16)
    a_held = gather_upper(attn_shard)

    def row_pair(first):
        return jnp.stack(
            [jnp.where(first, v[0], v[1]) for v in (tokens, cotangent)]
        )

    rows_send = row_pair(jnp.logical_not(first_y))
    rows_came = over_y(tie(rows_send, attn_shard))
    rows_keep = row_pair(first_y)
    rows_keep_core = over_core(rows_keep)

    a_held, rows_came = lax.optimization_barrier((a_held, rows_came))
    a_x, a_y = spread_over_plane(a_held)
    rows_came_core = over_core(rows_came)
    u_held = gather_upper(tie(mlp_low[0], a_held, rows_came_core, rows_keep_core))
    query_bias = both(vectors[6], cols)
    value_bias = both(vectors[7], cols)
    no_bias = jnp.zeros_like(query_bias)
    qkv_bias = jnp.concatenate([query_bias, no_bias, value_bias], axis=1)
    up_bias = both(vectors[8:].reshape(-1), hidden)

    a_turn = turn(*lax.optimization_barrier((a_x, a_y, rows_came_core, rows_keep_core, qkv_bias, up_bias))[:2])
    a_diagonal = mixed_two(a_turn)
    u_x, u_y = None, None
    d_first = mlp_low[1][None]

    seg_own = lax.dynamic_index_in_dim(segment_ids, y, 0, False)
    seg_row = seg_own[None, :]
    part_spec = whole((2, shard_len, width))
    piece_spec = whole((upper, rows, width))
    qkv_shape = jax.ShapeDtypeStruct((length, qkv_cols), BF16)
    qkv_spec = pl.BlockSpec((TILE, qkv_cols), lambda t, *_: (t, 0))
    block_shapes = [
        qkv_shape,
        jax.ShapeDtypeStruct((width, qkv_cols), BF16),
        jax.ShapeDtypeStruct((width, cols), BF16),
    ]
    block_specs = [qkv_spec, whole((width, qkv_cols)), whole((width, cols))]
    x_row, dy_row, normed_low, qkv_mine, w_mine, o_mine = placed(
        first_qkv_kernel,
        (tiles,),
        [part_spec] * 4 + [piece_spec] * 2 + [whole(vectors.shape), whole((1, qkv_cols))],
        [tile_spec] * 3 + block_specs,
        [row_shape] * 3 + block_shapes,
    )(tie(place, a_turn), rows_keep, rows_came, rows_keep_core, rows_came_core, a_held, a_x,
      vectors, qkv_bias[0:1])

    d_first_came = over_wide(tie(d_first, a_turn), 2)
    d_first, d_first_came = lax.optimization_barrier((d_first, d_first_came, qkv_mine))[:2]
    d_second = jnp.concatenate([d_first, d_first_came], axis=0)
    d_second_came = over_wide(d_second, 4)
    u_x, u_y = spread_over_plane(tie(u_held, qkv_mine, d_first_came))
    ctx_spec = pl.BlockSpec((TILE, cols), lambda t, *_: (t, 0))
    lse_spec = pl.BlockSpec((8, TILE), lambda t: (0, t))
    ctx_shape = jax.ShapeDtypeStruct((length, cols), BF16)
    lse_shape = jax.ShapeDtypeStruct((8, length), F32)
    o_spec = whole((width, cols))

    def attend(qkv, segments, extra):
        last = bool(extra)
        in_specs = [
            qkv_spec,
            whole((length, qkv_cols)),
            pl.BlockSpec((1, TILE), lambda t: (0, t)),
            whole((1, length)),
        ]
        out_specs = [ctx_spec, lse_spec]
        out_shape = [ctx_shape, lse_shape]
        if last:
            in_specs += [ctx_spec, o_spec, o_spec]
            out_specs += [tile_spec]
            out_shape += [row_shape]
        return call(
            functools.partial(attend_kernel, last),
            (tiles,),
            in_specs,
            out_specs,
            out_shape,
            flops=4 * length * length * cols if last else 0,
        )(qkv, qkv, segments, segments, *extra)

    ctx_mine, lse_mine = attend(qkv_mine, tie(seg_row, d_second), ())
    a_y, a_diagonal = lax.optimization_barrier((a_y, a_diagonal, ctx_mine))[:2]
    qkv_others, w_others, o_others = placed(
        second_qkv_kernel,
        (tiles,),
        [tile_spec] + [piece_spec] * 2 + [whole((1, qkv_cols))],
        block_specs,
        block_shapes,
    )(place, normed_low, a_y, a_diagonal, qkv_bias[1:2])
    u_turn = turn(*lax.optimization_barrier((u_x, u_y, qkv_others))[:2])
    u_diagonal = mixed_two(u_turn)
    d_second, d_second_came = lax.optimization_barrier((d_second, d_second_came, qkv_others))[:2]
    d_second = jnp.concatenate([d_second, d_second_came], axis=0)

    def gather_rest(held):
        for b in range(3, bits):
            held = jnp.concatenate([held, over_wide(held, 1 << b)], axis=0)
        return held

    d_held = d_second if bits == 3 else gather_rest(d_second)
    ctx_others, lse_others, out_part = attend(
        qkv_others, tie(seg_row, u_turn, d_held), (ctx_mine, o_mine, o_others)
    )
    out_part, u_diagonal = lax.optimization_barrier((out_part, u_diagonal))
    out_came = over_core(out_part)
    d_x, d_y = spread_over_plane(tie(d_held, u_turn))
    d_diagonal = swap(tie(d_held, u_turn), lambda w, n: (w ^ 1, n ^ 2))

    pair_spec = pl.BlockSpec((2, TILE, hidden), lambda t, *_: (0, t, 0))
    pair_shape = jax.ShapeDtypeStruct((2, length, hidden), BF16)
    half_spec = pl.BlockSpec((None, TILE, width), lambda t, *_: (t // 2, 0, 0))

    def half_shape(dtype):
        return jax.ShapeDtypeStruct((2, shard_len, width), dtype)

    grad_specs = [piece_spec, whole((2, upper, rows, width)), piece_spec]
    grad_shapes = [
        jax.ShapeDtypeStruct((upper, rows, hidden), BF16),
        jax.ShapeDtypeStruct((2, upper, rows, hidden), BF16),
        jax.ShapeDtypeStruct((upper, rows, hidden), BF16),
    ]
    (second_low, hidden_row, activated, slope,
     gd_own, gd_send, gd_keep) = placed(
        up_kernel,
        (tiles,),
        [tile_spec] * 4 + [whole(vectors.shape), whole((2, hidden))] + [piece_spec] * 4,
        [tile_spec, tile_spec, pair_spec, pair_spec] + grad_specs,
        [row_shape, row_shape, pair_shape, pair_shape] + grad_shapes,
        scratch=[pltpu.VMEM((2, width, hidden), F32)] + [pltpu.VMEM((width, hidden), BF16)] * 2,
        flops=2 * matmul * 2 * hidden,
        nbytes=20_000_000,
        trans=4 * length * hidden,
    )(place, x_row, out_part, out_came, dy_row, vectors, up_bias, u_held, u_x, u_y, u_diagonal)
    gd_came = mixed_two(gd_send)

    def weight_grad(where, left, right, block):
        spec = pl.BlockSpec((upper, rows, block), lambda i, p: (0, 0, i))
        return placed(
            grad_kernel,
            (hidden // block,),
            [whole((length, width)), pl.BlockSpec((2, length, block), lambda i, p: (0, 0, i))],
            [spec, pl.BlockSpec((2, upper, rows, block), lambda i, p: (0, 0, 0, i)), spec],
            grad_shapes,
            scratch=[pltpu.VMEM((width, length), BF16)],
            flops=matmul * 2 * hidden,
            nbytes=8_000_000,
        )(where, left, right)

    def attn_weight_grad(dqkv_first, dqkv_second):
        part = width // 2
        left = pl.BlockSpec((length, part), lambda i, p: (0, i))
        spec = pl.BlockSpec((upper // 2, rows, width), lambda i, p: (i, 0, 0))
        return placed(
            two_grads_kernel,
            (2,),
            [left] * 2 + [whole((length, qkv_cols))] * 2 + [whole((length, cols))] * 2,
            [spec, pl.BlockSpec((2, upper // 2, rows, width), lambda i, p: (0, i, 0, 0)), spec],
            grad_shapes,
        )(place, normed_low, resid_low, dqkv_first, dqkv_second, ctx_mine, ctx_others)

    grad_pre, down_keep, down_send, second_part, up_bias_sums = placed(
        down_kernel,
        (tiles,),
        [tile_spec, pair_spec, pair_spec] + [piece_spec] * 8,
        [pair_spec, half_spec, half_spec, tile_spec, whole((2, hidden))],
        [pair_shape, half_shape(BF16), half_shape(BF16), row_shape,
         jax.ShapeDtypeStruct((2, hidden), F32)],
        scratch=[pltpu.VMEM((width, hidden), BF16)] * 4,
        flops=3 * matmul * 2 * hidden,
        nbytes=20_000_000,
    )(tie(place, gd_send), dy_row, activated, slope, u_held, u_x, u_y, u_diagonal, d_held, d_x,
      d_y, d_diagonal)
    second_part, gd_came = lax.optimization_barrier((second_part, gd_came))

    down_came = over_core(down_send)
    second_came = over_core(second_part)
    gu_own, gu_send, gu_keep = weight_grad(
        tie(place, second_part), second_low, grad_pre, 256
    )
    gu_send, down_came = lax.optimization_barrier((gu_send, down_came))
    gu_came = mixed_two(gu_send)

    delta_spec = pl.BlockSpec((2, 8, TILE), lambda t, *_: (0, 0, t))
    resid_low, grad_ctx, delta, mid_sums, block_own, block_send = placed(
        mid_kernel,
        (tiles,),
        [tile_spec] * 4
        + [ctx_spec, ctx_spec, half_spec, half_spec, whole(vectors.shape), o_spec, o_spec],
        [tile_spec, pl.BlockSpec((2, TILE, cols), lambda t, *_: (0, t, 0)), delta_spec,
         whole((8, width)), half_spec, whole((shard_len, width))],
        [row_shape,
         jax.ShapeDtypeStruct((2, length, cols), BF16),
         jax.ShapeDtypeStruct((2, 8, length), F32),
         jax.ShapeDtypeStruct((8, width), F32), half_shape(BF16),
         jax.ShapeDtypeStruct((shard_len, width), BF16)],
        flops=matmul * 2 * cols,
        nbytes=10_000_000,
    )(place, hidden_row, dy_row, second_part, second_came, ctx_mine, ctx_others,
      down_keep, down_came, tie(vectors, gu_send), o_mine, o_others)

    block_came = over_y(block_send)

    def attend_back(j, qkv, lse, segments):
        return call(
            functools.partial(attend_back_kernel, heads),
            (1,),
            [whole((length, qkv_cols)),
             pl.BlockSpec((None, length, cols), lambda i: (j, 0, 0)),
             whole((8, length)),
             pl.BlockSpec((None, 8, length), lambda i: (j, 0, 0)),
             whole((1, length))],
            [whole((length, qkv_cols)), whole((1, qkv_cols))],
            [jax.ShapeDtypeStruct((length, qkv_cols), BF16),
             jax.ShapeDtypeStruct((1, qkv_cols), F32)],
            scratch=[pltpu.VMEM((length, HEAD_DIM), F32), pltpu.VMEM((length, HEAD_DIM), F32)],
        )(qkv, grad_ctx, lse, delta, segments)

    dqkv_mine, sums_mine = attend_back(0, qkv_mine, lse_mine, seg_row)
    gu_came = tie(gu_came, dqkv_mine)
    mlp_last_send = jnp.stack([add_low(gu_keep, gu_came[1]), add_low(gd_keep, gd_came[1])], axis=1)
    mlp_last = mixed_one(mlp_last_send)
    dqkv_others, sums_others = attend_back(1, qkv_others, lse_others, tie(seg_row, mlp_last_send))
    ga_own, ga_send, ga_keep = attn_weight_grad(dqkv_mine, dqkv_others)
    ga_came = mixed_two(ga_send)
    mlp_last = tie(mlp_last, ga_send)
    gu_sum = total_of(gu_own, gu_came[0], mlp_last[:, 0])
    gd_sum = total_of(gd_own, gd_came[0], mlp_last[:, 1])

    def halves(total, b):
        size = total.shape[0] // 2
        total = total.reshape(size, 2, *total.shape[1:])
        high = ((widx >> b) & 1) == 1
        return (
            jnp.where(high, total[:, 1], total[:, 0]),
            jnp.where(high, total[:, 0], total[:, 1]),
        )

    gu_keep, gu_send = halves(gu_sum, 1)
    gd_keep, gd_send = halves(gd_sum, 1)
    mlp_came = over_wide(jnp.stack([gu_send, gd_send], axis=1).astype(BF16), 2)

    half_out = pl.BlockSpec((None, TILE, width), lambda t, p: (t // 2, 0, 0))
    one_keep, one_send, one_sums = placed(
        input_grad_kernel,
        (tiles,),
        [tile_spec] + [pl.BlockSpec((TILE, qkv_cols), lambda t, p: (t, 0))] * 2
        + [whole((width, qkv_cols))] * 2,
        [half_out] * 2 + [whole((8, width))],
        [half_shape(BF16)] * 2 + [jax.ShapeDtypeStruct((8, width), F32)],
        flops=matmul * 2 * qkv_cols,
        nbytes=8_000_000,
    )(tie(place, gu_sum, gd_sum, block_came), x_row, dqkv_mine, dqkv_others, w_mine, w_others)
    one_send, mlp_came, ga_came = lax.optimization_barrier((one_send, mlp_came, ga_came))
    ga_send = add_low(ga_keep, ga_came[1])
    ga_last = mixed_one(ga_send)
    mlp_parts = [
        keep + mlp_came[:, i].astype(F32) for i, keep in enumerate((gu_keep, gd_keep))
    ]
    mlp_sends = []
    for b in range(2, bits):
        split = [halves(part, b) for part in mlp_parts]
        mlp_sends = [send.astype(BF16) for _, send in split]
        mlp_came = over_wide(jnp.stack(mlp_sends, axis=1), 1 << b)
        mlp_parts = [(keep, mlp_came[:, i]) for i, (keep, _) in enumerate(split)]
        if b < bits - 1:
            mlp_parts = [keep + came.astype(F32) for keep, came in mlp_parts]

    one_came = over_core(one_send)

    def spread(mine, others, size):
        empty = jnp.zeros((size * narrow,), F32)
        empty = lax.dynamic_update_slice_in_dim(empty, mine, nidx * size, 0)
        return lax.dynamic_update_slice_in_dim(empty, others, other * size, 0)

    vec_part = jnp.concatenate(
        [
            one_sums[:2],
            jnp.where(first_core, mid_sums[:4], 0.0),
            spread(sums_mine[0, :cols], sums_others[0, :cols], cols)[None],
            spread(sums_mine[0, 2 * cols :], sums_others[0, 2 * cols :], cols)[None],
            spread(up_bias_sums[0], up_bias_sums[1], hidden).reshape(-1, width),
        ],
        axis=0,
    )

    vec_came = mixed_two(vec_part)

    own_block = pl.BlockSpec((TILE, width), lambda t, p: (2 * t + p[1], 0))
    half_in = pl.BlockSpec((None, TILE, width), lambda t, p: (t, 0, 0))
    grad_own, last_send = placed(
        final_kernel,
        (2,),
        [own_block, half_in, half_in, own_block, whole(vectors.shape)],
        [half_in, whole((shard_len, width))],
        [half_shape(F32), jax.ShapeDtypeStruct((shard_len, width), BF16)],
        nbytes=9_000_000,
    )(tie(place, vec_part, ga_send, *mlp_sends), x_row, one_keep, one_came, resid_low, vectors)

    vec_came, last_send = lax.optimization_barrier((vec_came, last_send))
    vec_grad = vec_part + vec_came
    vec_grad = vec_grad + mixed_one(vec_grad)
    last_came = over_y(last_send)

    vec_here = vec_grad
    for b in range(1, bits - 1):
        vec_here = vec_here + over_wide(vec_here, 1 << b)
    ga_last = tie(ga_last, vec_grad, *mlp_sends)
    ga_sum = total_of(ga_own, ga_came[0], ga_last)
    ga_sum, vec_here = lax.optimization_barrier((ga_sum, vec_here))
    ga_sum, came = scatter_upper(ga_sum)
    vec_here = tie(vec_here, came[0])
    vec_grad = vec_here + over_wide(vec_here, 1 << (bits - 1))
    vec_grad = vec_grad + over_core(vec_grad)
    mlp_total = jnp.concatenate(
        [keep + tie(last, came[-1]).astype(F32) for keep, last in mlp_parts], axis=0
    )
    attn_total = ga_sum[0]

    def home(own, came):
        return lax.dynamic_update_slice(own, came[None].astype(own.dtype), (1 - y, 0, 0))

    block_out = home(block_own, block_came)
    block_input_gradient = home(grad_own, last_came)

    attn_grad = jnp.stack([attn_total[:, i * cols : (i + 1) * cols] for i in range(4)])
    mlp_grad = mlp_total
    attn_new, attn_m_new, attn_v_new = adamw_update(
        attn_w, attn_m, attn_v, attn_grad, RATE_MATRIX, DECAY_MATRIX
    )
    mlp_new, mlp_m_new, mlp_v_new = adamw_update(
        mlp_w, mlp_m, mlp_v, mlp_grad, RATE_MATRIX, DECAY_MATRIX
    )
    vec_new, vec_m_new, vec_v_new = adamw_update(vectors, vec_m, vec_v, vec_grad, RATE_VECTOR, 0.0)
    return (
        block_out,
        block_input_gradient,
        attn_grad,
        attn_new,
        attn_m_new,
        attn_v_new,
        mlp_grad,
        mlp_new,
        mlp_m_new,
        mlp_v_new,
        vec_grad,
        vec_new,
        vec_m_new,
        vec_v_new,
    )


def solution(mesh):
    matrix = P(None, "wide", "narrow")
    rows = P("wide", "narrow", None)
    in_specs = (rows, P("wide", None), rows) + (matrix,) * 6 + (P(),) * 3
    out_specs = (rows, rows) + (matrix,) * 8 + (P(),) * 4
    return jax.shard_map(local, mesh=mesh, in_specs=in_specs, out_specs=out_specs, check_vma=False)
```

```python
import functools

import jax
import jax.numpy as jnp
from jax import lax
from jax.experimental import pallas as pl
from jax.experimental.pallas import tpu as pltpu
from jax.sharding import PartitionSpec as P

HEAD_DIM = 64
STEP = 10


EPS_NORM = 1e-06
MASKED_SCORE = -1e30
BETA_ONE = 0.5
BETA_TWO = 0.5
EPS_ADAM = 1e-08
RATE_MATRIX = 0.04
RATE_VECTOR = 0.3
DECAY_MATRIX = 0.05
SCALE = HEAD_DIM ** (-0.5)
TILE = 256
F32 = jnp.float32
BF16 = jnp.bfloat16
AXES = ("wide", "narrow")
COST_SCALE = 1
VMEM_LIMIT = 48 * 1024 * 1024


def adamw_update(weight, first_mom, second, gradient, step_rate, decay_rate):
    first_new = BETA_ONE * first_mom + (1.0 - BETA_ONE) * gradient
    second_new = BETA_TWO * second + (1.0 - BETA_TWO) * gradient * gradient
    corrected = (
        first_new
        / (1.0 - BETA_ONE**STEP)
        / (jnp.sqrt(second_new / (1.0 - BETA_TWO**STEP)) + EPS_ADAM)
    )
    return (weight - step_rate * (corrected + decay_rate * weight), first_new, second_new)


def nn(a, b):
    return lax.dot_general(a, b, (((1,), (0,)), ((), ())), preferred_element_type=F32)


def nt(a, b):
    return lax.dot_general(a, b, (((1,), (1,)), ((), ())), preferred_element_type=F32)


def tn(a, b):
    return lax.dot_general(a, b, (((0,), (0,)), ((), ())), preferred_element_type=F32)


def standardize(v):
    centred = v - jnp.mean(v, axis=-1, keepdims=True)
    inv = lax.rsqrt(jnp.mean(centred * centred, axis=-1, keepdims=True) + EPS_NORM)
    return centred * inv, inv


def norm_back(grad_out, normed, inv, gain):
    scaled = grad_out * gain
    return inv * (
        scaled
        - jnp.mean(scaled, axis=-1, keepdims=True)
        - normed * jnp.mean(scaled * normed, axis=-1, keepdims=True)
    )


def whole(shape):
    return pl.BlockSpec(shape, lambda *_: (0,) * len(shape))


def params(cost=None):
    return pltpu.CompilerParams(
        dimension_semantics=("arbitrary",), vmem_limit_bytes=VMEM_LIMIT
    )


def call(kernel, grid, in_specs, out_specs, out_shape, scratch=(), flops=0, nbytes=0, trans=0):
    return pl.pallas_call(
        kernel,
        grid=grid,
        in_specs=in_specs,
        out_specs=out_specs,
        out_shape=out_shape,
        scratch_shapes=scratch,
        compiler_params=params(),
        cost_estimate=pl.CostEstimate(
            flops=flops // COST_SCALE,
            bytes_accessed=nbytes // COST_SCALE,
            transcendentals=trans // COST_SCALE,
        ),
    )


def placed(kernel, grid, in_specs, out_specs, out_shape, scratch=(), flops=0, nbytes=0, trans=0):
    return pl.pallas_call(
        kernel,
        grid_spec=pltpu.PrefetchScalarGridSpec(
            num_scalar_prefetch=1,
            grid=grid,
            in_specs=in_specs,
            out_specs=out_specs,
            scratch_shapes=scratch,
        ),
        out_shape=out_shape,
        compiler_params=params(),
        cost_estimate=pl.CostEstimate(
            flops=flops // COST_SCALE,
            bytes_accessed=nbytes // COST_SCALE,
            transcendentals=trans // COST_SCALE,
        ),
    )


def head_columns(h, heads):
    return tuple((kind * heads + h) * HEAD_DIM for kind in range(3))


def block_rows(place_ref, near_ref, far_ref, store):
    even = place_ref[0] == 0
    upper = place_ref[3]
    count, rows, _ = near_ref.shape
    for u in range(count):
        src = lax.bitwise_xor(upper, jnp.int32(u))
        for x in range(2):
            at = slice((2 * u + x) * rows, (2 * u + x + 1) * rows)
            same = even if x == 0 else jnp.logical_not(even)
            store(at, jnp.where(same, near_ref[src], far_ref[src]))


def natural(place_ref, pieces, targets):
    held_ref, from_x_ref, from_y_ref, diagonal_ref = pieces
    block_rows(place_ref, held_ref, from_x_ref, functools.partial(targets, 0))
    block_rows(place_ref, from_y_ref, diagonal_ref, functools.partial(targets, 1))


def pick_row(place_ref, tile, part, refs):
    keep_ref, came_ref, keep_core_ref, came_core_ref = refs
    same_y = tile // 2 == place_ref[2]
    same_core = tile % 2 == place_ref[1]
    return jnp.where(
        same_y,
        jnp.where(same_core, keep_ref[part], keep_core_ref[part]),
        jnp.where(same_core, came_ref[part], came_core_ref[part]),
    )


def project(place_ref, near_ref, far_ref, low, bias_ref, qkv_ref, w_ref, o_ref):
    cols = w_ref.shape[1]

    @pl.when(pl.program_id(0) == 0)
    def _():
        def store(at, value):
            w_ref[at] = value[:, :cols]
            o_ref[at] = value[:, cols:]

        block_rows(place_ref, near_ref, far_ref, store)

    qkv_ref[...] = (nn(low, w_ref[...]) + bias_ref[...]).astype(BF16)


def first_qkv_kernel(place_ref, *refs):
    rows = refs[:4]
    near_ref, far_ref, vec_ref, bias_ref, x_ref, dy_ref, a_ref, *outs = refs[4:]
    x = pick_row(place_ref, pl.program_id(0), 0, rows)
    x_ref[...] = x
    dy_ref[...] = pick_row(place_ref, pl.program_id(0), 1, rows)
    normed, _ = standardize(x.astype(F32))
    low = (normed * vec_ref[0:1] + vec_ref[1:2]).astype(BF16)
    a_ref[...] = low
    project(place_ref, near_ref, far_ref, low, bias_ref, *outs)


def second_qkv_kernel(place_ref, a_ref, near_ref, far_ref, bias_ref, *outs):
    project(place_ref, near_ref, far_ref, a_ref[...], bias_ref, *outs)


def column(row):
    return jnp.broadcast_to(row, (128, row.shape[1])).T[:, :1]


def attend_kernel(last, qkv_q_ref, qkv_ref, seg_tile_ref, seg_row_ref, *refs):
    if last:
        ctx_in_ref, o0_ref, o1_ref, ctx_ref, lse_ref, out_ref = refs
    else:
        ctx_ref, lse_ref = refs
    cols = ctx_ref.shape[1]
    heads = cols // HEAD_DIM
    same = column(seg_tile_ref[...]) == seg_row_ref[...]
    lane = lax.broadcasted_iota(jnp.int32, (TILE, 128), 1)
    totals = jnp.zeros((TILE, 128), F32)
    for h in range(heads):
        lo = h * HEAD_DIM
        at_q, at_k, at_v = head_columns(h, heads)
        q = qkv_q_ref[:, at_q : at_q + HEAD_DIM]
        k = qkv_ref[:, at_k : at_k + HEAD_DIM]
        v = qkv_ref[:, at_v : at_v + HEAD_DIM]
        s = jnp.where(same, nt(q, k) * SCALE, MASKED_SCORE)
        top = jnp.max(s, axis=-1, keepdims=True)
        e = jnp.exp(s - top)
        total = jnp.sum(e, axis=-1, keepdims=True)
        o = nn(e.astype(BF16), v) / total
        ctx_ref[:, lo : lo + HEAD_DIM] = o.astype(BF16)
        totals = jnp.where(lane == h, top + jnp.log(total), totals)
    lse_ref[...] = totals.T[: lse_ref.shape[0]]
    if last:
        out_ref[...] = (nt(ctx_in_ref[...], o0_ref[...]) + nt(ctx_ref[...], o1_ref[...])).astype(BF16)


def sort_grad(place_ref, mine, others, own_ref, send_ref, keep_ref, at):
    even = place_ref[0] == 0
    first = place_ref[1] == 0
    rows = own_ref.shape[1]
    for u in range(own_ref.shape[0]):
        lo = slice(2 * u * rows, (2 * u + 1) * rows)
        hi = slice((2 * u + 1) * rows, (2 * u + 2) * rows)
        own_ref[u, :, at] = jnp.where(even, mine[lo], mine[hi])
        to_x = jnp.where(even, mine[hi], mine[lo])
        to_y = jnp.where(even, others[lo], others[hi])
        send_ref[0, u, :, at] = jnp.where(first, to_y, to_x)
        keep_ref[u, :, at] = jnp.where(first, to_x, to_y)
        send_ref[1, u, :, at] = jnp.where(even, others[hi], others[lo])


def add_grad(total_ref, j, left, right):
    part = tn(left, right)

    @pl.when(pl.program_id(0) == 0)
    def _():
        total_ref[j] = part

    @pl.when(pl.program_id(0) > 0)
    def _():
        total_ref[j] += part


def up_kernel(place_ref, x_ref, p0_ref, p1_ref, dy_ref, vec_ref, bu_ref, *refs):
    pieces = refs[:4]
    (a_ref, h_ref, z_ref, slope_ref,
     g_own_ref, g_send_ref, g_keep_ref, total_ref, u0_ref, u1_ref) = refs[4:]
    tile = pl.program_id(0)

    @pl.when(tile == 0)
    def _():
        def store(j, at, value):
            (u0_ref, u1_ref)[j][at] = value

        natural(place_ref, pieces, store)

    h = x_ref[...].astype(F32) + (p0_ref[...].astype(F32) + p1_ref[...].astype(F32)) + vec_ref[4:5]

    h_ref[...] = h.astype(BF16)
    normed, _ = standardize(h)
    a = (normed * vec_ref[2:3] + vec_ref[3:4]).astype(BF16)
    a_ref[...] = a
    dy = dy_ref[...]
    for j, u_ref in enumerate((u0_ref, u1_ref)):
        u = nn(a, u_ref[...]) + bu_ref[j : j + 1]
        cdf = 0.5 + 0.5 * lax.erf(u * 0.7071067811865476)
        z = (u * cdf).astype(BF16)
        z_ref[j] = z
        slope_ref[j] = (cdf + u * (0.3989422804014327 * jnp.exp(-0.5 * u * u))).astype(BF16)
        add_grad(total_ref, j, dy, z)

    @pl.when(tile == pl.num_programs(0) - 1)
    def _():
        sort_grad(place_ref, total_ref[0].astype(BF16), total_ref[1].astype(BF16),
                  g_own_ref, g_send_ref, g_keep_ref, slice(None))


def down_kernel(place_ref, dy_ref, z_ref, slope_ref, *refs):
    up_pieces = refs[:4]
    pieces = refs[4:8]
    du_ref, keep_ref, send_ref, da_ref, gbu_ref, d0_ref, d1_ref, u0_ref, u1_ref = refs[8:]
    tile = pl.program_id(0)

    @pl.when(tile == 0)
    def _():
        gbu_ref[...] = jnp.zeros_like(gbu_ref)

        def store_up(j, at, value):
            (u0_ref, u1_ref)[j][at] = value

        def store(j, at, value):
            (d0_ref, d1_ref)[j][at] = value

        natural(place_ref, up_pieces, store_up)
        natural(place_ref, pieces, store)

    dy = dy_ref[...]
    down = jnp.zeros(da_ref.shape, F32)
    da = jnp.zeros(da_ref.shape, F32)
    for j, (u_ref, d_ref) in enumerate(((u0_ref, d0_ref), (u1_ref, d1_ref))):
        du = (nn(dy, d_ref[...]) * slope_ref[j].astype(F32)).astype(BF16)
        du_ref[j] = du
        gbu_ref[j : j + 1] += jnp.sum(du.astype(F32), axis=0, keepdims=True)
        down += nt(z_ref[j], d_ref[...])
        da += nt(du, u_ref[...])
    da_ref[...] = da.astype(BF16)
    down = down.astype(BF16)
    mine = tile % 2 == place_ref[1]

    @pl.when(mine)
    def _():
        keep_ref[...] = down

    @pl.when(jnp.logical_not(mine))
    def _():
        send_ref[...] = down


def grad_kernel(place_ref, left_ref, right_ref, own_ref, send_ref, keep_ref, turned_ref):
    @pl.when(pl.program_id(0) == 0)
    def _():
        turned_ref[...] = left_ref[...].T

    turned = turned_ref[...]
    mine = nn(turned, right_ref[0]).astype(BF16)
    others = nn(turned, right_ref[1]).astype(BF16)
    sort_grad(place_ref, mine, others, own_ref, send_ref, keep_ref, slice(None))


def two_grads_kernel(place_ref, left_ref, dh_ref, dqkv0_ref, dqkv1_ref, ctx0_ref, ctx1_ref,
                     own_ref, send_ref, keep_ref):
    many = dqkv0_ref.shape[1]
    turned = left_ref[...].T
    mine = nn(turned, dqkv0_ref[...]).astype(BF16)
    others = nn(turned, dqkv1_ref[...]).astype(BF16)
    sort_grad(place_ref, mine, others, own_ref, send_ref, keep_ref, slice(0, many))
    turned = dh_ref[...].T
    mine = nn(turned, ctx0_ref[...]).astype(BF16)
    others = nn(turned, ctx1_ref[...]).astype(BF16)
    sort_grad(place_ref, mine, others, own_ref, send_ref, keep_ref, slice(many, None))


def mid_kernel(place_ref, h_ref, dy_ref, da0_ref, da1_ref, ctx0_ref, ctx1_ref, keep_ref, came_ref,
               vec_ref, o0_ref, o1_ref, dh_ref, dctx_ref, delta_ref, sums_ref, out_ref, send_ref):
    tile = pl.program_id(0)

    @pl.when(tile % 2 == place_ref[1])
    def _():
        out = h_ref[...].astype(F32) + (keep_ref[...].astype(F32) + came_ref[...].astype(F32))
        out = (out + vec_ref[5:6]).astype(BF16)
        out_ref[...] = out

        @pl.when(tile // 2 != place_ref[2])
        def _():
            send_ref[...] = out

    @pl.when(pl.program_id(0) == 0)
    def _():
        sums_ref[...] = jnp.zeros_like(sums_ref)

    normed, inv = standardize(h_ref[...].astype(F32))
    da = da0_ref[...].astype(F32) + da1_ref[...].astype(F32)
    dy = dy_ref[...].astype(F32)
    dh = dy + norm_back(da, normed, inv, vec_ref[2:3])
    low = dh.astype(BF16)
    dh_ref[...] = low
    sums_ref[0:1] += jnp.sum(da * normed, axis=0, keepdims=True)
    sums_ref[1:2] += jnp.sum(da, axis=0, keepdims=True)
    sums_ref[2:3] += jnp.sum(dh, axis=0, keepdims=True)
    sums_ref[3:4] += jnp.sum(dy, axis=0, keepdims=True)
    cols = ctx0_ref.shape[1]
    head = lax.broadcasted_iota(jnp.int32, (8, cols), 0)
    owner = lax.broadcasted_iota(jnp.int32, (8, cols), 1) // HEAD_DIM
    member = jnp.where(head == owner, 1.0, 0.0).astype(BF16)
    for j, (o_ref, ctx_ref) in enumerate(((o0_ref, ctx0_ref), (o1_ref, ctx1_ref))):
        dctx = nn(low, o_ref[...]).astype(BF16)
        dctx_ref[j] = dctx
        prod = dctx.astype(F32) * ctx_ref[...].astype(F32)
        high = prod.astype(BF16)
        rest = (prod - high.astype(F32)).astype(BF16)
        delta_ref[j] = nt(member, high) + nt(member, rest)


def attend_back_kernel(heads, qkv_ref, dctx_ref, lse_ref, delta_ref, seg_row_ref,
                       dqkv_ref, sums_ref, dk_ref, dv_ref):
    length = qkv_ref.shape[0]
    seg_col = column(seg_row_ref[...])
    for h in range(heads):
        lo = h * HEAD_DIM
        at_q, at_k, at_v = head_columns(h, heads)
        k = qkv_ref[:, at_k : at_k + HEAD_DIM]
        v = qkv_ref[:, at_v : at_v + HEAD_DIM]
        for t in range(length // TILE):
            rows = slice(t * TILE, (t + 1) * TILE)
            q = qkv_ref[rows, at_q : at_q + HEAD_DIM]
            dc = dctx_ref[rows, lo : lo + HEAD_DIM]
            same = seg_col == seg_row_ref[:, rows]
            s = jnp.where(same, nt(k, q) * SCALE, MASKED_SCORE)
            p = jnp.exp(s - lse_ref[h : h + 1, rows])
            ds = (p * (nt(v, dc) - delta_ref[h : h + 1, rows])).astype(BF16)
            dv = nn(p.astype(BF16), dc)
            dk = nn(ds, q)
            if t == 0:
                dv_ref[...] = dv
                dk_ref[...] = dk
            else:
                dv_ref[...] += dv
                dk_ref[...] += dk
            dqkv_ref[rows, at_q : at_q + HEAD_DIM] = (tn(ds, k) * SCALE).astype(BF16)
        dqkv_ref[:, at_k : at_k + HEAD_DIM] = (dk_ref[...] * SCALE).astype(BF16)
        dqkv_ref[:, at_v : at_v + HEAD_DIM] = dv_ref[...].astype(BF16)
    sums_ref[...] = jnp.sum(dqkv_ref[...].astype(F32), axis=0, keepdims=True)


def input_grad_kernel(place_ref, x_ref, g0_ref, g1_ref, w0_ref, w1_ref, keep_ref, send_ref,
                      sums_ref):
    tile = pl.program_id(0)

    @pl.when(tile == 0)
    def _():
        sums_ref[...] = jnp.zeros_like(sums_ref)

    out = nt(g0_ref[...], w0_ref[...]) + nt(g1_ref[...], w1_ref[...])
    normed, _ = standardize(x_ref[...].astype(F32))
    sums_ref[0:1] += jnp.sum(out * normed, axis=0, keepdims=True)
    sums_ref[1:2] += jnp.sum(out, axis=0, keepdims=True)
    out = out.astype(BF16)
    mine = tile % 2 == place_ref[1]

    @pl.when(mine)
    def _():
        keep_ref[...] = out

    @pl.when(jnp.logical_not(mine))
    def _():
        send_ref[...] = out


def final_kernel(place_ref, x_ref, da0_ref, da1_ref, dh_ref, vec_ref, dx_ref, send_ref):
    normed, inv = standardize(x_ref[...].astype(F32))
    da = da0_ref[...].astype(F32) + da1_ref[...].astype(F32)
    dx = dh_ref[...].astype(F32) + norm_back(da, normed, inv, vec_ref[0:1])
    dx_ref[...] = dx

    @pl.when(pl.program_id(0) != place_ref[2])
    def _():
        send_ref[...] = dx.astype(BF16)


def local(
    tokens,
    segment_ids,
    cotangent,
    attn_w,
    attn_m,
    attn_v,
    mlp_w,
    mlp_m,
    mlp_v,
    vectors,
    vec_m,
    vec_v,
):
    wide = lax.axis_size("wide")
    narrow = lax.axis_size("narrow")
    widx = lax.axis_index("wide")
    nidx = lax.axis_index("narrow")
    y = nidx // 2
    c = nidx % 2
    other = (1 - y) * 2 + c
    xbit = widx % 2
    even = xbit == 0
    first_core = c == 0
    first_y = y == 0
    _, shard_len, width = tokens.shape
    length = segment_ids.shape[1]
    cols = attn_w.shape[2]
    rows = attn_w.shape[1]
    hidden = mlp_w.shape[2]
    heads = cols // HEAD_DIM
    bits = wide.bit_length() - 1
    upper = wide // 2
    steps = [(b, min(2, bits - b)) for b in range(1, bits, 2)]

    def swap(value, partner):
        pairs = [
            (w * narrow + n, (lambda t: t[0] * narrow + t[1])(partner(w, n)))
            for w in range(wide)
            for n in range(narrow)
        ]
        return lax.ppermute(value, AXES, pairs)

    def over_core(value):
        return swap(value, lambda w, n: (w, n ^ 1))

    def over_y(value):
        return swap(value, lambda w, n: (w, n ^ 2))

    def over_x(value):
        return swap(value, lambda w, n: (w ^ 1, n))

    def over_wide(value, mask):
        return swap(value, lambda w, n: (w ^ mask, n))

    def mixed_one(value):
        return swap(value, lambda w, n: (w ^ 1, n) if n % 2 == 0 else (w, n ^ 2))

    def mixed_two(value):
        return swap(value, lambda w, n: (w ^ 1, n) if n % 2 == 1 else (w, n ^ 2))

    def tie(value, *deps):
        return lax.optimization_barrier((value, *deps))[0]

    def pair(flag, first, second, axis):
        return jnp.stack(
            [jnp.where(flag, first, second), jnp.where(flag, second, first)], axis=axis
        )

    def add_low(keep, came):
        return (keep.astype(F32) + came.astype(F32)).astype(BF16)

    def total_of(own, came, last):
        return own.astype(F32) + came.astype(F32) + last.astype(F32)

    def choose(index, values):
        picked = values[0]
        for i in range(1, len(values)):
            picked = jnp.where(index == i, values[i], picked)
        return picked

    def gather_upper(shard):
        held = shard[None]
        for b, count in steps:
            came = [over_wide(held, k << b) for k in range(1, 1 << count)]
            held = jnp.concatenate([held, *came], axis=0)
        return held

    def scatter_upper(total):
        for b, count in reversed(steps):
            size = total.shape[0] >> count
            digit = (widx >> b) & ((1 << count) - 1)
            blocks = [total[i * size : (i + 1) * size] for i in range(1 << count)]
            came = []
            for k in range(1, 1 << count):
                send = choose(digit, [blocks[i ^ k] for i in range(1 << count)])
                came.append(over_wide(send.astype(BF16), k << b))
            total = choose(digit, blocks).astype(F32)
            for each in came:
                total = total + each.astype(F32)
        return total, came

    def both(vector, size):
        return jnp.stack(
            [
                lax.dynamic_slice_in_dim(vector, nidx * size, size),
                lax.dynamic_slice_in_dim(vector, other * size, size),
            ]
        )

    tiles = length // TILE
    tile_spec = pl.BlockSpec((TILE, width), lambda t, *_: (t, 0))
    qkv_cols = 3 * cols
    matmul = 2 * length * width
    row_shape = jax.ShapeDtypeStruct((length, width), BF16)
    zero = jnp.int32(0)
    place = jnp.stack([xbit, c, y, widx // 2, zero, zero, zero, zero]).astype(jnp.int32)

    def spread_over_plane(held):
        from_x = over_x(held)
        from_y = over_y(held)
        return from_x, from_y

    def turn(from_x, from_y):
        return jnp.where(first_core, from_x, from_y)

    attn_low = attn_w.astype(BF16)
    attn_shard = jnp.concatenate([attn_low[i] for i in range(4)], axis=-1)

    mlp_low = mlp_w.astype(BF16)
    a_held = gather_upper(attn_shard)

    def row_pair(first):
        return jnp.stack(
            [jnp.where(first, v[0], v[1]) for v in (tokens, cotangent)]
        )

    rows_send = row_pair(jnp.logical_not(first_y))
    rows_came = over_y(tie(rows_send, attn_shard))
    rows_keep = row_pair(first_y)
    rows_keep_core = over_core(rows_keep)

    a_held, rows_came = lax.optimization_barrier((a_held, rows_came))
    a_x, a_y = spread_over_plane(a_held)
    rows_came_core = over_core(rows_came)
    u_held = gather_upper(tie(mlp_low[0], a_held, rows_came_core, rows_keep_core))
    query_bias = both(vectors[6], cols)
    value_bias = both(vectors[7], cols)
    no_bias = jnp.zeros_like(query_bias)
    qkv_bias = jnp.concatenate([query_bias, no_bias, value_bias], axis=1)
    up_bias = both(vectors[8:].reshape(-1), hidden)

    a_turn = turn(*lax.optimization_barrier((a_x, a_y, rows_came_core, rows_keep_core, qkv_bias, up_bias))[:2])
    a_diagonal = mixed_two(a_turn)
    u_x, u_y = None, None
    d_first = mlp_low[1][None]

    seg_own = lax.dynamic_index_in_dim(segment_ids, y, 0, False)
    seg_row = seg_own[None, :]
    part_spec = whole((2, shard_len, width))
    piece_spec = whole((upper, rows, width))
    qkv_shape = jax.ShapeDtypeStruct((length, qkv_cols), BF16)
    qkv_spec = pl.BlockSpec((TILE, qkv_cols), lambda t, *_: (t, 0))
    block_shapes = [
        qkv_shape,
        jax.ShapeDtypeStruct((width, qkv_cols), BF16),
        jax.ShapeDtypeStruct((width, cols), BF16),
    ]
    block_specs = [qkv_spec, whole((width, qkv_cols)), whole((width, cols))]
    x_row, dy_row, normed_low, qkv_mine, w_mine, o_mine = placed(
        first_qkv_kernel,
        (tiles,),
        [part_spec] * 4 + [piece_spec] * 2 + [whole(vectors.shape), whole((1, qkv_cols))],
        [tile_spec] * 3 + block_specs,
        [row_shape] * 3 + block_shapes,
    )(tie(place, a_turn), rows_keep, rows_came, rows_keep_core, rows_came_core, a_held, a_x,
      vectors, qkv_bias[0:1])

    d_first_came = over_wide(tie(d_first, a_turn), 2)
    d_first, d_first_came = lax.optimization_barrier((d_first, d_first_came, qkv_mine))[:2]
    d_second = jnp.concatenate([d_first, d_first_came], axis=0)
    d_second_came = over_wide(d_second, 4)
    u_x, u_y = spread_over_plane(tie(u_held, qkv_mine, d_first_came))
    ctx_spec = pl.BlockSpec((TILE, cols), lambda t, *_: (t, 0))
    lse_spec = pl.BlockSpec((8, TILE), lambda t: (0, t))
    ctx_shape = jax.ShapeDtypeStruct((length, cols), BF16)
    lse_shape = jax.ShapeDtypeStruct((8, length), F32)
    o_spec = whole((width, cols))

    def attend(qkv, segments, extra):
        last = bool(extra)
        in_specs = [
            qkv_spec,
            whole((length, qkv_cols)),
            pl.BlockSpec((1, TILE), lambda t: (0, t)),
            whole((1, length)),
        ]
        out_specs = [ctx_spec, lse_spec]
        out_shape = [ctx_shape, lse_shape]
        if last:
            in_specs += [ctx_spec, o_spec, o_spec]
            out_specs += [tile_spec]
            out_shape += [row_shape]
        return call(
            functools.partial(attend_kernel, last),
            (tiles,),
            in_specs,
            out_specs,
            out_shape,
            flops=4 * length * length * cols if last else 0,
        )(qkv, qkv, segments, segments, *extra)

    ctx_mine, lse_mine = attend(qkv_mine, tie(seg_row, d_second), ())
    a_y, a_diagonal = lax.optimization_barrier((a_y, a_diagonal, ctx_mine))[:2]
    qkv_others, w_others, o_others = placed(
        second_qkv_kernel,
        (tiles,),
        [tile_spec] + [piece_spec] * 2 + [whole((1, qkv_cols))],
        block_specs,
        block_shapes,
    )(place, normed_low, a_y, a_diagonal, qkv_bias[1:2])
    u_turn = turn(*lax.optimization_barrier((u_x, u_y, qkv_others))[:2])
    u_diagonal = mixed_two(u_turn)
    d_second, d_second_came = lax.optimization_barrier((d_second, d_second_came, qkv_others))[:2]
    d_second = jnp.concatenate([d_second, d_second_came], axis=0)

    def gather_rest(held):
        for b in range(3, bits):
            held = jnp.concatenate([held, over_wide(held, 1 << b)], axis=0)
        return held

    d_held = d_second if bits == 3 else gather_rest(d_second)
    ctx_others, lse_others, out_part = attend(
        qkv_others, tie(seg_row, u_turn, d_held), (ctx_mine, o_mine, o_others)
    )
    out_part, u_diagonal = lax.optimization_barrier((out_part, u_diagonal))
    out_came = over_core(out_part)
    d_x, d_y = spread_over_plane(tie(d_held, u_turn))
    d_diagonal = swap(tie(d_held, u_turn), lambda w, n: (w ^ 1, n ^ 2))

    pair_spec = pl.BlockSpec((2, TILE, hidden), lambda t, *_: (0, t, 0))
    pair_shape = jax.ShapeDtypeStruct((2, length, hidden), BF16)
    half_spec = pl.BlockSpec((None, TILE, width), lambda t, *_: (t // 2, 0, 0))

    def half_shape(dtype):
        return jax.ShapeDtypeStruct((2, shard_len, width), dtype)

    grad_specs = [piece_spec, whole((2, upper, rows, width)), piece_spec]
    grad_shapes = [
        jax.ShapeDtypeStruct((upper, rows, hidden), BF16),
        jax.ShapeDtypeStruct((2, upper, rows, hidden), BF16),
        jax.ShapeDtypeStruct((upper, rows, hidden), BF16),
    ]
    (second_low, hidden_row, activated, slope,
     gd_own, gd_send, gd_keep) = placed(
        up_kernel,
        (tiles,),
        [tile_spec] * 4 + [whole(vectors.shape), whole((2, hidden))] + [piece_spec] * 4,
        [tile_spec, tile_spec, pair_spec, pair_spec] + grad_specs,
        [row_shape, row_shape, pair_shape, pair_shape] + grad_shapes,
        scratch=[pltpu.VMEM((2, width, hidden), F32)] + [pltpu.VMEM((width, hidden), BF16)] * 2,
        flops=2 * matmul * 2 * hidden,
        nbytes=20_000_000,
        trans=4 * length * hidden,
    )(place, x_row, out_part, out_came, dy_row, vectors, up_bias, u_held, u_x, u_y, u_diagonal)
    gd_came = mixed_two(gd_send)

    def weight_grad(where, left, right, block):
        spec = pl.BlockSpec((upper, rows, block), lambda i, p: (0, 0, i))
        return placed(
            grad_kernel,
            (hidden // block,),
            [whole((length, width)), pl.BlockSpec((2, length, block), lambda i, p: (0, 0, i))],
            [spec, pl.BlockSpec((2, upper, rows, block), lambda i, p: (0, 0, 0, i)), spec],
            grad_shapes,
            scratch=[pltpu.VMEM((width, length), BF16)],
            flops=matmul * 2 * hidden,
            nbytes=8_000_000,
        )(where, left, right)

    def attn_weight_grad(dqkv_first, dqkv_second):
        part = width // 2
        left = pl.BlockSpec((length, part), lambda i, p: (0, i))
        spec = pl.BlockSpec((upper // 2, rows, width), lambda i, p: (i, 0, 0))
        return placed(
            two_grads_kernel,
            (2,),
            [left] * 2 + [whole((length, qkv_cols))] * 2 + [whole((length, cols))] * 2,
            [spec, pl.BlockSpec((2, upper // 2, rows, width), lambda i, p: (0, i, 0, 0)), spec],
            grad_shapes,
        )(place, normed_low, resid_low, dqkv_first, dqkv_second, ctx_mine, ctx_others)

    grad_pre, down_keep, down_send, second_part, up_bias_sums = placed(
        down_kernel,
        (tiles,),
        [tile_spec, pair_spec, pair_spec] + [piece_spec] * 8,
        [pair_spec, half_spec, half_spec, tile_spec, whole((2, hidden))],
        [pair_shape, half_shape(BF16), half_shape(BF16), row_shape,
         jax.ShapeDtypeStruct((2, hidden), F32)],
        scratch=[pltpu.VMEM((width, hidden), BF16)] * 4,
        flops=3 * matmul * 2 * hidden,
        nbytes=20_000_000,
    )(tie(place, gd_send), dy_row, activated, slope, u_held, u_x, u_y, u_diagonal, d_held, d_x,
      d_y, d_diagonal)
    second_part, gd_came = lax.optimization_barrier((second_part, gd_came))

    down_came = over_core(down_send)
    second_came = over_core(second_part)
    gu_own, gu_send, gu_keep = weight_grad(
        tie(place, second_part), second_low, grad_pre, 256
    )
    gu_send, down_came = lax.optimization_barrier((gu_send, down_came))
    gu_came = mixed_two(gu_send)

    delta_spec = pl.BlockSpec((2, 8, TILE), lambda t, *_: (0, 0, t))
    resid_low, grad_ctx, delta, mid_sums, block_own, block_send = placed(
        mid_kernel,
        (tiles,),
        [tile_spec] * 4
        + [ctx_spec, ctx_spec, half_spec, half_spec, whole(vectors.shape), o_spec, o_spec],
        [tile_spec, pl.BlockSpec((2, TILE, cols), lambda t, *_: (0, t, 0)), delta_spec,
         whole((8, width)), half_spec, whole((shard_len, width))],
        [row_shape,
         jax.ShapeDtypeStruct((2, length, cols), BF16),
         jax.ShapeDtypeStruct((2, 8, length), F32),
         jax.ShapeDtypeStruct((8, width), F32), half_shape(BF16),
         jax.ShapeDtypeStruct((shard_len, width), BF16)],
        flops=matmul * 2 * cols,
        nbytes=10_000_000,
    )(place, hidden_row, dy_row, second_part, second_came, ctx_mine, ctx_others,
      down_keep, down_came, tie(vectors, gu_send), o_mine, o_others)

    block_came = over_y(block_send)

    def attend_back(j, qkv, lse, segments):
        return call(
            functools.partial(attend_back_kernel, heads),
            (1,),
            [whole((length, qkv_cols)),
             pl.BlockSpec((None, length, cols), lambda i: (j, 0, 0)),
             whole((8, length)),
             pl.BlockSpec((None, 8, length), lambda i: (j, 0, 0)),
             whole((1, length))],
            [whole((length, qkv_cols)), whole((1, qkv_cols))],
            [jax.ShapeDtypeStruct((length, qkv_cols), BF16),
             jax.ShapeDtypeStruct((1, qkv_cols), F32)],
            scratch=[pltpu.VMEM((length, HEAD_DIM), F32), pltpu.VMEM((length, HEAD_DIM), F32)],
        )(qkv, grad_ctx, lse, delta, segments)

    dqkv_mine, sums_mine = attend_back(0, qkv_mine, lse_mine, seg_row)
    gu_came = tie(gu_came, dqkv_mine)
    mlp_last_send = jnp.stack([add_low(gu_keep, gu_came[1]), add_low(gd_keep, gd_came[1])], axis=1)
    mlp_last = mixed_one(mlp_last_send)
    dqkv_others, sums_others = attend_back(1, qkv_others, lse_others, tie(seg_row, mlp_last_send))
    ga_own, ga_send, ga_keep = attn_weight_grad(dqkv_mine, dqkv_others)
    ga_came = mixed_two(ga_send)
    mlp_last = tie(mlp_last, ga_send)
    gu_sum = total_of(gu_own, gu_came[0], mlp_last[:, 0])
    gd_sum = total_of(gd_own, gd_came[0], mlp_last[:, 1])

    def halves(total, b):
        size = total.shape[0] // 2
        total = total.reshape(size, 2, *total.shape[1:])
        high = ((widx >> b) & 1) == 1
        return (
            jnp.where(high, total[:, 1], total[:, 0]),
            jnp.where(high, total[:, 0], total[:, 1]),
        )

    gu_keep, gu_send = halves(gu_sum, 1)
    gd_keep, gd_send = halves(gd_sum, 1)
    mlp_came = over_wide(jnp.stack([gu_send, gd_send], axis=1).astype(BF16), 2)

    half_out = pl.BlockSpec((None, TILE, width), lambda t, p: (t // 2, 0, 0))
    one_keep, one_send, one_sums = placed(
        input_grad_kernel,
        (tiles,),
        [tile_spec] + [pl.BlockSpec((TILE, qkv_cols), lambda t, p: (t, 0))] * 2
        + [whole((width, qkv_cols))] * 2,
        [half_out] * 2 + [whole((8, width))],
        [half_shape(BF16)] * 2 + [jax.ShapeDtypeStruct((8, width), F32)],
        flops=matmul * 2 * qkv_cols,
        nbytes=8_000_000,
    )(tie(place, gu_sum, gd_sum, block_came), x_row, dqkv_mine, dqkv_others, w_mine, w_others)
    one_send, mlp_came, ga_came = lax.optimization_barrier((one_send, mlp_came, ga_came))
    ga_send = add_low(ga_keep, ga_came[1])
    ga_last = mixed_one(ga_send)
    mlp_parts = [
        keep + mlp_came[:, i].astype(F32) for i, keep in enumerate((gu_keep, gd_keep))
    ]
    mlp_sends = []
    for b in range(2, bits):
        split = [halves(part, b) for part in mlp_parts]
        mlp_sends = [send.astype(BF16) for _, send in split]
        mlp_came = over_wide(jnp.stack(mlp_sends, axis=1), 1 << b)
        mlp_parts = [(keep, mlp_came[:, i]) for i, (keep, _) in enumerate(split)]
        if b < bits - 1:
            mlp_parts = [keep + came.astype(F32) for keep, came in mlp_parts]

    one_came = over_core(one_send)

    def spread(mine, others, size):
        empty = jnp.zeros((size * narrow,), F32)
        empty = lax.dynamic_update_slice_in_dim(empty, mine, nidx * size, 0)
        return lax.dynamic_update_slice_in_dim(empty, others, other * size, 0)

    vec_part = jnp.concatenate(
        [
            one_sums[:2],
            jnp.where(first_core, mid_sums[:4], 0.0),
            spread(sums_mine[0, :cols], sums_others[0, :cols], cols)[None],
            spread(sums_mine[0, 2 * cols :], sums_others[0, 2 * cols :], cols)[None],
            spread(up_bias_sums[0], up_bias_sums[1], hidden).reshape(-1, width),
        ],
        axis=0,
    )

    vec_came = mixed_two(vec_part)

    own_block = pl.BlockSpec((TILE, width), lambda t, p: (2 * t + p[1], 0))
    half_in = pl.BlockSpec((None, TILE, width), lambda t, p: (t, 0, 0))
    grad_own, last_send = placed(
        final_kernel,
        (2,),
        [own_block, half_in, half_in, own_block, whole(vectors.shape)],
        [half_in, whole((shard_len, width))],
        [half_shape(F32), jax.ShapeDtypeStruct((shard_len, width), BF16)],
        nbytes=9_000_000,
    )(tie(place, vec_part, ga_send, *mlp_sends), x_row, one_keep, one_came, resid_low, vectors)

    vec_came, last_send = lax.optimization_barrier((vec_came, last_send))
    vec_grad = vec_part + vec_came
    vec_grad = vec_grad + mixed_one(vec_grad)
    last_came = over_y(last_send)

    vec_here = vec_grad
    for b in range(1, bits - 1):
        vec_here = vec_here + over_wide(vec_here, 1 << b)
    ga_last = tie(ga_last, vec_grad, *mlp_sends)
    ga_sum = total_of(ga_own, ga_came[0], ga_last)
    ga_sum, vec_here = lax.optimization_barrier((ga_sum, vec_here))
    ga_sum, came = scatter_upper(ga_sum)
    vec_here = tie(vec_here, came[0])
    vec_grad = vec_here + over_wide(vec_here, 1 << (bits - 1))
    vec_grad = vec_grad + over_core(vec_grad)
    mlp_total = jnp.concatenate(
        [keep + tie(last, came[-1]).astype(F32) for keep, last in mlp_parts], axis=0
    )
    attn_total = ga_sum[0]

    def home(own, came):
        return lax.dynamic_update_slice(own, came[None].astype(own.dtype), (1 - y, 0, 0))

    block_out = home(block_own, tie(block_came, came[0]))
    block_input_gradient = home(grad_own, last_came)

    attn_grad = jnp.stack([attn_total[:, i * cols : (i + 1) * cols] for i in range(4)])
    mlp_grad = mlp_total
    attn_new, attn_m_new, attn_v_new = adamw_update(
        attn_w, attn_m, attn_v, attn_grad, RATE_MATRIX, DECAY_MATRIX
    )
    mlp_new, mlp_m_new, mlp_v_new = adamw_update(
        mlp_w, mlp_m, mlp_v, mlp_grad, RATE_MATRIX, DECAY_MATRIX
    )
    vec_new, vec_m_new, vec_v_new = adamw_update(vectors, vec_m, vec_v, vec_grad, RATE_VECTOR, 0.0)
    return (
        block_out,
        block_input_gradient,
        attn_grad,
        attn_new,
        attn_m_new,
        attn_v_new,
        mlp_grad,
        mlp_new,
        mlp_m_new,
        mlp_v_new,
        vec_grad,
        vec_new,
        vec_m_new,
        vec_v_new,
    )


def solution(mesh):
    matrix = P(None, "wide", "narrow")
    rows = P("wide", "narrow", None)
    in_specs = (rows, P("wide", None), rows) + (matrix,) * 6 + (P(),) * 3
    out_specs = (rows, rows) + (matrix,) * 8 + (P(),) * 4
    return jax.shard_map(local, mesh=mesh, in_specs=in_specs, out_specs=out_specs, check_vma=False)
```
